32 devices in a mesh: pos: 2 (over x), seq: 16 (over z, y, core).
Axes of the slice: x: 2, y: 2, z: 4, core: 2. Of those that a mesh axis runs over, the one named last changes fastest.
Arguments:
- tokens: bfloat16 [16, 1024, 768], P('seq', 'pos'), may hold values from -6 to 6
- segment_ids: int32 [16, 1024], P('seq'), may hold values from 0 to 5, never falling along the last dimension, each value on 1 to 512 neighbouring positions
- first_gain: float32 [768], replicated, may hold values from 0.5 to 1.5
- first_bias: float32 [768], replicated, may hold values from -1.5 to 1.5
- w_qkv: bfloat16 [768, 2304], replicated, may hold values from -0.21875 to 0.21875
- query_gain: float32 [64], replicated, may hold values from 0.7 to 1.5
- key_gain: float32 [64], replicated, may hold values from 0.7 to 1.5
- w_out: bfloat16 [768, 768], replicated, may hold values from -2.5 to 2.5
- second_gain: float32 [768], replicated, may hold values from 0.5 to 1.5
- second_bias: float32 [768], replicated, may hold values from -1.5 to 1.5
- w_up: bfloat16 [768, 3072], P(None, 'seq'), may hold values from -0.21875 to 0.21875
- w_down: bfloat16 [768, 3072], P(None, 'seq'), may hold values from -0.109375 to 0.109375
- out_grad: bfloat16 [16, 1024, 768], P('seq', 'pos'), may hold values from -6 to 6
Outputs:
- block_out: bfloat16 [16, 1024, 768], P('seq', 'pos')
- input_grad: float32 [16, 1024, 768], P('seq', 'pos')
- first_gain_grad: float32 [768], replicated
- first_bias_grad: float32 [768], replicated
- qkv_grad: float32 [768, 2304], replicated
- query_gain_grad: float32 [64], replicated
- key_gain_grad: float32 [64], replicated
- proj_grad: float32 [768, 768], replicated
- second_gain_grad: float32 [768], replicated
- second_bias_grad: float32 [768], replicated
- up_grad: float32 [768, 3072], P(None, 'seq')
- down_grad: float32 [768, 3072], P(None, 'seq')
The draws below stay inside these ranges and needn't reach their ends.
Inputs may be any that keep to these rules, and one draw needn't show every extreme that they name: `segment_ids`: in each sequence image numbers start at 0, never fall, each of the 6 images holds 1 to 512 patches, and one holds exactly 512.
All inputs are finite; a program needn't handle non-finite values.
Results may differ from the reference program's by a relative error of at most 0.015.
Values may be sent and summed in bfloat16 or wider, within the bound.
A program may use at most 768 MiB of HBM per device.

```python
import math
import jax
import jax.numpy as jnp
import numpy as np
from jax import lax

D = 768
H = 12
HD = 64
FF = 3072
LEN = 1024
SEGS = 6
SEQS = 16


def block_levels(stream_key, shape, shards, smallest, top_value):
    def one(position, shards_of):
        heights = jax.random.uniform(jax.random.fold_in(jax.random.fold_in(stream_key, 6), position), (shards_of,), jnp.float32, smallest / len(shards), top_value / len(shards))
        return jnp.repeat(jnp.exp(heights), shape[position] // shards_of).reshape((-1,) + (1,) * (len(shape) - position - 1))

    factor_of = one(*shards[0])
    for cut in shards[1:]:
        factor_of = factor_of * one(*cut)
    return factor_of


def split_up(count, total, reach, slope):
    weights = [(1 << 20) // math.isqrt(standing ** slope) + 1 for standing in range(2, count + 1)]
    rest, holding = total - reach - (count - 1), [1] * (count - 1)
    while rest > 0:
        candidates = [i for i in range(count - 1) if holding[i] < reach]
        mass, left = sum([weights[i] for i in candidates]), rest
        for i in candidates:
            more = min(reach - holding[i], max(1, left * weights[i] // mass), rest)
            holding[i] = holding[i] + more
            rest = rest - more
    return np.array([reach] + holding)


def ragged(rng, count, total, reach, lean):
    if count == 2:
        one = jax.random.randint(rng, (), max(1, total - reach), min(reach, total - 1) + 1)
        return jnp.stack([one, total - one])
    sizes = jnp.asarray(split_up(count, total, reach, lean), jnp.int32)
    twos = (count - 1) // 2
    donor, receiver = sizes[1:1 + 2 * twos:2], sizes[2:2 + 2 * twos:2]
    slack = jnp.minimum(donor - 1, reach - receiver)
    passed = jax.random.randint(jax.random.fold_in(rng, 1), (twos,), 0, 1 << 20) % (slack + 1)
    sizes = sizes.at[1:1 + 2 * twos:2].set(donor - passed).at[2:2 + 2 * twos:2].set(receiver + passed)
    return sizes[jax.random.permutation(jax.random.fold_in(rng, 2), count)]


def noise(key, extent, width, bound, cuts=(), held_as=jnp.bfloat16):
    factor_of = block_levels(key, extent, cuts, -0.22, 0.18) if cuts else 1.0
    array = jax.random.normal(key, extent, jnp.float32) * width * factor_of
    return jnp.minimum(jnp.maximum(array, -bound), bound).astype(held_as)


def setup_inputs(seed: int = 0) -> dict:
    seeds = jax.random.split(jax.random.key(seed), 14)
    return {
        "tokens": noise(seeds[0], (SEQS, LEN, D), 1.0, 6.0, ((0, 16), (1, 2))),
        "segment_ids": jax.vmap(lambda own: jnp.searchsorted(jnp.cumsum(ragged(own, SEGS, LEN, LEN // 2, 2)), jnp.arange(LEN), side="right"))(jax.random.split(seeds[1], SEQS)).reshape((SEQS, LEN)).astype(jnp.int32),
        "first_gain": jnp.clip(1.0 + 0.1 * jax.random.normal(seeds[2], (D,), jnp.float32), 0.5, 1.5),
        "first_bias": noise(seeds[3], (D,), 0.3, 1.5, (), jnp.float32),
        "w_qkv": noise(seeds[4], (D, 3 * D), D ** -0.5, 0.21875),
        "query_gain": jnp.clip(jax.random.uniform(seeds[5], (HD,), jnp.float32, 0.7, 1.5), 0.7, 1.5),
        "key_gain": jnp.clip(jax.random.uniform(seeds[6], (HD,), jnp.float32, 0.7, 1.5), 0.7, 1.5),
        "w_out": noise(seeds[7], (D, D), (max(4, D // 128)) ** -0.5, 2.5),
        "second_gain": jnp.clip(1.0 + 0.1 * jax.random.normal(seeds[8], (D,), jnp.float32), 0.5, 1.5),
        "second_bias": noise(seeds[9], (D,), 0.3, 1.5, (), jnp.float32),
        "w_up": noise(seeds[10], (D, FF), D ** -0.5, 0.21875, ((1, 16),)),
        "w_down": noise(seeds[11], (D, FF), FF ** -0.5, 0.109375, ((1, 16),)),
        "out_grad": noise(seeds[12], (SEQS, LEN, D), 1.0, 6.0, ((0, 16), (1, 2))),
    }


EPS = 1e-06
HIGH = lax.Precision.HIGHEST

@jax.custom_vjp
def low(v):
    return lax.optimization_barrier(v.astype(jnp.bfloat16)).astype(jnp.float32)

@jax.custom_vjp
def low_back(v):
    return v

def low_keep(v):
    return (low(v), None)

def low_pass(kept, grad):
    return (grad,)

def back_keep(v):
    return (v, None)

def back_low(kept, grad):
    return (low(grad),)
low.defvjp(low_keep, low_pass)
low_back.defvjp(back_keep, back_low)

def layer_norm(rows, gain, shift):
    average = lax.optimization_barrier(jnp.mean(rows, axis=-1, keepdims=True))
    centred = rows - average
    spread = lax.optimization_barrier(jnp.mean(centred * centred, axis=-1, keepdims=True))
    return centred * lax.rsqrt(spread + EPS) * gain + shift

def head_norm(values, gain):
    average = lax.optimization_barrier(jnp.mean(values, axis=-1, keepdims=True))
    centred = values - average
    spread = lax.optimization_barrier(jnp.mean(centred * centred, axis=-1, keepdims=True))
    return centred * lax.rsqrt(spread + EPS) * gain

def attend_one(packed):
    query, keys, values, labels = packed
    raw = low_back(jnp.einsum('qhd,khd->hqk', query, keys, precision=HIGH)) * HD ** (-0.5)
    allowed = labels[:, None] == labels[None, :]
    scores = jnp.where(allowed[None], raw, -1e+30)
    probs = low(jax.nn.softmax(scores, axis=-1))
    return jnp.einsum('hqk,khd->qhd', probs, values, precision=HIGH)

def forward(rows, labels, first_gain, first_bias, w_qkv, query_gain, key_gain, w_out, second_gain, second_bias, w_up, w_down):
    groups = rows.shape[0]
    normed = low(layer_norm(rows, first_gain, first_bias))
    mixed = low_back(jnp.einsum('gtd,de->gte', normed, w_qkv, precision=HIGH))
    shaped = mixed.reshape(groups, LEN, 3, H, HD)
    query = low(head_norm(shaped[:, :, 0], query_gain))
    keys = low(head_norm(shaped[:, :, 1], key_gain))
    values = low(shaped[:, :, 2])
    attended = lax.map(jax.checkpoint(attend_one), (query, keys, values, labels))
    attended = low(low_back(attended)).reshape(groups, LEN, D)
    branch = low_back(jnp.einsum('gtd,de->gte', attended, w_out, precision=HIGH))
    middle = rows + branch
    second = low(layer_norm(middle, second_gain, second_bias))
    pre = low_back(jnp.einsum('gtd,df->gtf', second, w_up, precision=HIGH))
    hidden = low(jax.nn.gelu(pre, approximate=False))
    return middle + jnp.einsum('gtf,df->gtd', hidden, w_down, precision=HIGH)

def group_count(total, length):
    best = 1
    for option in range(1, total + 1):
        if total % option == 0 and option * length <= 4096:
            best = option
    return best

def reference(tokens, segment_ids, first_gain, first_bias, w_qkv, query_gain, key_gain, w_out, second_gain, second_bias, w_up, w_down, out_grad):
    weights = tuple((item.astype(jnp.float32) for item in (first_gain, first_bias, w_qkv, query_gain, key_gain, w_out, second_gain, second_bias, w_up, w_down)))
    group = group_count(SEQS, LEN)
    blocks = SEQS // group
    inputs = tokens.astype(jnp.float32).reshape(blocks, group, LEN, D)
    labels = segment_ids.reshape(blocks, group, LEN)
    cotangent = out_grad.astype(jnp.float32).reshape(blocks, group, LEN, D)

    def visit(totals, packed):
        rows, marks, upstream = packed

        def closed(rows_in, *params):
            return forward(rows_in, marks, *params)
        result, pullback = jax.vjp(closed, rows, *weights)
        grads = pullback(upstream)
        totals = tuple((total + extra for total, extra in zip(totals, grads[1:])))
        return (totals, (result.astype(jnp.bfloat16), grads[0]))
    start = tuple((jnp.zeros_like(item) for item in weights))
    totals, (outputs, input_grads) = lax.scan(visit, start, (inputs, labels, cotangent))
    block_out = outputs.reshape(SEQS, LEN, D)
    input_grad = input_grads.reshape(SEQS, LEN, D)
    return (block_out, input_grad, totals[0], totals[1], totals[2], totals[3], totals[4], totals[5], totals[6], totals[7], totals[8], totals[9])
```

```python
import functools
import jax
import jax.numpy as jnp
from jax import lax
from jax.experimental import pallas as pl
from jax.experimental.pallas import tpu as pltpu
from jax.sharding import PartitionSpec as P

EPS = 1e-06
F32 = jnp.float32
BF16 = jnp.bfloat16
LOG2E = 1.4426950408889634
BIG = 16384.0
TILE = 256
NT = (((1,), (1,)), ((), ()))
NN = (((1,), (0,)), ((), ()))
TN = (((0,), (0,)), ((), ()))


def dot(a, b, dims=NN):
    return lax.dot_general(a, b, dims, preferred_element_type=F32)


def two(x):
    hi = x.astype(BF16)
    return hi, (x - hi.astype(F32)).astype(BF16)


def group_sum(x, ones):
    hi, lo = two(x)
    return dot(hi, ones) + dot(lo, ones)


def rows_norm(x):
    average = jnp.mean(x, axis=-1, keepdims=True)
    centred = x - average
    spread = jnp.mean(centred * centred, axis=-1, keepdims=True)
    scale = lax.rsqrt(spread + EPS)
    return centred * scale, scale


def tile_of(i, size=TILE):
    return pl.ds(pl.multiple_of(i * size, size), size)


def fwd_body(own, rem, fq, fk, g1, b1, wqkv, qg, kg, wout, g2, b2, ones,
             normed, kk, vv, rq, rk, qaug, att, mid, sec, qq):
    n, width = own.shape
    hd = width // (width // 64)
    cols = ones.shape[0]

    def project(x, base, queries):
        rows = tile_of(base)
        low = (rows_norm(x)[0] * g1[...] + b1[...]).astype(BF16)
        normed[rows, :] = low
        for block in range(0 if queries else width // cols, 3 * width // cols):
            raw = dot(low, wqkv[:, block * cols:(block + 1) * cols])
            part, at = divmod(block * cols, width)
            lanes = slice(at, at + cols)
            if part == 2:
                vv[rows, lanes] = raw.astype(BF16)
                continue
            centred = raw - group_sum(raw, ones[...]) * (1 / 64)
            scale = lax.rsqrt(group_sum(centred * centred, ones[...]) * (1 / 64) + EPS)
            if part == 0:
                qq[rows, lanes] = (centred * scale * qg[:, lanes]).astype(BF16)
                rq[rows, lanes] = scale
            else:
                kk[rows, lanes] = (centred * scale * kg[:, lanes]).astype(BF16)
                rk[rows, lanes] = scale

    def own_tile(i, c):
        project(own[tile_of(i), :].astype(F32), i, True)
        return c

    def rem_tile(i, c):
        project(rem[tile_of(i), :].astype(F32), i + n // TILE, False)
        return c

    lax.fori_loop(0, n // TILE, own_tile, 0)
    lax.fori_loop(0, n // TILE, rem_tile, 0)

    def pair(p, c):
        lanes = tile_of(p, 128)
        k, v = kk[:, lanes], vv[:, lanes]
        feat = fk[...]
        low_k = lax.broadcasted_iota(jnp.int32, k.shape, 1) < 64
        one = jnp.ones_like(v)
        ks = (jnp.where(low_k, k, feat), jnp.where(low_k, feat, k))
        vs = (jnp.where(low_k, v, one), jnp.where(low_k, one, v))
        lane = lax.broadcasted_iota(jnp.int32, (TILE, 128), 1)
        low = lane < 64

        def tile(t, c):
            rows = tile_of(t)
            q, mask = qq[rows, lanes], fq[rows, :]
            res = []
            for a in range(2):
                qa = jnp.where(low, q, mask) if a == 0 else jnp.where(low, mask, q)
                e = jnp.exp2(dot(qa, ks[a], NT) * (LOG2E / 8)).astype(BF16)
                o = dot(e, vs[a])
                res.append(o)
                shift = jnp.log(o) * -8.0
                hi, lo = two(shift)
                lo2 = (shift - hi.astype(F32) - lo.astype(F32)).astype(BF16)
                s = 64 * (1 - a)
                qaug[p * 2 + a, rows, :] = jnp.where(
                    lane == s + 6, hi, jnp.where(lane == s + 7, lo, jnp.where(lane == s + 8, lo2, qa)))
            num = jnp.where(low, res[0], res[1])
            den = pltpu.roll(jnp.where(low, res[1], res[0]), 64, 1)
            att[rows, lanes] = (num / den).astype(BF16)
            return c

        lax.fori_loop(0, n // TILE, tile, 0)
        return c

    lax.fori_loop(0, width // 128, pair, 0)

    def out_tile(i, c):
        rows = tile_of(i)
        m = own[rows, :].astype(F32) + dot(att[rows, :], wout[...])
        mid[rows, :] = m
        sec[rows, :] = (rows_norm(m)[0] * g2[...] + b2[...]).astype(BF16)
        return c

    lax.fori_loop(0, n // TILE, out_tile, 0)


def bwd_body(own, rem, gsec, mid, gy, fk, g1, wqkv, qg, kg, wout, g2, ones, swap,
             normed, kk, vv, rq, rk, qaug, att,
             gall, gn_own, gn_rem, gmid, small, gbr, gat, gmix, dk, dv):
    n, width = own.shape
    pairs = width // 128
    small[...] = jnp.zeros_like(small)

    def mid_tile(i, c):
        rows = tile_of(i)
        xh, r = rows_norm(mid[rows, :])
        dy = gsec[rows, :]
        small[2:3, :] += jnp.sum(dy * xh, axis=0, keepdims=True)
        small[3:4, :] += jnp.sum(dy, axis=0, keepdims=True)
        gd = dy * g2[...]
        dx = r * (gd - jnp.mean(gd, -1, keepdims=True) - xh * jnp.mean(gd * xh, -1, keepdims=True))
        gm = gy[rows, :].astype(F32) + dx
        gmid[rows, :] = gm
        low = gm.astype(BF16)
        gbr[rows, :] = low
        gat[rows, :] = dot(low, wout[...], NT).astype(BF16)
        return c

    lax.fori_loop(0, n // TILE, mid_tile, 0)

    def proj_tile(i, c):
        cols = tile_of(i)
        gall[cols, 3 * width:] = dot(att[:, cols], gbr[...], TN).astype(BF16)
        return c

    lax.fori_loop(0, width // TILE, proj_tile, 0)

    def pair(p, c):
        lanes = tile_of(p, 128)
        lane = lax.broadcasted_iota(jnp.int32, (n, 128), 1)
        low_q = lane < 64
        do = gat[:, lanes]
        delta = -group_sum(do.astype(F32) * att[:, lanes].astype(F32), swap[...])
        hi, lo = two(delta)
        zero = jnp.zeros_like(do)
        das = []
        for a in range(2):
            s = 64 * (1 - a)
            extra = jnp.where(lane == s, hi, jnp.where(lane == s + 1, lo, zero))
            das.append(jnp.where(low_q, do, extra) if a == 0 else jnp.where(low_q, extra, do))
        low = lax.broadcasted_iota(jnp.int32, (TILE, 128), 1) < 64

        def keys(t, acc):
            rows = tile_of(t)
            k, v, feat = kk[rows, lanes], vv[rows, lanes], fk[rows, :]
            one = jnp.ones_like(v)
            dks, dvs, out = [], [], []
            for a in range(2):
                ka = jnp.where(low, k, feat) if a == 0 else jnp.where(low, feat, k)
                va = jnp.where(low, v, one) if a == 0 else jnp.where(low, one, v)
                qa = qaug[p * 2 + a]
                e = jnp.exp2(dot(ka, qa, NT) * (LOG2E / 8))
                ds = (e * dot(va, das[a], NT)).astype(BF16)
                dvs.append(dot(e.astype(BF16), das[a]))
                dks.append(dot(ds, qa))
                out.append(acc[a] + dot(ka, ds, TN))
            dk[rows, :] = jnp.where(low, dks[0], dks[1])
            gmix[rows, tile_of(p + 2 * pairs, 128)] = jnp.where(low, dvs[0], dvs[1]).astype(BF16)
            return tuple(out)

        zeros = jnp.zeros((128, n), F32)
        acc = lax.fori_loop(0, 2 * n // TILE, keys, (zeros, zeros))
        low_s = lax.broadcasted_iota(jnp.int32, (128, n), 0) < 64
        dq = jnp.where(low_s, acc[0], acc[1]).T
        gain = qg[:, lanes]

        def norm_back(dy, y, r, gain):
            dy = dy * 0.125
            prod = dy * y.astype(F32)
            gd = dy * gain
            m1 = group_sum(gd, ones[...]) * (1 / 64)
            m2 = group_sum(prod, ones[...]) * (1 / 64)
            inv = 1.0 / gain
            return r * (gd - m1 - y.astype(F32) * inv * m2), jnp.sum(prod, 0, keepdims=True) * inv

        low_half = lane < 64
        qa = jnp.where(low_half, qaug[p * 2], qaug[p * 2 + 1])
        dx, gg = norm_back(dq, qa, rq[:, lanes], gain)
        gmix[0:n, lanes] = dx.astype(BF16)
        small[4:5, lanes] = gg
        dx, gg = norm_back(dk[...], kk[:, lanes], rk[:, lanes], kg[:, lanes])
        gmix[:, tile_of(p + pairs, 128)] = dx.astype(BF16)
        small[5:6, lanes] = gg
        return c

    lax.fori_loop(0, pairs, pair, 0)

    def qkv_tile(i, c):
        cols = tile_of(i)
        gall[cols, 0:width] = dot(normed[0:n, cols], gmix[0:n, 0:width], TN).astype(BF16)
        for part in (1, 2):
            at = slice(part * width, (part + 1) * width)
            gall[cols, at] = dot(normed[:, cols], gmix[:, at], TN).astype(BF16)
        return c

    lax.fori_loop(0, width // TILE, qkv_tile, 0)

    def gain_sums(x, gn):
        xh, _ = rows_norm(x.astype(F32))
        small[0:1, :] += jnp.sum(gn * xh, axis=0, keepdims=True)
        small[1:2, :] += jnp.sum(gn, axis=0, keepdims=True)

    def own_tile(i, c):
        rows = tile_of(i)
        gn = dot(gmix[rows, :], wqkv[...], NT)
        gn_own[rows, :] = gn
        gain_sums(own[rows, :], gn)
        return c

    def rem_tile(i, c):
        rows, at = tile_of(i), tile_of(i + n // TILE)
        gn = dot(gmix[at, width:], wqkv[:, width:], NT)
        gn_rem[rows, :] = gn.astype(BF16)
        gain_sums(rem[rows, :], gn)
        return c

    lax.fori_loop(0, n // TILE, own_tile, 0)
    lax.fori_loop(0, n // TILE, rem_tile, 0)


VM = pl.BlockSpec(memory_space=pltpu.VMEM)
LIMIT = 60 * 1024 * 1024


def sds(shape, dtype):
    return jax.ShapeDtypeStruct(shape, dtype)


def fwd_call(own, rem, fq, fk, g1, b1, wqkv, qg, kg, wout, g2, b2, ones):
    n, width = own.shape
    heads = width // 64
    outs = (sds((2 * n, width), BF16), sds((2 * n, width), BF16), sds((2 * n, width), BF16),
            sds((n, width), F32), sds((2 * n, width), F32), sds((heads, n, 128), BF16),
            sds((n, width), BF16), sds((n, width), F32), sds((n, width), BF16))
    return pl.pallas_call(
        fwd_body, out_shape=outs, in_specs=[VM] * 13, out_specs=tuple([VM] * 9),
        scratch_shapes=[pltpu.VMEM((n, width), BF16)],
        compiler_params=pltpu.CompilerParams(vmem_limit_bytes=LIMIT),
        name="fwd",
    )(own, rem, fq, fk, g1, b1, wqkv, qg, kg, wout, g2, b2, ones)


def bwd_call(*args):
    own = args[0]
    n, width = own.shape
    outs = (sds((width, 4 * width), BF16), sds((n, width), F32),
            sds((n, width), BF16), sds((n, width), F32), sds((8, width), F32))
    return pl.pallas_call(
        bwd_body, out_shape=outs, in_specs=[VM] * 21, out_specs=tuple([VM] * 5),
        scratch_shapes=[pltpu.VMEM((n, width), BF16), pltpu.VMEM((n, width), BF16),
                        pltpu.VMEM((2 * n, 3 * width), BF16), pltpu.VMEM((2 * n, 128), F32),
                        pltpu.VMEM((8, 128), F32)],
        compiler_params=pltpu.CompilerParams(vmem_limit_bytes=LIMIT),
        name="bwd",
    )(*args)


def ring_places(n_seq):
    s = lax.axis_index("seq")
    core, chip = s % 2, s // 2
    chips = n_seq // 2
    half = chips // 2
    odd = chip % 2
    place = (1 - odd) * (chip // 2) + odd * (chips - 1 - chip // 2)

    def device(p):
        far = p // half
        return ((1 - far) * 2 * p + far * (2 * (chips - 1 - p) + 1)) * 2 + core

    right = device((place + 1) % chips)
    left = device((place + chips - 1) % chips)
    return core, place, right, left, s + 1 - 2 * core


def copy_to(src, dst, send, recv, target):
    return pltpu.make_async_remote_copy(
        src_ref=src, dst_ref=dst, send_sem=send, recv_sem=recv, device_id=target,
        device_id_type=pl.DeviceIdType.MESH)


def greet(targets):
    barrier = pltpu.get_barrier_semaphore()
    for t in targets:
        pl.semaphore_signal(barrier, inc=1, device_id=t, device_id_type=pl.DeviceIdType.MESH)
    pl.semaphore_wait(barrier, len(targets))


def ffn_body(n_seq, sec, gy, mid, w_own, out, gsec, grads,
             sx, sg, wbuf, accin, accout, first, hid, gpre, blk, gs, prec,
             wsend, wrecv, asend, arecv, psend, precv):
    n, width = sec.shape
    f = w_own.shape[1]
    h = f // 2
    chips = n_seq // 2
    core, place, right, left, partner = ring_places(n_seq)
    right, left, partner = {"seq": right}, {"seq": left}, {"seq": partner}
    greet((right, left, partner))

    shares = (copy_to(sec, sx.at[pl.ds(n, n)], psend.at[0], precv.at[0], partner),
              copy_to(gy, sg.at[pl.ds(n, n)], psend.at[1], precv.at[1], partner))
    parts = (copy_to(blk.at[pl.ds(n, n)], prec.at[0], psend.at[2], precv.at[2], partner),
             copy_to(gs.at[pl.ds(n, n)], prec.at[1], psend.at[3], precv.at[3], partner))

    def w_copy(d, s):
        rows = pl.ds(d * h, h)
        return copy_to(wbuf.at[s, :, rows], wbuf.at[s + 1, :, rows], wsend.at[d, s], wrecv.at[d, s],
                       left if d else right)

    def w_first(d):
        rows = pl.ds(d * h, h)
        return copy_to(w_own.at[:, rows], wbuf.at[1, :, rows], wsend.at[d, 0], wrecv.at[d, 0],
                       left if d else right)

    def a_copy(d, s):
        rows = pl.ds(d * h, h)
        return copy_to(accout.at[s - 1, :, rows], accin.at[s - 1, :, rows], asend.at[d, s - 1],
                       arecv.at[d, s - 1], left if d else right)

    for d in range(2):
        w_first(d).start()
    for c in shares:
        c.start()
    wbuf[0] = w_own[...]
    sx[0:n, :] = sec[...]
    sg[0:n, :] = gy[...]
    blk[...] = jnp.zeros_like(blk)
    gs[...] = jnp.zeros_like(gs)
    for c in shares:
        c.wait_recv()

    def step(s, carry):
        @pl.when(s > 0)
        def _():
            for d in range(2):
                w_copy(d, s - 1).wait_recv()

            @pl.when(s < chips - 1)
            def _():
                for d in range(2):
                    w_copy(d, s).start()

        def tile(i, c):
            rows = tile_of(i)
            up, down = wbuf[s, 0], wbuf[s, 1]
            pre = dot(sx[rows, :], up, NT)
            gh = dot(sg[rows, :], down, NT)
            cdf = 0.5 + 0.5 * lax.erf(pre * 0.7071067811865476)
            slope = cdf + pre * (jnp.exp(-0.5 * pre * pre) * 0.3989422804014327)
            a = (pre * cdf).astype(BF16)
            b = (gh * slope).astype(BF16)
            hid[rows, :] = a
            gpre[rows, :] = b
            blk[rows, :] += dot(a, down)
            gs[rows, :] += dot(b, up)
            return c

        lax.fori_loop(0, 2 * n // TILE, tile, 0)

        @pl.when(s > 1)
        def _():
            for d in range(2):
                a_copy(d, s - 1).wait_recv()

        def block(j, c):
            cols = tile_of(j)
            for k, (lhs, rhs) in enumerate(((gpre, sx), (hid, sg))):
                part = dot(lhs[...], rhs[:, cols], TN)

                @pl.when(s == 0)
                def _():
                    first[k, :, cols] = part

                @pl.when(s == 1)
                def _():
                    accout[0, k, :, cols] = part.astype(BF16)

                @pl.when(s > 1)
                def _():
                    accout[s - 1, k, :, cols] = (part + accin[s - 2, k, :, cols].astype(F32)).astype(BF16)
            return c

        lax.fori_loop(0, width // TILE, block, 0)

        @pl.when(s > 0)
        def _():
            for d in range(2):
                a_copy(d, s).start()
        return carry

    lax.fori_loop(0, chips, step, 0)
    for c in parts:
        c.start()
    for c in parts:
        c.wait_recv()
    out[...] = (mid[...] + (blk[0:n, :] + prec[0])).astype(BF16)
    gsec[...] = gs[0:n, :] + prec[1]
    for d in range(2):
        a_copy(d, chips - 1).wait_recv()
    grads[...] = (first[...] + accin[chips - 2].astype(F32)).astype(BF16)

    def drain(s, c):
        for d in range(2):
            a_copy(d, s + 1).wait_send()

            @pl.when(s > 0)
            def _():
                w_copy(d, s).wait_send()
        return c

    lax.fori_loop(0, chips - 1, drain, 0)
    for d in range(2):
        w_first(d).wait_send()
    for c in shares + parts:
        c.wait_send()


def ffn_call(n_seq, sec, gy, mid, w_own):
    n, width = sec.shape
    f = w_own.shape[1]
    chips = n_seq // 2
    V, D = pltpu.VMEM, pltpu.SemaphoreType.DMA
    return pl.pallas_call(
        functools.partial(ffn_body, n_seq),
        out_shape=(sds((n, width), BF16), sds((n, width), F32), sds((2, f, width), BF16)),
        in_specs=[VM] * 4, out_specs=(VM,) * 3,
        scratch_shapes=[
            V((2 * n, width), BF16), V((2 * n, width), BF16), V((chips, 2, f, width), BF16),
            V((chips - 1, 2, f, width), BF16), V((chips - 1, 2, f, width), BF16),
            V((2, f, width), F32), V((2 * n, f), BF16), V((2 * n, f), BF16),
            V((2 * n, width), F32), V((2 * n, width), F32), V((2, n, width), F32),
            D((2, chips - 1)), D((2, chips - 1)), D((2, chips - 1)), D((2, chips - 1)), D((4,)), D((4,))],
        compiler_params=pltpu.CompilerParams(
            vmem_limit_bytes=LIMIT, collective_id=1, has_side_effects=True),
        name="ffn",
    )(sec, gy, mid, w_own)


SPLIT = 2


def sum_body(n_seq, g, small, own, gn_own, gn_rem, gmid, g1, out, sout, igrad,
             pbuf, accin, accout, xin, xout, fin, srec, sring, gback,
             psend, precv, asend, arecv, xsend, xrecv, fsend, frecv, qsend, qrecv, ssend, srecv, gsend, grecv):
    rows, cols = g.shape
    chips = n_seq // 2
    half = rows // 2
    cr = half // chips
    cw = cols // (2 * SPLIT)
    core, place, right, left, partner = ring_places(n_seq)
    x = lax.axis_index("pos")
    right, left, partner, across = {"seq": right}, {"seq": left}, {"seq": partner}, {"pos": 1 - x}
    greet((right, left, partner, across))

    def chunk(p):
        return (p + 2 * chips) % chips

    def at(d, k):
        return pl.ds((d * SPLIT + k) * cw, cw)

    def rows_of(c, p):
        return pl.ds(pl.multiple_of(c * half + p * cr, cr), cr)

    def p_copy(q):
        return copy_to(g.at[rows_of(1 - core, q)], pbuf.at[q], psend.at[q], precv.at[q], partner)

    def a_copy(d, k, s):
        return copy_to(accout.at[s, d * SPLIT + k], accin.at[s, d * SPLIT + k], asend.at[s, d * SPLIT + k],
                       arecv.at[s, d * SPLIT + k], left if d else right)

    def x_copy(d, k):
        i = d * SPLIT + k
        return copy_to(xout.at[i], xin.at[i], xsend.at[i], xrecv.at[i], across)

    def f_copy(d, k, s):
        p = chunk(place + s) if d else chunk(place - s)
        ref = fin.at[rows_of(core, p), at(d, k)]
        return copy_to(ref, ref, fsend.at[s, d * SPLIT + k], frecv.at[s, d * SPLIT + k], left if d else right)

    def f_recv(d, k, s):
        p = chunk(place + s + 1) if d else chunk(place - s - 1)
        ref = fin.at[rows_of(core, p), at(d, k)]
        return copy_to(ref, ref, fsend.at[s, d * SPLIT + k], frecv.at[s, d * SPLIT + k], left if d else right)

    def q_copy(d, k, s):
        p = chunk(place + s) if d else chunk(place - s)
        ref = fin.at[rows_of(core, p), at(d, k)]
        return copy_to(ref, ref, qsend.at[s, d * SPLIT + k], qrecv.at[s, d * SPLIT + k], partner)

    def q_recv(d, k, s):
        p = chunk(place + s) if d else chunk(place - s)
        ref = fin.at[rows_of(1 - core, p), at(d, k)]
        return copy_to(ref, ref, qsend.at[s, d * SPLIT + k], qrecv.at[s, d * SPLIT + k], partner)

    def s_copy(s):
        return copy_to(sring.at[chunk(place - s)], sring.at[chunk(place - s)], ssend.at[s], srecv.at[s], right)

    def s_recv(s):
        p = chunk(place - s - 1)
        return copy_to(sring.at[p], sring.at[p], ssend.at[s], srecv.at[s], right)

    both = [(d, k) for k in range(SPLIT) for d in range(2)]
    back = copy_to(gn_rem, gback, gsend.at[0], grecv.at[0], across)
    small_p = copy_to(small, srec.at[0], gsend.at[1], grecv.at[1], partner)
    small_x = copy_to(srec.at[1], srec.at[2], gsend.at[2], grecv.at[2], across)

    def order(s):
        return chunk(place - s), chunk(place + s)

    small_p.start()
    for s in range(1, chips // 2 + 1):
        for q in order(s)[: 1 if 2 * s == chips else 2]:
            p_copy(q).start()
    p_copy(place).start()
    back.start()

    def part(d, k, q):
        cs = at(d, k)
        return g[rows_of(core, q), cs].astype(F32) + pbuf[q, :, cs].astype(F32)

    def reduce_step(s, c):
        @pl.when(s <= chips // 2)
        def _():
            p_copy(chunk(place - s)).wait_recv()

            @pl.when(2 * s < chips)
            def _():
                p_copy(chunk(place + s)).wait_recv()

        for d, k in both:
            q = chunk(place + s) if d else chunk(place - s)

            @pl.when(s == 1)
            def _():
                accout[s - 1, d * SPLIT + k] = part(d, k, q).astype(BF16)

            @pl.when(s > 1)
            def _():
                a_copy(d, k, s - 2).wait_recv()
                accout[s - 1, d * SPLIT + k] = (part(d, k, q) + accin[s - 2, d * SPLIT + k].astype(F32)).astype(BF16)

            a_copy(d, k, s - 1).start()
        return c

    lax.fori_loop(1, chips, reduce_step, 0)
    p_copy(place).wait_recv()
    for d, k in both:
        a_copy(d, k, chips - 2).wait_recv()
        xout[d * SPLIT + k] = (part(d, k, place) + accin[chips - 2, d * SPLIT + k].astype(F32)).astype(BF16)
        x_copy(d, k).start()
    small_p.wait_recv()
    srec[1] = small[...] + srec[0]
    small_x.start()
    back.wait_recv()
    n = own.shape[0]

    def norm_tile(i, c):
        rs = tile_of(i)
        xh, r = rows_norm(own[rs, :].astype(F32))
        dy = (gn_own[rs, :] + gback[rs, :].astype(F32)) * g1[...]
        dx = r * (dy - jnp.mean(dy, -1, keepdims=True) - xh * jnp.mean(dy * xh, -1, keepdims=True))
        igrad[rs, :] = gmid[rs, :] + dx
        return c

    lax.fori_loop(0, n // TILE, norm_tile, 0)
    small_x.wait_recv()
    sring[place] = srec[1] + srec[2]
    s_copy(0).start()
    for d, k in both:
        x_copy(d, k).wait_recv()
        i = d * SPLIT + k
        fin[rows_of(core, place), at(d, k)] = (xout[i].astype(F32) + xin[i].astype(F32)).astype(BF16)
        f_copy(d, k, 0).start()
        q_copy(d, k, 0).start()

    def gather_step(s, c):
        for d, k in both:
            f_recv(d, k, s - 1).wait_recv()

            @pl.when(s < chips - 1)
            def _():
                f_copy(d, k, s).start()

            q_copy(d, k, s).start()
        s_recv(s - 1).wait_recv()

        @pl.when(s < chips - 1)
        def _():
            s_copy(s).start()
        return c

    lax.fori_loop(1, chips, gather_step, 0)

    def finish(s, c):
        for d, k in both:
            q_recv(d, k, s).wait_recv()
        return c

    lax.fori_loop(0, chips, finish, 0)
    total = sring[0]
    for s in range(1, chips):
        total = total + sring[s]
    sout[...] = total

    def widen(i, c):
        rs = pl.ds(pl.multiple_of(i * 32, 32), 32)
        out[rs, :] = fin[rs, :].astype(F32)
        return c

    lax.fori_loop(0, rows // 32, widen, 0)

    def drain(s, c):
        for d, k in both:
            q_copy(d, k, s).wait_send()

            @pl.when(s < chips - 1)
            def _():
                a_copy(d, k, s).wait_send()
                f_copy(d, k, s).wait_send()

        @pl.when(s < chips - 1)
        def _():
            s_copy(s).wait_send()
        p_copy(s).wait_send()
        return c

    lax.fori_loop(0, chips, drain, 0)
    for d, k in both:
        x_copy(d, k).wait_send()
    for c in (back, small_p, small_x):
        c.wait_send()


def sum_call(n_seq, g, small, own, gn_own, gn_rem, gmid, g1):
    rows, cols = g.shape
    n, width = own.shape
    chips = n_seq // 2
    cr, lanes, cw = rows // 2 // chips, 2 * SPLIT, cols // (2 * SPLIT)
    V, D = pltpu.VMEM, pltpu.SemaphoreType.DMA
    return pl.pallas_call(
        functools.partial(sum_body, n_seq),
        out_shape=(sds((rows, cols), F32), sds(small.shape, F32), sds((n, width), F32)),
        in_specs=[VM] * 7, out_specs=(VM,) * 3,
        scratch_shapes=[
            V((chips, cr, cols), BF16), V((chips - 1, lanes, cr, cw), BF16), V((chips - 1, lanes, cr, cw), BF16),
            V((lanes, cr, cw), BF16), V((lanes, cr, cw), BF16), V((rows, cols), BF16),
            V((3,) + small.shape, F32), V((chips,) + small.shape, F32), V((n, width), BF16),
            D((chips,)), D((chips,)), D((chips - 1, lanes)), D((chips - 1, lanes)), D((lanes,)), D((lanes,)),
            D((chips - 1, lanes)), D((chips - 1, lanes)), D((chips, lanes)), D((chips, lanes)),
            D((chips - 1,)), D((chips - 1,)), D((3,)), D((3,))],
        compiler_params=pltpu.CompilerParams(
            vmem_limit_bytes=LIMIT, collective_id=2, has_side_effects=True),
        name="sums",
    )(g, small, own, gn_own, gn_rem, gmid, g1)


def features(marks):
    lane = lax.broadcasted_iota(jnp.int32, (1, 128), 1) % 64
    same = marks[:, None] == lane
    extra = (lane >= 6) & (lane <= 8)
    keys = jnp.where(extra, 1.0, jnp.where(same & (lane < 6), 1.0, 0.0)).astype(BF16)
    query = jnp.where((lane < 6) & ~same, -BIG, 0.0).astype(BF16)
    return query, keys


def local_one(tokens, segment_ids, first_gain, first_bias, w_qkv, query_gain, key_gain, w_out,
              second_gain, second_bias, w_up, w_down, out_grad):
    _, n, width = tokens.shape
    heads = width // query_gain.shape[0]
    me = lax.axis_index("pos")
    own = tokens[0]
    rem = lax.ppermute(own, "pos", [(0, 1), (1, 0)])
    marks = lax.dynamic_slice_in_dim(segment_ids[0], me * n, n)
    far = lax.dynamic_slice_in_dim(segment_ids[0], (1 - me) * n, n)
    fq, fk = features(marks)
    fk = jnp.concatenate([fk, features(far)[1]], 0)
    row = lambda v: v.reshape(1, -1)
    qg, kg = row(jnp.tile(query_gain, heads)), row(jnp.tile(key_gain, heads))
    group = jnp.arange(256) // 64
    ones = (group[:, None] == group[None, :]).astype(BF16)
    swap = (group[:128, None] != group[None, :128]).astype(BF16)
    g1, b1, g2, b2 = row(first_gain), row(first_bias), row(second_gain), row(second_bias)
    normed, kk, vv, rq, rk, qaug, att, mid, sec = fwd_call(
        own, rem, fq, fk, g1, b1, w_qkv, qg, kg, w_out, g2, b2, ones)
    gy = out_grad[0]
    n_seq = lax.axis_size("seq")
    w_own = jnp.stack([w_up.T, w_down.T])
    block_out, gsec, grads = ffn_call(n_seq, sec, gy, mid, w_own)
    g, gn_own, gn_rem, gmid, small = bwd_call(
        own, rem, gsec, mid, gy, fk, g1, w_qkv, qg, kg, w_out, g2, ones[:128, :128], swap,
        normed, kk, vv, rq, rk, qaug, att)
    grads = lax.psum(grads, "pos").astype(F32)
    g, small, input_grad = sum_call(n_seq, g, small, own, gn_own, gn_rem, gmid, g1)
    fold = lambda v: v.reshape(heads, -1).sum(0)
    return (block_out[None], input_grad[None], small[0], small[1], g[:, :3 * width], fold(small[4]), fold(small[5]),
            g[:, 3 * width:], small[2], small[3], grads[0].T, grads[1].T)


def layer_norm(rows, gain, shift):
    average = jnp.mean(rows, axis=-1, keepdims=True)
    centred = rows - average
    spread = jnp.mean(centred * centred, axis=-1, keepdims=True)
    return centred * lax.rsqrt(spread + EPS) * gain + shift


def head_norm(values, gain):
    average = jnp.mean(values, axis=-1, keepdims=True)
    centred = values - average
    spread = jnp.mean(centred * centred, axis=-1, keepdims=True)
    return centred * lax.rsqrt(spread + EPS) * gain


def qk_norms(raw_query, raw_keys, query_gain, key_gain):
    return (head_norm(raw_query, query_gain), head_norm(raw_keys, key_gain))


def gelu_exact(values):
    return jax.nn.gelu(values, approximate=False)


def gelu_back(pre, upstream):
    return jax.vjp(gelu_exact, pre)[1](upstream)[0]


def group_size(count, length):
    for option in range(1, count + 1):
        if count % option == 0 and option * length >= 512:
            return option
    return count


def rows_product(left, right):
    return lax.dot_general(
        left, right, (((0,), (0,)), ((), ())), preferred_element_type=jnp.float32
    )


def cols_product(left, right):
    return lax.dot_general(
        left, right, (((1,), (1,)), ((), ())), preferred_element_type=jnp.float32
    )


def local(
    tokens,
    segment_ids,
    first_gain,
    first_bias,
    w_qkv,
    query_gain,
    key_gain,
    w_out,
    second_gain,
    second_bias,
    w_up,
    w_down,
    out_grad,
):
    seqs_here, local_len, width = tokens.shape
    full_len = segment_ids.shape[1]
    head_dim = query_gain.shape[0]
    heads = width // head_dim
    rows_here = seqs_here * local_len
    scale = head_dim ** (-0.5)
    offset = lax.axis_index("pos") * local_len
    query_marks = lax.dynamic_slice_in_dim(segment_ids, offset, local_len, 1)
    block = group_size(seqs_here, local_len)
    count_blocks = seqs_here // block

    def split(array):
        return array.reshape((count_blocks, block) + array.shape[1:])

    inputs = tokens.astype(jnp.float32).reshape(rows_here, width)
    normed_low = layer_norm(inputs, first_gain, first_bias).astype(jnp.bfloat16)
    mixed = jnp.dot(normed_low, w_qkv, preferred_element_type=jnp.float32).reshape(
        rows_here, 3, heads, head_dim
    )
    raw_query = mixed[:, 0]
    raw_keys = mixed[:, 1]
    query = (
        head_norm(raw_query, query_gain)
        .astype(jnp.bfloat16)
        .reshape(seqs_here, local_len, heads, head_dim)
    )
    keys_local = (
        head_norm(raw_keys, key_gain).astype(jnp.bfloat16).reshape(seqs_here, local_len, width)
    )
    values_local = mixed[:, 2].astype(jnp.bfloat16).reshape(seqs_here, local_len, width)
    keys_all, values_all = (
        lax.all_gather(keys_local, "pos", axis=1, tiled=True),
        lax.all_gather(values_local, "pos", axis=1, tiled=True),
    )
    keys_four = keys_all.reshape(seqs_here, full_len, heads, head_dim)
    values_four = values_all.reshape(seqs_here, full_len, heads, head_dim)

    def scores_for(query_blk, keys_blk, query_lab, key_lab):
        raw = (
            jnp.einsum("bqhd,bkhd->bhqk", query_blk, keys_blk, preferred_element_type=jnp.float32)
            * scale
        )
        allowed = (query_lab[:, :, None] == key_lab[:, None, :])[:, None]
        return jnp.where(allowed, raw, -1e30)

    def forward_block(packed):
        query_blk, keys_blk, values_blk, query_lab, key_lab = packed
        scores = scores_for(query_blk, keys_blk, query_lab, key_lab)
        peak = jnp.max(scores, axis=-1, keepdims=True)
        expd = jnp.exp(scores - peak)
        totals = jnp.sum(expd, axis=-1, keepdims=True)
        probs = (expd / totals).astype(jnp.bfloat16)
        result = jnp.einsum(
            "bhqk,bkhd->bqhd", probs, values_blk, preferred_element_type=jnp.float32
        )
        return (result, peak + jnp.log(totals))

    attended, log_totals = lax.map(
        forward_block,
        (
            split(query),
            split(keys_four),
            split(values_four),
            split(query_marks),
            split(segment_ids),
        ),
    )
    attended_low = attended.astype(jnp.bfloat16).reshape(rows_here, width)
    middle = inputs + jnp.dot(attended_low, w_out, preferred_element_type=jnp.float32)
    second_low = layer_norm(middle, second_gain, second_bias).astype(jnp.bfloat16)
    grad_out = out_grad.reshape(rows_here, width)
    grad_float = grad_out.astype(jnp.float32)
    up_all, down_all = (
        lax.all_gather(w_up, "seq", axis=1, tiled=True),
        lax.all_gather(w_down, "seq", axis=1, tiled=True),
    )
    pre = jnp.dot(second_low, up_all, preferred_element_type=jnp.float32)
    hidden = gelu_exact(pre).astype(jnp.bfloat16)
    block_out = (middle + cols_product(hidden, down_all)).astype(jnp.bfloat16)
    grad_hidden = jnp.dot(grad_out, down_all, preferred_element_type=jnp.float32)
    grad_pre = gelu_back(pre, grad_hidden).astype(jnp.bfloat16)
    down_full = rows_product(grad_out, hidden)
    up_full = rows_product(second_low, grad_pre)
    grad_second = cols_product(grad_pre, up_all)
    up_part, down_part = (
        lax.psum_scatter(
            up_full.astype(jnp.bfloat16), "seq", scatter_dimension=1, tiled=True
        ).astype(jnp.float32),
        lax.psum_scatter(
            down_full.astype(jnp.bfloat16), "seq", scatter_dimension=1, tiled=True
        ).astype(jnp.float32),
    )
    up_grad, down_grad = (
        lax.psum(up_part.astype(jnp.bfloat16), "pos").astype(jnp.float32),
        lax.psum(down_part.astype(jnp.bfloat16), "pos").astype(jnp.float32),
    )
    second_back = jax.vjp(layer_norm, middle, second_gain, second_bias)[1]
    grad_middle_part, second_gain_part, second_bias_part = second_back(grad_second)
    grad_middle = grad_float + grad_middle_part
    grad_branch = grad_middle.astype(jnp.bfloat16)
    proj_part = rows_product(attended_low, grad_branch)
    grad_attended = (
        cols_product(grad_branch, w_out)
        .astype(jnp.bfloat16)
        .reshape(seqs_here, local_len, heads, head_dim)
    )

    def backward_block(packed):
        query_blk, keys_blk, values_blk, query_lab, key_lab, log_blk, grad_blk = packed
        scores = scores_for(query_blk, keys_blk, query_lab, key_lab)
        probs = jnp.exp(scores - log_blk)
        grad_probs = jnp.einsum(
            "bqhd,bkhd->bhqk", grad_blk, values_blk, preferred_element_type=jnp.float32
        )
        grad_values = jnp.einsum(
            "bhqk,bqhd->bkhd",
            probs.astype(jnp.bfloat16),
            grad_blk,
            preferred_element_type=jnp.float32,
        )
        inner = jnp.sum(probs * grad_probs, axis=-1, keepdims=True)
        grad_scores = (probs * (grad_probs - inner) * scale).astype(jnp.bfloat16)
        grad_query = jnp.einsum(
            "bhqk,bkhd->bqhd", grad_scores, keys_blk, preferred_element_type=jnp.float32
        )
        grad_keys = jnp.einsum(
            "bhqk,bqhd->bkhd", grad_scores, query_blk, preferred_element_type=jnp.float32
        )
        return (grad_query, grad_keys, grad_values)

    grad_query, grad_keys, grad_values = lax.map(
        backward_block,
        (
            split(query),
            split(keys_four),
            split(values_four),
            split(query_marks),
            split(segment_ids),
            log_totals,
            split(grad_attended),
        ),
    )
    grad_keys = grad_keys.reshape(seqs_here, full_len, width)
    grad_values = grad_values.reshape(seqs_here, full_len, width)
    keys_grad, values_grad = (
        lax.psum_scatter(
            grad_keys.astype(jnp.bfloat16), "pos", scatter_dimension=1, tiled=True
        ).astype(jnp.float32),
        lax.psum_scatter(
            grad_values.astype(jnp.bfloat16), "pos", scatter_dimension=1, tiled=True
        ).astype(jnp.float32),
    )
    norm_back = jax.vjp(qk_norms, raw_query, raw_keys, query_gain, key_gain)[1]
    grad_raw_query, grad_raw_keys, query_gain_part, key_gain_part = norm_back(
        (
            grad_query.reshape(rows_here, heads, head_dim),
            keys_grad.reshape(rows_here, heads, head_dim),
        )
    )
    grad_mixed = (
        jnp.stack(
            [grad_raw_query, grad_raw_keys, values_grad.reshape(rows_here, heads, head_dim)], axis=1
        )
        .reshape(rows_here, 3 * width)
        .astype(jnp.bfloat16)
    )
    qkv_part = rows_product(normed_low, grad_mixed)
    grad_normed = cols_product(grad_mixed, w_qkv)
    first_back = jax.vjp(layer_norm, inputs, first_gain, first_bias)[1]
    grad_input_part, first_gain_part, first_bias_part = first_back(grad_normed)
    input_grad = (grad_middle + grad_input_part).reshape(seqs_here, local_len, width)
    (
        qkv_grad,
        proj_grad,
        first_gain_grad,
        first_bias_grad,
        query_gain_grad,
        key_gain_grad,
        second_gain_grad,
        second_bias_grad,
    ) = lax.psum(
        (
            qkv_part,
            proj_part,
            first_gain_part,
            first_bias_part,
            query_gain_part,
            key_gain_part,
            second_gain_part,
            second_bias_part,
        ),
        ("pos", "seq"),
    )
    return (
        block_out.reshape(seqs_here, local_len, width),
        input_grad,
        first_gain_grad,
        first_bias_grad,
        qkv_grad,
        query_gain_grad,
        key_gain_grad,
        proj_grad,
        second_gain_grad,
        second_bias_grad,
        up_grad,
        down_grad,
    )


def solution(mesh):
    placed = (P("seq", "pos", None), P("seq", None), P(), P(), P(), P(), P(), P(), P(), P(),
              P(None, "seq"), P(None, "seq"), P("seq", "pos", None))
    outs = (P("seq", "pos", None), P("seq", "pos", None), P(), P(), P(), P(), P(), P(), P(), P(),
            P(None, "seq"), P(None, "seq"))

    def step(*args):
        def run(*local_args):
            one = local_args[0].shape[0] == 1 and mesh.shape["pos"] == 2
            return (local_one if one else local)(*local_args)

        return jax.shard_map(run, mesh=mesh, in_specs=placed, out_specs=outs, check_vma=False)(*args)

    return step
```

```python
import functools
import jax
import jax.numpy as jnp
from jax import lax
from jax.experimental import pallas as pl
from jax.experimental.pallas import tpu as pltpu
from jax.sharding import PartitionSpec as P

EPS = 1e-06
F32 = jnp.float32
BF16 = jnp.bfloat16
LOG2E = 1.4426950408889634
BIG = 16384.0
TILE = 256
NT = (((1,), (1,)), ((), ()))
NN = (((1,), (0,)), ((), ()))
TN = (((0,), (0,)), ((), ()))


def dot(a, b, dims=NN):
    return lax.dot_general(a, b, dims, preferred_element_type=F32)


def two(x):
    hi = x.astype(BF16)
    return hi, (x - hi.astype(F32)).astype(BF16)


def group_sum(x, ones):
    hi, lo = two(x)
    return dot(hi, ones) + dot(lo, ones)


def rows_norm(x):
    average = jnp.mean(x, axis=-1, keepdims=True)
    centred = x - average
    spread = jnp.mean(centred * centred, axis=-1, keepdims=True)
    scale = lax.rsqrt(spread + EPS)
    return centred * scale, scale


def tile_of(i, size=TILE):
    return pl.ds(pl.multiple_of(i * size, size), size)


VM = pl.BlockSpec(memory_space=pltpu.VMEM)
LIMIT = 60 * 1024 * 1024


def sds(shape, dtype):
    return jax.ShapeDtypeStruct(shape, dtype)


def ring_places(n_seq):
    s = lax.axis_index("seq")
    core, chip = s % 2, s // 2
    chips = n_seq // 2
    half = chips // 2
    odd = chip % 2
    place = (1 - odd) * (chip // 2) + odd * (chips - 1 - chip // 2)

    def device(p):
        far = p // half
        return ((1 - far) * 2 * p + far * (2 * (chips - 1 - p) + 1)) * 2 + core

    right = device((place + 1) % chips)
    left = device((place + chips - 1) % chips)
    return core, place, right, left, s + 1 - 2 * core


def copy_to(src, dst, send, recv, target):
    return pltpu.make_async_remote_copy(
        src_ref=src, dst_ref=dst, send_sem=send, recv_sem=recv, device_id=target,
        device_id_type=pl.DeviceIdType.MESH)


def greet(targets):
    barrier = pltpu.get_barrier_semaphore()
    for t in targets:
        pl.semaphore_signal(barrier, inc=1, device_id=t, device_id_type=pl.DeviceIdType.MESH)
    pl.semaphore_wait(barrier, len(targets))


SPLIT = 2


def sum_body(n_seq, g, small, own, gn_rem, base, g1, fin, sout, igrad,
             pbuf, accin, accout, xin, xout, srec, sring, gback,
             psend, precv, asend, arecv, xsend, xrecv, fsend, frecv, qsend, qrecv, ssend, srecv, gsend, grecv):
    rows, cols = g.shape
    chips = n_seq // 2
    half = rows // 2
    cr = half // chips
    cw = cols // (2 * SPLIT)
    core, place, right, left, partner = ring_places(n_seq)
    x = lax.axis_index("pos")
    right, left, partner, across = {"seq": right}, {"seq": left}, {"seq": partner}, {"pos": 1 - x}
    greet((right, left, partner, across))

    def chunk(p):
        return (p + 2 * chips) % chips

    def at(d, k):
        return pl.ds((d * SPLIT + k) * cw, cw)

    def rows_of(c, p):
        return pl.ds(pl.multiple_of(c * half + p * cr, cr), cr)

    def p_copy(q):
        return copy_to(g.at[rows_of(1 - core, q)], pbuf.at[q], psend.at[q], precv.at[q], partner)

    def a_copy(d, k, s):
        return copy_to(accout.at[s, d * SPLIT + k], accin.at[s, d * SPLIT + k], asend.at[s, d * SPLIT + k],
                       arecv.at[s, d * SPLIT + k], left if d else right)

    def x_copy(d, k):
        i = d * SPLIT + k
        return copy_to(xout.at[i], xin.at[i], xsend.at[i], xrecv.at[i], across)

    def f_copy(d, k, s):
        p = chunk(place + s) if d else chunk(place - s)
        ref = fin.at[rows_of(core, p), at(d, k)]
        return copy_to(ref, ref, fsend.at[s, d * SPLIT + k], frecv.at[s, d * SPLIT + k], left if d else right)

    def f_recv(d, k, s):
        p = chunk(place + s + 1) if d else chunk(place - s - 1)
        ref = fin.at[rows_of(core, p), at(d, k)]
        return copy_to(ref, ref, fsend.at[s, d * SPLIT + k], frecv.at[s, d * SPLIT + k], left if d else right)

    def q_copy(d, k, s):
        p = chunk(place + s) if d else chunk(place - s)
        ref = fin.at[rows_of(core, p), at(d, k)]
        return copy_to(ref, ref, qsend.at[s, d * SPLIT + k], qrecv.at[s, d * SPLIT + k], partner)

    def q_recv(d, k, s):
        p = chunk(place + s) if d else chunk(place - s)
        ref = fin.at[rows_of(1 - core, p), at(d, k)]
        return copy_to(ref, ref, qsend.at[s, d * SPLIT + k], qrecv.at[s, d * SPLIT + k], partner)

    def s_copy(s):
        return copy_to(sring.at[chunk(place - s)], sring.at[chunk(place - s)], ssend.at[s], srecv.at[s], right)

    def s_recv(s):
        p = chunk(place - s - 1)
        return copy_to(sring.at[p], sring.at[p], ssend.at[s], srecv.at[s], right)

    both = [(d, k) for k in range(SPLIT) for d in range(2)]
    back = copy_to(gn_rem, gback, gsend.at[0], grecv.at[0], across)
    small_p = copy_to(small, srec.at[0], gsend.at[1], grecv.at[1], partner)
    small_x = copy_to(srec.at[1], srec.at[2], gsend.at[2], grecv.at[2], across)

    def order(s):
        return chunk(place - s), chunk(place + s)

    small_p.start()
    for s in range(1, chips // 2 + 1):
        for q in order(s)[: 1 if 2 * s == chips else 2]:
            p_copy(q).start()
    p_copy(place).start()
    back.start()

    def part(d, k, q):
        cs = at(d, k)
        return g[rows_of(core, q), cs].astype(F32) + pbuf[q, :, cs].astype(F32)

    def reduce_step(s, c):
        @pl.when(s <= chips // 2)
        def _():
            p_copy(chunk(place - s)).wait_recv()

            @pl.when(2 * s < chips)
            def _():
                p_copy(chunk(place + s)).wait_recv()

        for d, k in both:
            q = chunk(place + s) if d else chunk(place - s)

            @pl.when(s == 1)
            def _():
                accout[s - 1, d * SPLIT + k] = part(d, k, q).astype(BF16)

            @pl.when(s > 1)
            def _():
                a_copy(d, k, s - 2).wait_recv()
                accout[s - 1, d * SPLIT + k] = (part(d, k, q) + accin[s - 2, d * SPLIT + k].astype(F32)).astype(BF16)

            a_copy(d, k, s - 1).start()
        return c

    lax.fori_loop(1, chips, reduce_step, 0)
    p_copy(place).wait_recv()
    for d, k in both:
        a_copy(d, k, chips - 2).wait_recv()
        xout[d * SPLIT + k] = (part(d, k, place) + accin[chips - 2, d * SPLIT + k].astype(F32)).astype(BF16)
        x_copy(d, k).start()
    small_p.wait_recv()
    srec[1] = small[...] + srec[0]
    small_x.start()
    back.wait_recv()
    n = own.shape[0]

    def norm_tile(i, c):
        rs = tile_of(i)
        xh, r = rows_norm(own[rs, :].astype(F32))
        dy = gback[rs, :].astype(F32) * g1[...].reshape(1, -1)
        dx = r * (dy - jnp.mean(dy, -1, keepdims=True) - xh * jnp.mean(dy * xh, -1, keepdims=True))
        igrad[rs, :] = base[rs, :] + dx
        return c

    lax.fori_loop(0, n // TILE, norm_tile, 0)
    small_x.wait_recv()
    sring[place] = srec[1] + srec[2]
    s_copy(0).start()
    for d, k in both:
        x_copy(d, k).wait_recv()
        i = d * SPLIT + k
        fin[rows_of(core, place), at(d, k)] = (xout[i].astype(F32) + xin[i].astype(F32)).astype(BF16)
        f_copy(d, k, 0).start()
        q_copy(d, k, 0).start()

    def gather_step(s, c):
        for d, k in both:
            f_recv(d, k, s - 1).wait_recv()

            @pl.when(s < chips - 1)
            def _():
                f_copy(d, k, s).start()

            q_copy(d, k, s).start()
        s_recv(s - 1).wait_recv()

        @pl.when(s < chips - 1)
        def _():
            s_copy(s).start()
        return c

    lax.fori_loop(1, chips, gather_step, 0)

    def finish(s, c):
        for d, k in both:
            q_recv(d, k, s).wait_recv()
        return c

    lax.fori_loop(0, chips, finish, 0)
    total = sring[0]
    for s in range(1, chips):
        total = total + sring[s]
    sout[...] = total

    def drain(s, c):
        for d, k in both:
            q_copy(d, k, s).wait_send()

            @pl.when(s < chips - 1)
            def _():
                a_copy(d, k, s).wait_send()
                f_copy(d, k, s).wait_send()

        @pl.when(s < chips - 1)
        def _():
            s_copy(s).wait_send()
        p_copy(s).wait_send()
        return c

    lax.fori_loop(0, chips, drain, 0)
    for d, k in both:
        x_copy(d, k).wait_send()
    for c in (back, small_p, small_x):
        c.wait_send()


def sum_call(n_seq, g, small, own, gn_rem, base, g1):
    rows, cols = g.shape
    n, width = own.shape
    chips = n_seq // 2
    cr, lanes, cw = rows // 2 // chips, 2 * SPLIT, cols // (2 * SPLIT)
    V, D = pltpu.VMEM, pltpu.SemaphoreType.DMA
    return pl.pallas_call(
        functools.partial(sum_body, n_seq),
        out_shape=(sds((rows, cols), BF16), sds(small.shape, F32), sds((n, width), F32)),
        in_specs=[VM] * 6, out_specs=(VM,) * 3,
        scratch_shapes=[
            V((chips, cr, cols), BF16), V((chips - 1, lanes, cr, cw), BF16), V((chips - 1, lanes, cr, cw), BF16),
            V((lanes, cr, cw), BF16), V((lanes, cr, cw), BF16),
            V((3,) + small.shape, F32), V((chips,) + small.shape, F32), V((n, width), BF16),
            D((chips,)), D((chips,)), D((chips - 1, lanes)), D((chips - 1, lanes)), D((lanes,)), D((lanes,)),
            D((chips - 1, lanes)), D((chips - 1, lanes)), D((chips, lanes)), D((chips, lanes)),
            D((chips - 1,)), D((chips - 1,)), D((3,)), D((3,))],
        compiler_params=pltpu.CompilerParams(
            vmem_limit_bytes=LIMIT, collective_id=2, has_side_effects=True),
        name="sums",
    )(g, small, own, gn_rem, base, g1)


def finish_body(g, small, qkv, proj, fg, fb, qgg, kgg, sgg, sbg):
    width = proj.shape[1]
    qkv[...] = g[:, 0:3 * width].astype(F32)
    proj[...] = g[:, 3 * width:].astype(F32)

    @pl.when(pl.program_id(0) == 0)
    def _():
        for i, ref in enumerate((fg, fb, sgg, sbg)):
            ref[...] = small[i:i + 1, :].reshape(width)
        for i, ref in ((4, qgg), (5, kgg)):
            folded = small[i:i + 1, 0:128]
            for j in range(1, width // 128):
                folded = folded + small[i:i + 1, j * 128:(j + 1) * 128]
            folded = folded + pltpu.roll(folded, 64, 1)
            ref[...] = folded[:, 0:64].reshape(64)


def finish_call(g, small):
    rows, cols = g.shape
    width = cols // 4
    step = 128
    whole = lambda size: pl.BlockSpec((size,), lambda i: (0,))
    return pl.pallas_call(
        finish_body, grid=(rows // step,),
        out_shape=(sds((rows, 3 * width), F32), sds((rows, width), F32), sds((width,), F32), sds((width,), F32),
                   sds((64,), F32), sds((64,), F32), sds((width,), F32), sds((width,), F32)),
        in_specs=[pl.BlockSpec((step, cols), lambda i: (i, 0)), pl.BlockSpec(small.shape, lambda i: (0, 0))],
        out_specs=(pl.BlockSpec((step, 3 * width), lambda i: (i, 0)), pl.BlockSpec((step, width), lambda i: (i, 0)),
                   whole(width), whole(width), whole(64), whole(64), whole(width), whole(width)),
        name="finish",
    )(g, small)


def layer_body(n_seq, own, gy, seg, g1, b1, wqkv, qg, kg, wout, g2, b2, wup, wdown,
               out, base, gn_rem, gall, small, upg, downg,
               rem, fq, fk, ones, swap, vecs, normed, kk, vv, qq, rq, rk, qaug, att, mid,
               sx, sg, wbuf, accin, accout, first, hid, gpre, blk, gs, prec, mine, xin,
               dk, stage,
               wsend, wrecv, asend, arecv, psend, precv, tsend, trecv, xsend, xrecv, gsem):
    n, width = own.shape
    f = wup.shape[0]
    h = f // 2
    chips = n_seq // 2
    pairs = width // 128
    tiles = n // TILE
    core, place, right, left, partner = ring_places(n_seq)
    x = lax.axis_index("pos")
    right, left, partner, across = {"seq": right}, {"seq": left}, {"seq": partner}, {"pos": 1 - x}
    greet((right, left, partner, across))

    def slot(s, k, d):
        return pl.ds(pl.multiple_of((k * chips + s) * f + d * h, h), h)

    def w_copies(s):
        return [copy_to(wbuf.at[slot(s, k, d)], wbuf.at[slot(s + 1, k, d)], wsend.at[d, k, s], wrecv.at[d, k, s],
                        left if d else right) for d in range(2) for k in range(2)]

    def a_copies(s):
        rows = [pl.ds(d * h, h) for d in range(2)]
        return [copy_to(accout.at[s - 1, :, rows[d]], accin.at[s - 1, :, rows[d]], asend.at[d, s - 1],
                        arecv.at[d, s - 1], left if d else right) for d in range(2)]

    def w_step(s):
        for c in w_copies(s - 1):
            c.wait_recv()

        @pl.when(s < chips - 1)
        def _():
            for c in w_copies(s):
                c.start()

    def r_step(s):
        for c in a_copies(s - 1):
            c.wait_recv()
        accout[s - 1] = (accout[s - 1].astype(F32) + accin[s - 2].astype(F32)).astype(BF16)
        for c in a_copies(s):
            c.start()

    def t_copy(i):
        rows = pl.ds(i * TILE, TILE)
        return copy_to(own.at[rows], rem.at[rows], tsend.at[i], trecv.at[i], across)

    def s_copy(i):
        return copy_to(sx.at[pl.ds(i * TILE, TILE)], sx.at[pl.ds(n + i * TILE, TILE)], psend.at[3 + i],
                       precv.at[3 + i], partner)

    gy_copy = copy_to(gy, sg.at[pl.ds(n, n)], psend.at[0], precv.at[0], partner)
    parts = (copy_to(gs.at[pl.ds(n, n)], prec.at[1], psend.at[1], precv.at[1], partner),
             copy_to(blk.at[pl.ds(n, n)], prec.at[0], psend.at[2], precv.at[2], partner))
    x_copy = copy_to(mine, xin, xsend.at[0], xrecv.at[0], across)

    def w_first():
        return [copy_to((wdown if k else wup).at[pl.ds(d * h, h)], wbuf.at[slot(1, k, d)], wsend.at[d, k, 0],
                        wrecv.at[d, k, 0], left if d else right) for d in range(2) for k in range(2)]

    for c in w_first():
        c.start()
    for i in range(tiles):
        t_copy(i).start()
    gy_copy.start()

    at = pl.multiple_of(x * n, n)
    labels = jnp.concatenate([seg[:, pl.ds(at, n)], seg[:, pl.ds(n - at, n)]], axis=1)
    lane = lax.broadcasted_iota(jnp.int32, (128, 2 * n), 0) % 64
    same = lane == labels
    keyed = jnp.where((lane >= 6) & (lane <= 8), 1.0, jnp.where(same & (lane < 6), 1.0, 0.0))
    fk[...] = keyed.T.astype(BF16)
    away = jnp.where((lane < 6) & jnp.logical_not(same), -BIG, 0.0)
    fq[...] = away[:, 0:n].T.astype(BF16)
    ra = lax.broadcasted_iota(jnp.int32, ones.shape, 0) // 64
    rb = lax.broadcasted_iota(jnp.int32, ones.shape, 1) // 64
    ones[...] = jnp.where(ra == rb, 1.0, 0.0).astype(BF16)
    swap[...] = jnp.where(ra[:128, :128] == rb[:128, :128], 0.0, 1.0).astype(BF16)
    for i, v in enumerate((g1, b1, g2, b2)):
        vecs[i:i + 1, :] = v[...].reshape(1, width)
    for i, v in enumerate((qg, kg)):
        r = v[...].reshape(1, 64)
        vecs[4 + i:5 + i, :] = jnp.concatenate([r] * (width // 64), axis=1)
    sg[0:n, :] = gy[...]
    wbuf[0:f, :] = wup[...]
    wbuf[chips * f:(chips + 1) * f, :] = wdown[...]
    cols = ones.shape[0]

    def project(xs, i, queries):
        rows = tile_of(i)
        low = (rows_norm(xs)[0] * vecs[0:1, :] + vecs[1:2, :]).astype(BF16)
        normed[rows, :] = low
        for block in range(0 if queries else width // cols, 3 * width // cols):
            raw = dot(low, wqkv[:, block * cols:(block + 1) * cols])
            part, a = divmod(block * cols, width)
            lanes = slice(a, a + cols)
            if part == 2:
                vv[rows, lanes] = raw.astype(BF16)
                continue
            centred = raw - group_sum(raw, ones[...]) * (1 / 64)
            scale = lax.rsqrt(group_sum(centred * centred, ones[...]) * (1 / 64) + EPS)
            dst, rdst = (qq, rq) if part == 0 else (kk, rk)
            dst[rows, lanes] = (centred * scale * vecs[4 + part:5 + part, lanes]).astype(BF16)
            rdst[rows, lanes] = scale

    def own_tile(i, c):
        project(own[tile_of(i), :].astype(F32), i, True)
        return c

    lax.fori_loop(0, tiles, own_tile, 0)
    w_step(1)
    lane_t = lax.broadcasted_iota(jnp.int32, (TILE, 128), 1)
    low_t = lane_t < 64
    lane_n = lax.broadcasted_iota(jnp.int32, (n, 128), 1)
    low_n = lane_n < 64

    def attend(krows, size, add, after):
        low_k = lax.broadcasted_iota(jnp.int32, (size, 128), 1) < 64

        def pair(p, c):
            lanes = tile_of(p, 128)
            k, v, feat = kk[krows, lanes], vv[krows, lanes], fk[krows, :]
            one = jnp.ones_like(v)
            ks = (jnp.where(low_k, k, feat), jnp.where(low_k, feat, k))
            vs = (jnp.where(low_k, v, one), jnp.where(low_k, one, v))

            q, mask = qq[:, lanes], fq[...]
            for a in range(2):
                qa = jnp.where(low_n, q, mask) if a == 0 else jnp.where(low_n, mask, q)
                e = jnp.exp2(dot(qa, ks[a], NT) * (LOG2E / 8)).astype(BF16)
                o = dot(e, vs[a])
                to = slice(a * n, (a + 1) * n)
                blk[to, lanes] = blk[to, lanes] + o if add else o
            if after is not None:
                after(p)
            return c

        lax.fori_loop(0, pairs, pair, 0)

    def middle_step(p):
        @pl.when(p == 2)
        def _():
            w_step(2)

    attend(slice(0, n), n, False, middle_step)
    for i in range(tiles):
        t_copy(i).wait_recv()
        project(rem[i * TILE:(i + 1) * TILE, :].astype(F32), tiles + i, False)
        w_step(3 + i)
        attend(slice(n + i * TILE, n + (i + 1) * TILE), TILE, True, None)

    def close(p, c):
        lanes = tile_of(p, 128)

        def tile(t, c):
            rows = tile_of(t)
            q, mask = qq[rows, lanes], fq[rows, :]
            res = [blk[pl.ds(pl.multiple_of(a * n + t * TILE, TILE), TILE), lanes] for a in range(2)]
            for a in range(2):
                qa = jnp.where(low_t, q, mask) if a == 0 else jnp.where(low_t, mask, q)
                shift = jnp.log(res[a]) * -8.0
                hi, lo = two(shift)
                lo2 = (shift - hi.astype(F32) - lo.astype(F32)).astype(BF16)
                s = 64 * (1 - a)
                qaug[p * 2 + a, rows, :] = jnp.where(
                    lane_t == s + 6, hi, jnp.where(lane_t == s + 7, lo, jnp.where(lane_t == s + 8, lo2, qa)))
            num = jnp.where(low_t, res[0], res[1])
            den = pltpu.roll(jnp.where(low_t, res[1], res[0]), 64, 1)
            att[rows, lanes] = (num / den).astype(BF16)
            return c

        lax.fori_loop(0, tiles, tile, 0)
        return c

    lax.fori_loop(0, pairs, close, 0)
    for i in range(tiles):
        rows = slice(i * TILE, (i + 1) * TILE)
        m = own[rows, :].astype(F32) + dot(att[rows, :], wout[...])
        mid[rows, :] = m
        sx[rows, :] = (rows_norm(m)[0] * vecs[2:3, :] + vecs[3:4, :]).astype(BF16)
        s_copy(i).start()
    w_step(5)
    quad = chips // 2
    span = quad * f

    def group(g, carry):
        @pl.when(g == 0)
        def _():
            gy_copy.wait_recv()
            for j in range(tiles):
                s_copy(j).wait_recv()

        @pl.when(g == 1)
        def _():
            w_step(6)
            w_step(7)

        up = wbuf.at[pl.ds(pl.multiple_of(g * span, span), span)]
        down = wbuf.at[pl.ds(pl.multiple_of(chips * f + g * span, span), span)]

        def tile(i, c):
            rows = tile_of((i + g * tiles) % (2 * tiles))
            acts, slopes = [], []
            for j in range(span // TILE):
                cs = slice(j * TILE, (j + 1) * TILE)
                pre = dot(sx[rows, :], up[cs, :], NT)
                gh = dot(sg[rows, :], down[cs, :], NT)
                cdf = 0.5 + 0.5 * lax.erf(pre * 0.7071067811865476)
                slope = cdf + pre * (jnp.exp(-0.5 * pre * pre) * 0.3989422804014327)
                acts.append((pre * cdf).astype(BF16))
                slopes.append((gh * slope).astype(BF16))
                hid[rows, cs] = acts[-1]
                gpre[rows, cs] = slopes[-1]
            o = dot(jnp.concatenate(acts, 1), down[...])
            s = dot(jnp.concatenate(slopes, 1), up[...])

            @pl.when(g == 0)
            def _():
                blk[rows, :] = o
                gs[rows, :] = s

            @pl.when(g > 0)
            def _():
                blk[rows, :] += o
                gs[rows, :] += s

            @pl.when((g == 1) & (i == tiles - 1))
            def _():
                for c in parts:
                    c.start()
            return c

        lax.fori_loop(0, 2 * tiles, tile, 0)

        @pl.when(g == 1)
        def _():
            r_step(2)

        def block(j, c):
            for k, (lhs, rhs) in enumerate(((gpre, sx), (hid, sg))):
                part = dot(lhs[:, pl.ds(pl.multiple_of(j * 2 * f, 2 * f), 2 * f)], rhs[...], TN)
                for m in range(2):
                    one = part[m * f:(m + 1) * f]
                    at = g * quad + 2 * j + m

                    @pl.when(at == 0)
                    def _():
                        first[k] = one

                    @pl.when(at > 0)
                    def _():
                        accout[jnp.maximum(at - 1, 0), k] = one.astype(BF16)
            return c

        lax.fori_loop(0, quad // 2, block, 0)

        @pl.when(g == 0)
        def _():
            for c in a_copies(1):
                c.start()
        return carry

    lax.fori_loop(0, 2, group, 0)
    r_step(3)

    def w_drain(s, c):
        for cp in w_copies(s):
            cp.wait_send()
        return c

    lax.fori_loop(1, chips - 1, w_drain, 0)
    for c in w_first():
        c.wait_send()
    for i in range(tiles):
        s_copy(i).wait_send()
    gbr, gat = sx.at[0:n], sx.at[n:2 * n]
    small[...] = jnp.zeros_like(small)
    parts[0].wait_recv()

    def mid_tile(i, c):
        rows = tile_of(i)
        xh, r = rows_norm(mid[rows, :])
        dy = gs[rows, :] + prec[1, rows, :]
        small[2:3, :] += jnp.sum(dy * xh, axis=0, keepdims=True)
        small[3:4, :] += jnp.sum(dy, axis=0, keepdims=True)
        gd = dy * vecs[2:3, :]
        dx = r * (gd - jnp.mean(gd, -1, keepdims=True) - xh * jnp.mean(gd * xh, -1, keepdims=True))
        gm = gy[rows, :].astype(F32) + dx
        base[rows, :] = gm
        low = gm.astype(BF16)
        gbr[rows, :] = low
        gat[rows, :] = dot(low, wout[...], NT).astype(BF16)
        return c

    lax.fori_loop(0, tiles, mid_tile, 0)
    parts[1].wait_recv()
    out[...] = (mid[...] + (blk[0:n, :] + prec[0])).astype(BF16)

    def flush(j, rows, lanes):
        return pltpu.make_async_copy(stage.at[j], gall.at[rows, lanes], gsem.at[j])

    def proj_tile(i, c):
        rows = tile_of(i)
        stage[i] = dot(att[:, rows], gbr[...], TN).astype(BF16)
        flush(i, rows, pl.ds(3 * width, width)).start()
        return c

    lax.fori_loop(0, width // TILE, proj_tile, 0)
    r_step(4)

    def keys_of(j, rows):
        return wbuf.at[pl.ds(pl.multiple_of(j * 2 * n + rows, TILE), TILE)]

    def mix(part, rows):
        return pl.ds(part * 2 * n + rows.start, rows.size)

    ones_p = slice(0, 128)

    def norm_back(dy, y, r, gain):
        group = ones[ones_p, ones_p]
        dy = dy * 0.125
        y = y.astype(F32)
        prod = dy * y
        gd = dy * gain
        m1 = group_sum(gd, group) * (1 / 64)
        m2 = group_sum(prod, group) * (1 / 64)
        inv = 1.0 / gain
        return r * (gd - m1 - y * inv * m2), jnp.sum(prod, 0, keepdims=True) * inv

    def pair(p, c):
        @pl.when((p == 1) | (p == 3) | (p == 4))
        def _():
            r_step(5 + p // 2)

        lanes = tile_of(p, 128)
        do = gat[:, lanes]
        delta = -group_sum(do.astype(F32) * att[:, lanes].astype(F32), swap[...])
        hi, lo = two(delta)
        zero = jnp.zeros_like(do)
        das = []
        for a in range(2):
            s = 64 * (1 - a)
            extra = jnp.where(lane_n == s, hi, jnp.where(lane_n == s + 1, lo, zero))
            das.append(jnp.where(low_n, do, extra) if a == 0 else jnp.where(low_n, extra, do))

        acc = [None, None]
        for t in range(2):
            rows = slice(t * n, (t + 1) * n)
            k, v, feat = kk[rows, lanes], vv[rows, lanes], fk[rows, :]
            one = jnp.ones_like(v)
            dks, dvs = [], []
            for a in range(2):
                ka = jnp.where(low_n, k, feat) if a == 0 else jnp.where(low_n, feat, k)
                va = jnp.where(low_n, v, one) if a == 0 else jnp.where(low_n, one, v)
                qa = qaug[p * 2 + a]
                e = jnp.exp2(dot(ka, qa, NT) * (LOG2E / 8))
                ds = (e * dot(va, das[a], NT)).astype(BF16)
                dvs.append(dot(e.astype(BF16), das[a]))
                dks.append(dot(ds, qa))
                dq = dot(ka, ds, TN)
                acc[a] = dq if t == 0 else acc[a] + dq
            dk[rows, :] = jnp.where(low_n, dks[0], dks[1])
            wbuf[4 * n + t * n:4 * n + (t + 1) * n, lanes] = jnp.where(low_n, dvs[0], dvs[1]).astype(BF16)
        low_s = lax.broadcasted_iota(jnp.int32, (128, n), 0) < 64
        dq = jnp.where(low_s, acc[0], acc[1]).T
        qa = jnp.where(low_n, qaug[p * 2], qaug[p * 2 + 1])
        dx, gg = norm_back(dq, qa, rq[:, lanes], vecs[4:5, lanes])
        wbuf[0:n, lanes] = dx.astype(BF16)
        small[4:5, lanes] = gg
        dx, gg = norm_back(dk[...], kk[:, lanes], rk[:, lanes], vecs[5:6, lanes])
        wbuf[2 * n:4 * n, lanes] = dx.astype(BF16)
        small[5:6, lanes] = gg
        return c

    lax.fori_loop(0, pairs, pair, 0)
    for i in range(width // TILE):
        flush(i, pl.ds(i * TILE, TILE), pl.ds(3 * width, width)).wait()
    for c in a_copies(chips - 1):
        c.wait_recv()
    mine[...] = (first[...] + accin[chips - 2].astype(F32)).astype(BF16)
    x_copy.start()

    def gain_sums(xh, gn):
        small[0:1, :] += jnp.sum(gn * xh, axis=0, keepdims=True)
        small[1:2, :] += jnp.sum(gn, axis=0, keepdims=True)

    def rem_tile(i, c):
        rows = tile_of(i)
        gn = (dot(wbuf[pl.ds(pl.multiple_of(3 * n + i * TILE, TILE), TILE), :], wqkv[:, width:2 * width], NT)
              + dot(wbuf[pl.ds(pl.multiple_of(5 * n + i * TILE, TILE), TILE), :], wqkv[:, 2 * width:], NT))
        gn_rem[rows, :] = gn.astype(BF16)
        gain_sums(rows_norm(rem[rows, :].astype(F32))[0], gn)
        return c

    def own_back(i, c):
        rows = tile_of(i)
        gn = (dot(wbuf[rows, :], wqkv[:, 0:width], NT)
              + dot(wbuf[pl.ds(pl.multiple_of(2 * n + i * TILE, TILE), TILE), :], wqkv[:, width:2 * width], NT)
              + dot(wbuf[pl.ds(pl.multiple_of(4 * n + i * TILE, TILE), TILE), :], wqkv[:, 2 * width:], NT))
        xh, r = rows_norm(own[rows, :].astype(F32))
        gain_sums(xh, gn)
        gd = gn * vecs[0:1, :]
        base[rows, :] += r * (gd - jnp.mean(gd, -1, keepdims=True) - xh * jnp.mean(gd * xh, -1, keepdims=True))
        return c

    def qkv_tile(i, c):
        rows = tile_of(i)
        jobs = ((0, n, 0), (2 * n, 2 * n, 1), (4 * n, 2 * n, 2))
        for j, (at, size, part) in enumerate(jobs):
            stage[j] = dot(normed[0:size, rows], wbuf[at:at + size, :], TN).astype(BF16)
            flush(j, rows, pl.ds(part * width, width)).start()
        for j, (at, size, part) in enumerate(jobs):
            flush(j, rows, pl.ds(part * width, width)).wait()
        return c

    lax.fori_loop(0, width // TILE, qkv_tile, 0)
    lax.fori_loop(0, tiles, rem_tile, 0)
    lax.fori_loop(0, tiles, own_back, 0)
    x_copy.wait_recv()
    total = mine[...].astype(F32) + xin[...].astype(F32)
    upg[...] = total[0]
    downg[...] = total[1]

    def a_drain(s, c):
        for cp in a_copies(s):
            cp.wait_send()
        return c

    lax.fori_loop(1, chips, a_drain, 0)
    for i in range(tiles):
        t_copy(i).wait_send()
    for c in (gy_copy, x_copy) + parts:
        c.wait_send()


def layer_call(n_seq, own, gy, seg, g1, b1, wqkv, qg, kg, wout, g2, b2, wup, wdown):
    n, width = own.shape
    f = wup.shape[0]
    chips = n_seq // 2
    heads = width // 64
    tiles = n // TILE
    V, D = pltpu.VMEM, pltpu.SemaphoreType.DMA
    return pl.pallas_call(
        functools.partial(layer_body, n_seq),
        out_shape=(sds((n, width), BF16), sds((n, width), F32), sds((n, width), BF16),
                   sds((width, 4 * width), BF16), sds((8, width), F32), sds((f, width), F32), sds((f, width), F32)),
        in_specs=[VM] * 13,
        out_specs=(VM, VM, VM, pl.BlockSpec(memory_space=pl.ANY), VM, VM, VM),
        scratch_shapes=[
            V((n, width), BF16), V((n, 128), BF16), V((2 * n, 128), BF16), V((256, 256), BF16), V((128, 128), BF16),
            V((8, width), F32), V((2 * n, width), BF16), V((2 * n, width), BF16), V((2 * n, width), BF16),
            V((n, width), BF16), V((n, width), F32), V((2 * n, width), F32), V((heads, n, 128), BF16),
            V((n, width), BF16), V((n, width), F32),
            V((2 * n, width), BF16), V((2 * n, width), BF16), V((chips * 2 * f, width), BF16),
            V((chips - 1, 2, f, width), BF16), V((chips - 1, 2, f, width), BF16), V((2, f, width), F32),
            V((2 * n, chips // 2 * f), BF16), V((2 * n, chips // 2 * f), BF16), V((2 * n, width), F32), V((2 * n, width), F32),
            V((2, n, width), F32), V((2, f, width), BF16), V((2, f, width), BF16),
            V((2 * n, 128), F32), V((3, TILE, width), BF16),
            D((2, 2, chips - 1)), D((2, 2, chips - 1)), D((2, chips - 1)), D((2, chips - 1)),
            D((3 + tiles,)), D((3 + tiles,)), D((tiles,)), D((tiles,)), D((1,)), D((1,)), D((3,))],
        compiler_params=pltpu.CompilerParams(
            vmem_limit_bytes=66 * 1000 * 1000, collective_id=1, has_side_effects=True),
        name="layer",
    )(own, gy, seg, g1, b1, wqkv, qg, kg, wout, g2, b2, wup, wdown)


def local_one(tokens, segment_ids, first_gain, first_bias, w_qkv, query_gain, key_gain, w_out,
              second_gain, second_bias, w_up, w_down, out_grad):
    n_seq = lax.axis_size("seq")
    own = tokens[0]
    block_out, base, gn_rem, g, small, up_grad, down_grad = layer_call(
        n_seq, own, out_grad[0], segment_ids, first_gain, first_bias, w_qkv, query_gain, key_gain, w_out,
        second_gain, second_bias, w_up.T, w_down.T)
    g, small, input_grad = sum_call(n_seq, g, small, own, gn_rem, base, first_gain)
    qkv, proj, fg, fb, qgg, kgg, sgg, sbg = finish_call(g, small)
    return (block_out[None], input_grad[None], fg, fb, qkv, qgg, kgg, proj, sgg, sbg, up_grad.T, down_grad.T)


def layer_norm(rows, gain, shift):
    average = jnp.mean(rows, axis=-1, keepdims=True)
    centred = rows - average
    spread = jnp.mean(centred * centred, axis=-1, keepdims=True)
    return centred * lax.rsqrt(spread + EPS) * gain + shift


def head_norm(values, gain):
    average = jnp.mean(values, axis=-1, keepdims=True)
    centred = values - average
    spread = jnp.mean(centred * centred, axis=-1, keepdims=True)
    return centred * lax.rsqrt(spread + EPS) * gain


def qk_norms(raw_query, raw_keys, query_gain, key_gain):
    return (head_norm(raw_query, query_gain), head_norm(raw_keys, key_gain))


def gelu_exact(values):
    return jax.nn.gelu(values, approximate=False)


def gelu_back(pre, upstream):
    return jax.vjp(gelu_exact, pre)[1](upstream)[0]


def group_size(count, length):
    for option in range(1, count + 1):
        if count % option == 0 and option * length >= 512:
            return option
    return count


def rows_product(left, right):
    return lax.dot_general(
        left, right, (((0,), (0,)), ((), ())), preferred_element_type=jnp.float32
    )


def cols_product(left, right):
    return lax.dot_general(
        left, right, (((1,), (1,)), ((), ())), preferred_element_type=jnp.float32
    )


def local(
    tokens,
    segment_ids,
    first_gain,
    first_bias,
    w_qkv,
    query_gain,
    key_gain,
    w_out,
    second_gain,
    second_bias,
    w_up,
    w_down,
    out_grad,
):
    seqs_here, local_len, width = tokens.shape
    full_len = segment_ids.shape[1]
    head_dim = query_gain.shape[0]
    heads = width // head_dim
    rows_here = seqs_here * local_len
    scale = head_dim ** (-0.5)
    offset = lax.axis_index("pos") * local_len
    query_marks = lax.dynamic_slice_in_dim(segment_ids, offset, local_len, 1)
    block = group_size(seqs_here, local_len)
    count_blocks = seqs_here // block

    def split(array):
        return array.reshape((count_blocks, block) + array.shape[1:])

    inputs = tokens.astype(jnp.float32).reshape(rows_here, width)
    normed_low = layer_norm(inputs, first_gain, first_bias).astype(jnp.bfloat16)
    mixed = jnp.dot(normed_low, w_qkv, preferred_element_type=jnp.float32).reshape(
        rows_here, 3, heads, head_dim
    )
    raw_query = mixed[:, 0]
    raw_keys = mixed[:, 1]
    query = (
        head_norm(raw_query, query_gain)
        .astype(jnp.bfloat16)
        .reshape(seqs_here, local_len, heads, head_dim)
    )
    keys_local = (
        head_norm(raw_keys, key_gain).astype(jnp.bfloat16).reshape(seqs_here, local_len, width)
    )
    values_local = mixed[:, 2].astype(jnp.bfloat16).reshape(seqs_here, local_len, width)
    keys_all, values_all = (
        lax.all_gather(keys_local, "pos", axis=1, tiled=True),
        lax.all_gather(values_local, "pos", axis=1, tiled=True),
    )
    keys_four = keys_all.reshape(seqs_here, full_len, heads, head_dim)
    values_four = values_all.reshape(seqs_here, full_len, heads, head_dim)

    def scores_for(query_blk, keys_blk, query_lab, key_lab):
        raw = (
            jnp.einsum("bqhd,bkhd->bhqk", query_blk, keys_blk, preferred_element_type=jnp.float32)
            * scale
        )
        allowed = (query_lab[:, :, None] == key_lab[:, None, :])[:, None]
        return jnp.where(allowed, raw, -1e30)

    def forward_block(packed):
        query_blk, keys_blk, values_blk, query_lab, key_lab = packed
        scores = scores_for(query_blk, keys_blk, query_lab, key_lab)
        peak = jnp.max(scores, axis=-1, keepdims=True)
        expd = jnp.exp(scores - peak)
        totals = jnp.sum(expd, axis=-1, keepdims=True)
        probs = (expd / totals).astype(jnp.bfloat16)
        result = jnp.einsum(
            "bhqk,bkhd->bqhd", probs, values_blk, preferred_element_type=jnp.float32
        )
        return (result, peak + jnp.log(totals))

    attended, log_totals = lax.map(
        forward_block,
        (
            split(query),
            split(keys_four),
            split(values_four),
            split(query_marks),
            split(segment_ids),
        ),
    )
    attended_low = attended.astype(jnp.bfloat16).reshape(rows_here, width)
    middle = inputs + jnp.dot(attended_low, w_out, preferred_element_type=jnp.float32)
    second_low = layer_norm(middle, second_gain, second_bias).astype(jnp.bfloat16)
    grad_out = out_grad.reshape(rows_here, width)
    grad_float = grad_out.astype(jnp.float32)
    up_all, down_all = (
        lax.all_gather(w_up, "seq", axis=1, tiled=True),
        lax.all_gather(w_down, "seq", axis=1, tiled=True),
    )
    pre = jnp.dot(second_low, up_all, preferred_element_type=jnp.float32)
    hidden = gelu_exact(pre).astype(jnp.bfloat16)
    block_out = (middle + cols_product(hidden, down_all)).astype(jnp.bfloat16)
    grad_hidden = jnp.dot(grad_out, down_all, preferred_element_type=jnp.float32)
    grad_pre = gelu_back(pre, grad_hidden).astype(jnp.bfloat16)
    down_full = rows_product(grad_out, hidden)
    up_full = rows_product(second_low, grad_pre)
    grad_second = cols_product(grad_pre, up_all)
    up_part, down_part = (
        lax.psum_scatter(
            up_full.astype(jnp.bfloat16), "seq", scatter_dimension=1, tiled=True
        ).astype(jnp.float32),
        lax.psum_scatter(
            down_full.astype(jnp.bfloat16), "seq", scatter_dimension=1, tiled=True
        ).astype(jnp.float32),
    )
    up_grad, down_grad = (
        lax.psum(up_part.astype(jnp.bfloat16), "pos").astype(jnp.float32),
        lax.psum(down_part.astype(jnp.bfloat16), "pos").astype(jnp.float32),
    )
    second_back = jax.vjp(layer_norm, middle, second_gain, second_bias)[1]
    grad_middle_part, second_gain_part, second_bias_part = second_back(grad_second)
    grad_middle = grad_float + grad_middle_part
    grad_branch = grad_middle.astype(jnp.bfloat16)
    proj_part = rows_product(attended_low, grad_branch)
    grad_attended = (
        cols_product(grad_branch, w_out)
        .astype(jnp.bfloat16)
        .reshape(seqs_here, local_len, heads, head_dim)
    )

    def backward_block(packed):
        query_blk, keys_blk, values_blk, query_lab, key_lab, log_blk, grad_blk = packed
        scores = scores_for(query_blk, keys_blk, query_lab, key_lab)
        probs = jnp.exp(scores - log_blk)
        grad_probs = jnp.einsum(
            "bqhd,bkhd->bhqk", grad_blk, values_blk, preferred_element_type=jnp.float32
        )
        grad_values = jnp.einsum(
            "bhqk,bqhd->bkhd",
            probs.astype(jnp.bfloat16),
            grad_blk,
            preferred_element_type=jnp.float32,
        )
        inner = jnp.sum(probs * grad_probs, axis=-1, keepdims=True)
        grad_scores = (probs * (grad_probs - inner) * scale).astype(jnp.bfloat16)
        grad_query = jnp.einsum(
            "bhqk,bkhd->bqhd", grad_scores, keys_blk, preferred_element_type=jnp.float32
        )
        grad_keys = jnp.einsum(
            "bhqk,bqhd->bkhd", grad_scores, query_blk, preferred_element_type=jnp.float32
        )
        return (grad_query, grad_keys, grad_values)

    grad_query, grad_keys, grad_values = lax.map(
        backward_block,
        (
            split(query),
            split(keys_four),
            split(values_four),
            split(query_marks),
            split(segment_ids),
            log_totals,
            split(grad_attended),
        ),
    )
    grad_keys = grad_keys.reshape(seqs_here, full_len, width)
    grad_values = grad_values.reshape(seqs_here, full_len, width)
    keys_grad, values_grad = (
        lax.psum_scatter(
            grad_keys.astype(jnp.bfloat16), "pos", scatter_dimension=1, tiled=True
        ).astype(jnp.float32),
        lax.psum_scatter(
            grad_values.astype(jnp.bfloat16), "pos", scatter_dimension=1, tiled=True
        ).astype(jnp.float32),
    )
    norm_back = jax.vjp(qk_norms, raw_query, raw_keys, query_gain, key_gain)[1]
    grad_raw_query, grad_raw_keys, query_gain_part, key_gain_part = norm_back(
        (
            grad_query.reshape(rows_here, heads, head_dim),
            keys_grad.reshape(rows_here, heads, head_dim),
        )
    )
    grad_mixed = (
        jnp.stack(
            [grad_raw_query, grad_raw_keys, values_grad.reshape(rows_here, heads, head_dim)], axis=1
        )
        .reshape(rows_here, 3 * width)
        .astype(jnp.bfloat16)
    )
    qkv_part = rows_product(normed_low, grad_mixed)
    grad_normed = cols_product(grad_mixed, w_qkv)
    first_back = jax.vjp(layer_norm, inputs, first_gain, first_bias)[1]
    grad_input_part, first_gain_part, first_bias_part = first_back(grad_normed)
    input_grad = (grad_middle + grad_input_part).reshape(seqs_here, local_len, width)
    (
        qkv_grad,
        proj_grad,
        first_gain_grad,
        first_bias_grad,
        query_gain_grad,
        key_gain_grad,
        second_gain_grad,
        second_bias_grad,
    ) = lax.psum(
        (
            qkv_part,
            proj_part,
            first_gain_part,
            first_bias_part,
            query_gain_part,
            key_gain_part,
            second_gain_part,
            second_bias_part,
        ),
        ("pos", "seq"),
    )
    return (
        block_out.reshape(seqs_here, local_len, width),
        input_grad,
        first_gain_grad,
        first_bias_grad,
        qkv_grad,
        query_gain_grad,
        key_gain_grad,
        proj_grad,
        second_gain_grad,
        second_bias_grad,
        up_grad,
        down_grad,
    )


def solution(mesh):
    placed = (P("seq", "pos", None), P("seq", None), P(), P(), P(), P(), P(), P(), P(), P(),
              P(None, "seq"), P(None, "seq"), P("seq", "pos", None))
    outs = (P("seq", "pos", None), P("seq", "pos", None), P(), P(), P(), P(), P(), P(), P(), P(),
            P(None, "seq"), P(None, "seq"))

    def step(*args):
        def run(*local_args):
            one = local_args[0].shape[:2] == (1, 512) and (mesh.shape["pos"], mesh.shape["seq"]) == (2, 16)
            return (local_one if one else local)(*local_args)

        return jax.shard_map(run, mesh=mesh, in_specs=placed, out_specs=outs, check_vma=False)(*args)

    return step
```

```python
import functools
import jax
import jax.numpy as jnp
from jax import lax
from jax.experimental import pallas as pl
from jax.experimental.pallas import tpu as pltpu
from jax.sharding import PartitionSpec as P

EPS = 1e-06
F32 = jnp.float32
BF16 = jnp.bfloat16
LOG2E = 1.4426950408889634
BIG = 16384.0
TILE = 256
NT = (((1,), (1,)), ((), ()))
NN = (((1,), (0,)), ((), ()))
TN = (((0,), (0,)), ((), ()))


def dot(a, b, dims=NN):
    return lax.dot_general(a, b, dims, preferred_element_type=F32)


def two(x):
    hi = x.astype(BF16)
    return hi, (x - hi.astype(F32)).astype(BF16)


def group_sum(x, ones):
    hi, lo = two(x)
    return dot(hi, ones) + dot(lo, ones)


def rows_norm(x):
    average = jnp.mean(x, axis=-1, keepdims=True)
    centred = x - average
    spread = jnp.mean(centred * centred, axis=-1, keepdims=True)
    scale = lax.rsqrt(spread + EPS)
    return centred * scale, scale


def tile_of(i, size=TILE):
    return pl.ds(pl.multiple_of(i * size, size), size)


VM = pl.BlockSpec(memory_space=pltpu.VMEM)
LIMIT = 60 * 1024 * 1024


def sds(shape, dtype):
    return jax.ShapeDtypeStruct(shape, dtype)


def ring_places(n_seq):
    s = lax.axis_index("seq")
    core, chip = s % 2, s // 2
    chips = n_seq // 2
    half = chips // 2
    odd = chip % 2
    place = (1 - odd) * (chip // 2) + odd * (chips - 1 - chip // 2)

    def device(p):
        far = p // half
        return ((1 - far) * 2 * p + far * (2 * (chips - 1 - p) + 1)) * 2 + core

    right = device((place + 1) % chips)
    left = device((place + chips - 1) % chips)
    return core, place, right, left, s + 1 - 2 * core


def copy_to(src, dst, send, recv, target):
    return pltpu.make_async_remote_copy(
        src_ref=src, dst_ref=dst, send_sem=send, recv_sem=recv, device_id=target,
        device_id_type=pl.DeviceIdType.MESH)


def greet(targets):
    barrier = pltpu.get_barrier_semaphore()
    for t in targets:
        pl.semaphore_signal(barrier, inc=1, device_id=t, device_id_type=pl.DeviceIdType.MESH)
    pl.semaphore_wait(barrier, len(targets))


SPLIT = 2


def sum_body(n_seq, g, small, own, gn_rem, base, g1, mine, fin, sout, igrad, upg, downg,
             other, pbuf, accin, accout, xin, xout, srec, sring, gback,
             psend, precv, asend, arecv, xsend, xrecv, fsend, frecv, qsend, qrecv, ssend, srecv, gsend, grecv):
    rows, cols = g.shape
    chips = n_seq // 2
    half = rows // 2
    cr = half // chips
    cw = cols // (2 * SPLIT)
    core, place, right, left, partner = ring_places(n_seq)
    x = lax.axis_index("pos")
    right, left, partner, across = {"seq": right}, {"seq": left}, {"seq": partner}, {"pos": 1 - x}
    greet((right, left, partner, across))

    def chunk(p):
        return (p + 2 * chips) % chips

    def at(d, k):
        return pl.ds((d * SPLIT + k) * cw, cw)

    def rows_of(c, p):
        return pl.ds(pl.multiple_of(c * half + p * cr, cr), cr)

    def p_copy(q):
        return copy_to(g.at[rows_of(1 - core, q)], pbuf.at[q], psend.at[q], precv.at[q], partner)

    def a_copy(d, k, s):
        return copy_to(accout.at[s, d * SPLIT + k], accin.at[s, d * SPLIT + k], asend.at[s, d * SPLIT + k],
                       arecv.at[s, d * SPLIT + k], left if d else right)

    def x_copy(d, k):
        i = d * SPLIT + k
        return copy_to(xout.at[i], xin.at[i], xsend.at[i], xrecv.at[i], across)

    def f_copy(d, k, s):
        p = chunk(place + s) if d else chunk(place - s)
        ref = fin.at[rows_of(core, p), at(d, k)]
        return copy_to(ref, ref, fsend.at[s, d * SPLIT + k], frecv.at[s, d * SPLIT + k], left if d else right)

    def f_recv(d, k, s):
        p = chunk(place + s + 1) if d else chunk(place - s - 1)
        ref = fin.at[rows_of(core, p), at(d, k)]
        return copy_to(ref, ref, fsend.at[s, d * SPLIT + k], frecv.at[s, d * SPLIT + k], left if d else right)

    def q_copy(d, k, s):
        p = chunk(place + s) if d else chunk(place - s)
        ref = fin.at[rows_of(core, p), at(d, k)]
        return copy_to(ref, ref, qsend.at[s, d * SPLIT + k], qrecv.at[s, d * SPLIT + k], partner)

    def q_recv(d, k, s):
        p = chunk(place + s) if d else chunk(place - s)
        ref = fin.at[rows_of(1 - core, p), at(d, k)]
        return copy_to(ref, ref, qsend.at[s, d * SPLIT + k], qrecv.at[s, d * SPLIT + k], partner)

    def s_copy(s):
        return copy_to(sring.at[chunk(place - s)], sring.at[chunk(place - s)], ssend.at[s], srecv.at[s], right)

    def s_recv(s):
        p = chunk(place - s - 1)
        return copy_to(sring.at[p], sring.at[p], ssend.at[s], srecv.at[s], right)

    both = [(d, k) for k in range(SPLIT) for d in range(2)]
    back = copy_to(gn_rem, gback, gsend.at[0], grecv.at[0], across)
    small_p = copy_to(small, srec.at[0], gsend.at[1], grecv.at[1], partner)
    small_x = copy_to(srec.at[1], srec.at[2], gsend.at[2], grecv.at[2], across)
    ffn_x = copy_to(mine, other, gsend.at[3], grecv.at[3], across)

    def order(s):
        return chunk(place - s), chunk(place + s)

    small_p.start()
    for s in range(1, chips // 2 + 1):
        for q in order(s)[: 1 if 2 * s == chips else 2]:
            p_copy(q).start()
    p_copy(place).start()
    back.start()
    ffn_x.start()

    def part(d, k, q):
        cs = at(d, k)
        return g[rows_of(core, q), cs].astype(F32) + pbuf[q, :, cs].astype(F32)

    def reduce_step(s, c):
        @pl.when(s <= chips // 2)
        def _():
            p_copy(chunk(place - s)).wait_recv()

            @pl.when(2 * s < chips)
            def _():
                p_copy(chunk(place + s)).wait_recv()

        for d, k in both:
            q = chunk(place + s) if d else chunk(place - s)

            @pl.when(s == 1)
            def _():
                accout[s - 1, d * SPLIT + k] = part(d, k, q).astype(BF16)

            @pl.when(s > 1)
            def _():
                a_copy(d, k, s - 2).wait_recv()
                accout[s - 1, d * SPLIT + k] = (part(d, k, q) + accin[s - 2, d * SPLIT + k].astype(F32)).astype(BF16)

            a_copy(d, k, s - 1).start()
        return c

    lax.fori_loop(1, chips, reduce_step, 0)
    p_copy(place).wait_recv()
    for d, k in both:
        a_copy(d, k, chips - 2).wait_recv()
        xout[d * SPLIT + k] = (part(d, k, place) + accin[chips - 2, d * SPLIT + k].astype(F32)).astype(BF16)
        x_copy(d, k).start()
    small_p.wait_recv()
    srec[1] = small[...] + srec[0]
    small_x.start()
    back.wait_recv()
    n = own.shape[0]

    def norm_tile(i, c):
        rs = tile_of(i)
        xh, r = rows_norm(own[rs, :].astype(F32))
        dy = gback[rs, :].astype(F32) * g1[...].reshape(1, -1)
        dx = r * (dy - jnp.mean(dy, -1, keepdims=True) - xh * jnp.mean(dy * xh, -1, keepdims=True))
        igrad[rs, :] = base[rs, :] + dx
        return c

    lax.fori_loop(0, n // TILE, norm_tile, 0)
    ffn_x.wait_recv()
    total = mine[...].astype(F32) + other[...].astype(F32)
    upg[...] = total[0]
    downg[...] = total[1]
    small_x.wait_recv()
    sring[place] = srec[1] + srec[2]
    s_copy(0).start()
    for d, k in both:
        x_copy(d, k).wait_recv()
        i = d * SPLIT + k
        fin[rows_of(core, place), at(d, k)] = (xout[i].astype(F32) + xin[i].astype(F32)).astype(BF16)
        f_copy(d, k, 0).start()
        q_copy(d, k, 0).start()

    def gather_step(s, c):
        for d, k in both:
            f_recv(d, k, s - 1).wait_recv()

            @pl.when(s < chips - 1)
            def _():
                f_copy(d, k, s).start()

            q_copy(d, k, s).start()
        s_recv(s - 1).wait_recv()

        @pl.when(s < chips - 1)
        def _():
            s_copy(s).start()
        return c

    lax.fori_loop(1, chips, gather_step, 0)

    def finish(s, c):
        for d, k in both:
            q_recv(d, k, s).wait_recv()
        return c

    lax.fori_loop(0, chips, finish, 0)
    total = sring[0]
    for s in range(1, chips):
        total = total + sring[s]
    sout[...] = total

    def drain(s, c):
        for d, k in both:
            q_copy(d, k, s).wait_send()

            @pl.when(s < chips - 1)
            def _():
                a_copy(d, k, s).wait_send()
                f_copy(d, k, s).wait_send()

        @pl.when(s < chips - 1)
        def _():
            s_copy(s).wait_send()
        p_copy(s).wait_send()
        return c

    lax.fori_loop(0, chips, drain, 0)
    for d, k in both:
        x_copy(d, k).wait_send()
    for c in (back, small_p, small_x, ffn_x):
        c.wait_send()


def sum_call(n_seq, g, small, own, gn_rem, base, g1, mine):
    rows, cols = g.shape
    n, width = own.shape
    chips = n_seq // 2
    cr, lanes, cw = rows // 2 // chips, 2 * SPLIT, cols // (2 * SPLIT)
    V, D = pltpu.VMEM, pltpu.SemaphoreType.DMA
    return pl.pallas_call(
        functools.partial(sum_body, n_seq),
        out_shape=(sds((rows, cols), BF16), sds(small.shape, F32), sds((n, width), F32),
                   sds(mine.shape[1:], F32), sds(mine.shape[1:], F32)),
        in_specs=[VM] * 7, out_specs=(VM,) * 5,
        scratch_shapes=[
            V(mine.shape, BF16),
            V((chips, cr, cols), BF16), V((chips - 1, lanes, cr, cw), BF16), V((chips - 1, lanes, cr, cw), BF16),
            V((lanes, cr, cw), BF16), V((lanes, cr, cw), BF16),
            V((3,) + small.shape, F32), V((chips,) + small.shape, F32), V((n, width), BF16),
            D((chips,)), D((chips,)), D((chips - 1, lanes)), D((chips - 1, lanes)), D((lanes,)), D((lanes,)),
            D((chips - 1, lanes)), D((chips - 1, lanes)), D((chips, lanes)), D((chips, lanes)),
            D((chips - 1,)), D((chips - 1,)), D((4,)), D((4,))],
        compiler_params=pltpu.CompilerParams(
            vmem_limit_bytes=LIMIT, collective_id=2, has_side_effects=True),
        name="sums",
    )(g, small, own, gn_rem, base, g1, mine)


def finish_body(g, small, qkv, proj, fg, fb, qgg, kgg, sgg, sbg):
    width = proj.shape[1]
    qkv[...] = g[:, 0:3 * width].astype(F32)
    proj[...] = g[:, 3 * width:].astype(F32)

    @pl.when(pl.program_id(0) == 0)
    def _():
        for i, ref in enumerate((fg, fb, sgg, sbg)):
            ref[...] = small[i:i + 1, :].reshape(width)
        for i, ref in ((4, qgg), (5, kgg)):
            folded = small[i:i + 1, 0:128]
            for j in range(1, width // 128):
                folded = folded + small[i:i + 1, j * 128:(j + 1) * 128]
            folded = folded + pltpu.roll(folded, 64, 1)
            ref[...] = folded[:, 0:64].reshape(64)


def finish_call(g, small):
    rows, cols = g.shape
    width = cols // 4
    step = 128
    whole = lambda size: pl.BlockSpec((size,), lambda i: (0,))
    return pl.pallas_call(
        finish_body, grid=(rows // step,),
        out_shape=(sds((rows, 3 * width), F32), sds((rows, width), F32), sds((width,), F32), sds((width,), F32),
                   sds((64,), F32), sds((64,), F32), sds((width,), F32), sds((width,), F32)),
        in_specs=[pl.BlockSpec((step, cols), lambda i: (i, 0)), pl.BlockSpec(small.shape, lambda i: (0, 0))],
        out_specs=(pl.BlockSpec((step, 3 * width), lambda i: (i, 0)), pl.BlockSpec((step, width), lambda i: (i, 0)),
                   whole(width), whole(width), whole(64), whole(64), whole(width), whole(width)),
        name="finish",
    )(g, small)


def layer_body(n_seq, own, gy, seg, g1, b1, wqkv, qg, kg, wout, g2, b2, wup, wdown,
               out, base, gn_rem, gall, small, mine,
               rem, fq, fk, ones, swap, vecs, normed, kk, vv, qq, rq, rk, qaug, att, mid,
               sx, sg, wbuf, accin, accout, first, hid, gpre, blk, gs, prec,
               dk, stage,
               wsend, wrecv, asend, arecv, psend, precv, tsend, trecv, gsem):
    n, width = own.shape
    f = wup.shape[0]
    h = f // 2
    chips = n_seq // 2
    pairs = width // 128
    tiles = n // TILE
    core, place, right, left, partner = ring_places(n_seq)
    x = lax.axis_index("pos")
    right, left, partner, across = {"seq": right}, {"seq": left}, {"seq": partner}, {"pos": 1 - x}
    greet((right, left, partner, across))

    def slot(s, k, d):
        return pl.ds(pl.multiple_of((k * chips + s) * f + d * h, h), h)

    def w_copies(s, k):
        return [copy_to(wbuf.at[slot(s, k, d)] if s else (wdown if k else wup).at[pl.ds(d * h, h)],
                        wbuf.at[slot(s + 1, k, d)], wsend.at[d, k, s], wrecv.at[d, k, s],
                        left if d else right) for d in range(2)]

    def a_copies(s, k):
        rows = [pl.ds(d * h, h) for d in range(2)]
        return [copy_to(accout.at[s - 1, k, rows[d]], accin.at[s - 1, k, rows[d]], asend.at[d, k, s - 1],
                        arecv.at[d, k, s - 1], left if d else right) for d in range(2)]

    def w_step(i):
        s, k = i // 2 + 1, i % 2
        for c in w_copies(s - 1, k):
            c.wait_recv()
        if s < chips - 1:
            for c in w_copies(s, k):
                c.start()

    def r_step(j):
        s, k = j // 2 + 1, j % 2
        for c in a_copies(s, k):
            c.wait_recv()
        if s < chips - 1:
            accout[s, k] = (accout[s, k].astype(F32) + accin[s - 1, k].astype(F32)).astype(BF16)
            for c in a_copies(s + 1, k):
                c.start()

    def at_points(now, points, step):
        for when, item in points:
            @pl.when(now == when)
            def _():
                step(item)

    def t_copy(i):
        rows = pl.ds(i * TILE, TILE)
        return copy_to(own.at[rows], rem.at[rows], tsend.at[i], trecv.at[i], across)

    def s_copy(i):
        return copy_to(sx.at[pl.ds(i * TILE, TILE)], sx.at[pl.ds(n + i * TILE, TILE)], psend.at[3 + i],
                       precv.at[3 + i], partner)

    gy_copy = copy_to(gy, sg.at[pl.ds(n, n)], psend.at[0], precv.at[0], partner)
    parts = (copy_to(gs.at[pl.ds(n, n)], prec.at[1], psend.at[1], precv.at[1], partner),
             copy_to(blk.at[pl.ds(n, n)], prec.at[0], psend.at[2], precv.at[2], partner))

    for k in range(2):
        for c in w_copies(0, k):
            c.start()
    for i in range(tiles):
        t_copy(i).start()
    gy_copy.start()

    at = pl.multiple_of(x * n, n)
    labels = jnp.concatenate([seg[:, pl.ds(at, n)], seg[:, pl.ds(n - at, n)]], axis=1)
    lane = lax.broadcasted_iota(jnp.int32, (128, 2 * n), 0) % 64
    same = lane == labels
    keyed = jnp.where((lane >= 6) & (lane <= 8), 1.0, jnp.where(same & (lane < 6), 1.0, 0.0))
    fk[...] = keyed.T.astype(BF16)
    away = jnp.where((lane < 6) & jnp.logical_not(same), -BIG, 0.0)
    fq[...] = away[:, 0:n].T.astype(BF16)
    ra = lax.broadcasted_iota(jnp.int32, ones.shape, 0) // 64
    rb = lax.broadcasted_iota(jnp.int32, ones.shape, 1) // 64
    ones[...] = jnp.where(ra == rb, 1.0, 0.0).astype(BF16)
    swap[...] = jnp.where(ra[:128, :128] == rb[:128, :128], 0.0, 1.0).astype(BF16)
    for i, v in enumerate((g1, b1, g2, b2)):
        vecs[i:i + 1, :] = v[...].reshape(1, width)
    for i, v in enumerate((qg, kg)):
        r = v[...].reshape(1, 64)
        vecs[4 + i:5 + i, :] = jnp.concatenate([r] * (width // 64), axis=1)
    sg[0:n, :] = gy[...]
    wbuf[0:f, :] = wup[...]
    wbuf[chips * f:(chips + 1) * f, :] = wdown[...]
    cols = ones.shape[0]

    def project(xs, i, queries):
        rows = tile_of(i)
        low = (rows_norm(xs)[0] * vecs[0:1, :] + vecs[1:2, :]).astype(BF16)
        normed[rows, :] = low
        for block in range(0 if queries else width // cols, 3 * width // cols):
            raw = dot(low, wqkv[:, block * cols:(block + 1) * cols])
            part, a = divmod(block * cols, width)
            lanes = slice(a, a + cols)
            if part == 2:
                vv[rows, lanes] = raw.astype(BF16)
                continue
            centred = raw - group_sum(raw, ones[...]) * (1 / 64)
            scale = lax.rsqrt(group_sum(centred * centred, ones[...]) * (1 / 64) + EPS)
            dst, rdst = (qq, rq) if part == 0 else (kk, rk)
            dst[rows, lanes] = (centred * scale * vecs[4 + part:5 + part, lanes]).astype(BF16)
            rdst[rows, lanes] = scale

    def own_tile(i, c):
        project(own[tile_of(i), :].astype(F32), i, True)
        return c

    lax.fori_loop(0, tiles, own_tile, 0)
    w_step(0)
    lane_t = lax.broadcasted_iota(jnp.int32, (TILE, 128), 1)
    low_t = lane_t < 64
    lane_n = lax.broadcasted_iota(jnp.int32, (n, 128), 1)
    low_n = lane_n < 64

    def attend(krows, size, add, after):
        low_k = lax.broadcasted_iota(jnp.int32, (size, 128), 1) < 64

        def pair(p, c):
            lanes = tile_of(p, 128)
            k, v, feat = kk[krows, lanes], vv[krows, lanes], fk[krows, :]
            one = jnp.ones_like(v)
            ks = (jnp.where(low_k, k, feat), jnp.where(low_k, feat, k))
            vs = (jnp.where(low_k, v, one), jnp.where(low_k, one, v))

            q, mask = qq[:, lanes], fq[...]
            for a in range(2):
                qa = jnp.where(low_n, q, mask) if a == 0 else jnp.where(low_n, mask, q)
                e = jnp.exp2(dot(qa, ks[a], NT) * (LOG2E / 8)).astype(BF16)
                o = dot(e, vs[a])
                to = slice(a * n, (a + 1) * n)
                blk[to, lanes] = blk[to, lanes] + o if add else o
            if after is not None:
                after(p)
            return c

        lax.fori_loop(0, pairs, pair, 0)

    attend(slice(0, n), n, False, lambda p: at_points(p, ((1, 1), (4, 2)), w_step))
    for i in range(tiles):
        t_copy(i).wait_recv()
        project(rem[i * TILE:(i + 1) * TILE, :].astype(F32), tiles + i, False)
        if i == 0:
            w_step(3)
        attend(slice(n + i * TILE, n + (i + 1) * TILE), TILE, True,
               lambda p: at_points(p, ((1, 5),) if i else ((5, 4),), w_step))

    def close(p, c):
        lanes = tile_of(p, 128)

        def tile(t, c):
            rows = tile_of(t)
            q, mask = qq[rows, lanes], fq[rows, :]
            res = [blk[pl.ds(pl.multiple_of(a * n + t * TILE, TILE), TILE), lanes] for a in range(2)]
            for a in range(2):
                qa = jnp.where(low_t, q, mask) if a == 0 else jnp.where(low_t, mask, q)
                shift = jnp.log(res[a]) * -8.0
                hi, lo = two(shift)
                lo2 = (shift - hi.astype(F32) - lo.astype(F32)).astype(BF16)
                s = 64 * (1 - a)
                qaug[p * 2 + a, rows, :] = jnp.where(
                    lane_t == s + 6, hi, jnp.where(lane_t == s + 7, lo, jnp.where(lane_t == s + 8, lo2, qa)))
            num = jnp.where(low_t, res[0], res[1])
            den = pltpu.roll(jnp.where(low_t, res[1], res[0]), 64, 1)
            att[rows, lanes] = (num / den).astype(BF16)
            return c

        lax.fori_loop(0, tiles, tile, 0)
        return c

    lax.fori_loop(0, pairs, close, 0)
    w_step(6)
    for i in range(tiles):
        rows = slice(i * TILE, (i + 1) * TILE)
        m = own[rows, :].astype(F32) + dot(att[rows, :], wout[...])
        mid[rows, :] = m
        sx[rows, :] = (rows_norm(m)[0] * vecs[2:3, :] + vecs[3:4, :]).astype(BF16)
        s_copy(i).start()
    quad = chips // 2
    gy_copy.wait_recv()
    for j in range(tiles):
        s_copy(j).wait_recv()

    def feed(begin, span, lanes, turn, after):
        up = wbuf.at[begin:begin + span]
        down = wbuf.at[chips * f + begin:chips * f + begin + span]

        def tile(i, c):
            rows = tile_of((i + turn) % (2 * tiles))
            acts, slopes = [], []
            for j in range(span // TILE):
                cs = slice(j * TILE, (j + 1) * TILE)
                to = slice(lanes + j * TILE, lanes + (j + 1) * TILE)
                pre = dot(sx[rows, :], up[cs, :], NT)
                gh = dot(sg[rows, :], down[cs, :], NT)
                cdf = 0.5 + 0.5 * lax.erf(pre * 0.7071067811865476)
                slope = cdf + pre * (jnp.exp(-0.5 * pre * pre) * 0.3989422804014327)
                acts.append((pre * cdf).astype(BF16))
                slopes.append((gh * slope).astype(BF16))
                hid[rows, to] = acts[-1]
                gpre[rows, to] = slopes[-1]
            o = dot(jnp.concatenate(acts, 1), down[...])
            t = dot(jnp.concatenate(slopes, 1), up[...])
            blk[rows, :] = blk[rows, :] + o if begin else o
            gs[rows, :] = gs[rows, :] + t if begin else t
            after(i)
            return c

        lax.fori_loop(0, 2 * tiles, tile, 0)

    def outer(g):
        def block(j, c):
            for k, (lhs, rhs) in enumerate(((gpre, sx), (hid, sg))):
                part = dot(lhs[:, pl.ds(pl.multiple_of(j * 2 * f, 2 * f), 2 * f)], rhs[...], TN)
                for m in range(2):
                    one = part[m * f:(m + 1) * f]
                    at = g * quad + 2 * j + m

                    @pl.when(at == 0)
                    def _():
                        first[k] = one

                    @pl.when(at > 0)
                    def _():
                        accout[jnp.maximum(at - 1, 0), k] = one.astype(BF16)
            return c

        lax.fori_loop(0, quad // 2, block, 0)

    half_way = quad * f
    last = 2 * quad * f - TILE
    feed(0, half_way, 0, 0, lambda i: at_points(i, ((0, 7), (1, 8), (3, 9)), w_step))
    outer(0)
    w_step(10)
    w_step(11)
    for k in range(2):
        for c in a_copies(1, k):
            c.start()
    feed(half_way, last - half_way, 0, tiles, lambda i: None)
    w_step(12)
    w_step(13)

    def send_parts(i):
        @pl.when(i == tiles - 1)
        def _():
            for c in parts:
                c.start()

    feed(last, TILE, last - half_way, tiles, send_parts)
    r_step(0)
    outer(1)

    for j in range(chips - 1):
        for k in range(2):
            for c in w_copies(j, k):
                c.wait_send()
    for i in range(tiles):
        s_copy(i).wait_send()
    gbr, gat = sx.at[0:n], sx.at[n:2 * n]
    small[...] = jnp.zeros_like(small)
    parts[0].wait_recv()

    def mid_tile(i, c):
        rows = tile_of(i)
        xh, r = rows_norm(mid[rows, :])
        dy = gs[rows, :] + prec[1, rows, :]
        small[2:3, :] += jnp.sum(dy * xh, axis=0, keepdims=True)
        small[3:4, :] += jnp.sum(dy, axis=0, keepdims=True)
        gd = dy * vecs[2:3, :]
        dx = r * (gd - jnp.mean(gd, -1, keepdims=True) - xh * jnp.mean(gd * xh, -1, keepdims=True))
        gm = gy[rows, :].astype(F32) + dx
        base[rows, :] = gm
        low = gm.astype(BF16)
        gbr[rows, :] = low
        gat[rows, :] = dot(low, wout[...], NT).astype(BF16)
        return c

    lax.fori_loop(0, tiles, mid_tile, 0)
    r_step(1)
    parts[1].wait_recv()
    out[...] = (mid[...] + (blk[0:n, :] + prec[0])).astype(BF16)

    def flush(j, rows, lanes):
        return pltpu.make_async_copy(stage.at[j], gall.at[rows, lanes], gsem.at[j])

    def proj_tile(i, c):
        rows = tile_of(i)
        stage[i] = dot(att[:, rows], gbr[...], TN).astype(BF16)
        flush(i, rows, pl.ds(3 * width, width)).start()
        return c

    lax.fori_loop(0, width // TILE, proj_tile, 0)

    def keys_of(j, rows):
        return wbuf.at[pl.ds(pl.multiple_of(j * 2 * n + rows, TILE), TILE)]

    def mix(part, rows):
        return pl.ds(part * 2 * n + rows.start, rows.size)

    ones_p = slice(0, 128)

    def norm_back(dy, y, r, gain):
        group = ones[ones_p, ones_p]
        dy = dy * 0.125
        y = y.astype(F32)
        prod = dy * y
        gd = dy * gain
        m1 = group_sum(gd, group) * (1 / 64)
        m2 = group_sum(prod, group) * (1 / 64)
        inv = 1.0 / gain
        return r * (gd - m1 - y * inv * m2), jnp.sum(prod, 0, keepdims=True) * inv

    def pair(p, c):
        at_points(p, ((1, 3), (2, 4), (4, 7), (5, 8)), r_step)
        lanes = tile_of(p, 128)
        do = gat[:, lanes]
        delta = -group_sum(do.astype(F32) * att[:, lanes].astype(F32), swap[...])
        hi, lo = two(delta)
        zero = jnp.zeros_like(do)
        das = []
        for a in range(2):
            s = 64 * (1 - a)
            extra = jnp.where(lane_n == s, hi, jnp.where(lane_n == s + 1, lo, zero))
            das.append(jnp.where(low_n, do, extra) if a == 0 else jnp.where(low_n, extra, do))

        acc = [None, None]
        for t in range(2):
            if t:
                at_points(p, ((0, 2), (2, 5), (3, 6)), r_step)
            rows = slice(t * n, (t + 1) * n)
            k, v, feat = kk[rows, lanes], vv[rows, lanes], fk[rows, :]
            one = jnp.ones_like(v)
            dks, dvs = [], []
            for a in range(2):
                ka = jnp.where(low_n, k, feat) if a == 0 else jnp.where(low_n, feat, k)
                va = jnp.where(low_n, v, one) if a == 0 else jnp.where(low_n, one, v)
                qa = qaug[p * 2 + a]
                e = jnp.exp2(dot(ka, qa, NT) * (LOG2E / 8))
                ds = (e * dot(va, das[a], NT)).astype(BF16)
                dvs.append(dot(e.astype(BF16), das[a]))
                dks.append(dot(ds, qa))
                dq = dot(ka, ds, TN)
                acc[a] = dq if t == 0 else acc[a] + dq
            dk[rows, :] = jnp.where(low_n, dks[0], dks[1])
            wbuf[4 * n + t * n:4 * n + (t + 1) * n, lanes] = jnp.where(low_n, dvs[0], dvs[1]).astype(BF16)
        low_s = lax.broadcasted_iota(jnp.int32, (128, n), 0) < 64
        dq = jnp.where(low_s, acc[0], acc[1]).T
        qa = jnp.where(low_n, qaug[p * 2], qaug[p * 2 + 1])
        dx, gg = norm_back(dq, qa, rq[:, lanes], vecs[4:5, lanes])
        wbuf[0:n, lanes] = dx.astype(BF16)
        small[4:5, lanes] = gg
        dx, gg = norm_back(dk[...], kk[:, lanes], rk[:, lanes], vecs[5:6, lanes])
        wbuf[2 * n:4 * n, lanes] = dx.astype(BF16)
        small[5:6, lanes] = gg
        return c

    lax.fori_loop(0, pairs, pair, 0)
    for i in range(width // TILE):
        flush(i, pl.ds(i * TILE, TILE), pl.ds(3 * width, width)).wait()
    r_step(9)

    def gain_sums(xh, gn):
        small[0:1, :] += jnp.sum(gn * xh, axis=0, keepdims=True)
        small[1:2, :] += jnp.sum(gn, axis=0, keepdims=True)

    def rem_tile(i, c):
        rows = tile_of(i)
        gn = (dot(wbuf[pl.ds(pl.multiple_of(3 * n + i * TILE, TILE), TILE), :], wqkv[:, width:2 * width], NT)
              + dot(wbuf[pl.ds(pl.multiple_of(5 * n + i * TILE, TILE), TILE), :], wqkv[:, 2 * width:], NT))
        gn_rem[rows, :] = gn.astype(BF16)
        gain_sums(rows_norm(rem[rows, :].astype(F32))[0], gn)
        return c

    def own_back(i, c):
        rows = tile_of(i)
        gn = (dot(wbuf[rows, :], wqkv[:, 0:width], NT)
              + dot(wbuf[pl.ds(pl.multiple_of(2 * n + i * TILE, TILE), TILE), :], wqkv[:, width:2 * width], NT)
              + dot(wbuf[pl.ds(pl.multiple_of(4 * n + i * TILE, TILE), TILE), :], wqkv[:, 2 * width:], NT))
        xh, r = rows_norm(own[rows, :].astype(F32))
        gain_sums(xh, gn)
        gd = gn * vecs[0:1, :]
        base[rows, :] += r * (gd - jnp.mean(gd, -1, keepdims=True) - xh * jnp.mean(gd * xh, -1, keepdims=True))
        return c

    def qkv_tile(i, c):
        rows = tile_of(i)
        jobs = ((0, n, 0), (2 * n, 2 * n, 1), (4 * n, 2 * n, 2))
        for j, (at, size, part) in enumerate(jobs):
            stage[j] = dot(normed[0:size, rows], wbuf[at:at + size, :], TN).astype(BF16)
            flush(j, rows, pl.ds(part * width, width)).start()
        for j, (at, size, part) in enumerate(jobs):
            flush(j, rows, pl.ds(part * width, width)).wait()
        at_points(i, ((0, 10), (2, 11)), r_step)
        return c

    lax.fori_loop(0, width // TILE, qkv_tile, 0)
    lax.fori_loop(0, tiles, rem_tile, 0)
    r_step(12)
    lax.fori_loop(0, tiles, own_back, 0)
    r_step(13)
    mine[...] = (first[...] + accin[chips - 2].astype(F32)).astype(BF16)
    for j in range(1, chips):
        for k in range(2):
            for c in a_copies(j, k):
                c.wait_send()
    for i in range(tiles):
        t_copy(i).wait_send()
    for c in (gy_copy,) + parts:
        c.wait_send()


def layer_call(n_seq, own, gy, seg, g1, b1, wqkv, qg, kg, wout, g2, b2, wup, wdown):
    n, width = own.shape
    f = wup.shape[0]
    chips = n_seq // 2
    heads = width // 64
    tiles = n // TILE
    V, D = pltpu.VMEM, pltpu.SemaphoreType.DMA
    return pl.pallas_call(
        functools.partial(layer_body, n_seq),
        out_shape=(sds((n, width), BF16), sds((n, width), F32), sds((n, width), BF16),
                   sds((width, 4 * width), BF16), sds((8, width), F32), sds((2, f, width), BF16)),
        in_specs=[VM] * 13,
        out_specs=(VM, VM, VM, pl.BlockSpec(memory_space=pl.ANY), VM, VM),
        scratch_shapes=[
            V((n, width), BF16), V((n, 128), BF16), V((2 * n, 128), BF16), V((256, 256), BF16), V((128, 128), BF16),
            V((8, width), F32), V((2 * n, width), BF16), V((2 * n, width), BF16), V((2 * n, width), BF16),
            V((n, width), BF16), V((n, width), F32), V((2 * n, width), F32), V((heads, n, 128), BF16),
            V((n, width), BF16), V((n, width), F32),
            V((2 * n, width), BF16), V((2 * n, width), BF16), V((chips * 2 * f, width), BF16),
            V((chips - 1, 2, f, width), BF16), V((chips - 1, 2, f, width), BF16), V((2, f, width), F32),
            V((2 * n, chips // 2 * f), BF16), V((2 * n, chips // 2 * f), BF16), V((2 * n, width), F32), V((2 * n, width), F32),
            V((2, n, width), F32),
            V((2 * n, 128), F32), V((3, TILE, width), BF16),
            D((2, 2, chips - 1)), D((2, 2, chips - 1)), D((2, 2, chips - 1)), D((2, 2, chips - 1)),
            D((3 + tiles,)), D((3 + tiles,)), D((tiles,)), D((tiles,)), D((3,))],
        compiler_params=pltpu.CompilerParams(
            vmem_limit_bytes=66 * 1000 * 1000, collective_id=1, has_side_effects=True),
        name="layer",
    )(own, gy, seg, g1, b1, wqkv, qg, kg, wout, g2, b2, wup, wdown)


def local_one(tokens, segment_ids, first_gain, first_bias, w_qkv, query_gain, key_gain, w_out,
              second_gain, second_bias, w_up, w_down, out_grad):
    n_seq = lax.axis_size("seq")
    own = tokens[0]
    block_out, base, gn_rem, g, small, mine = layer_call(
        n_seq, own, out_grad[0], segment_ids, first_gain, first_bias, w_qkv, query_gain, key_gain, w_out,
        second_gain, second_bias, w_up.T, w_down.T)
    g, small, input_grad, up_grad, down_grad = sum_call(n_seq, g, small, own, gn_rem, base, first_gain, mine)
    qkv, proj, fg, fb, qgg, kgg, sgg, sbg = finish_call(g, small)
    return (block_out[None], input_grad[None], fg, fb, qkv, qgg, kgg, proj, sgg, sbg, up_grad.T, down_grad.T)


def layer_norm(rows, gain, shift):
    average = jnp.mean(rows, axis=-1, keepdims=True)
    centred = rows - average
    spread = jnp.mean(centred * centred, axis=-1, keepdims=True)
    return centred * lax.rsqrt(spread + EPS) * gain + shift


def head_norm(values, gain):
    average = jnp.mean(values, axis=-1, keepdims=True)
    centred = values - average
    spread = jnp.mean(centred * centred, axis=-1, keepdims=True)
    return centred * lax.rsqrt(spread + EPS) * gain


def qk_norms(raw_query, raw_keys, query_gain, key_gain):
    return (head_norm(raw_query, query_gain), head_norm(raw_keys, key_gain))


def gelu_exact(values):
    return jax.nn.gelu(values, approximate=False)


def gelu_back(pre, upstream):
    return jax.vjp(gelu_exact, pre)[1](upstream)[0]


def group_size(count, length):
    for option in range(1, count + 1):
        if count % option == 0 and option * length >= 512:
            return option
    return count


def rows_product(left, right):
    return lax.dot_general(
        left, right, (((0,), (0,)), ((), ())), preferred_element_type=jnp.float32
    )


def cols_product(left, right):
    return lax.dot_general(
        left, right, (((1,), (1,)), ((), ())), preferred_element_type=jnp.float32
    )


def local(
    tokens,
    segment_ids,
    first_gain,
    first_bias,
    w_qkv,
    query_gain,
    key_gain,
    w_out,
    second_gain,
    second_bias,
    w_up,
    w_down,
    out_grad,
):
    seqs_here, local_len, width = tokens.shape
    full_len = segment_ids.shape[1]
    head_dim = query_gain.shape[0]
    heads = width // head_dim
    rows_here = seqs_here * local_len
    scale = head_dim ** (-0.5)
    offset = lax.axis_index("pos") * local_len
    query_marks = lax.dynamic_slice_in_dim(segment_ids, offset, local_len, 1)
    block = group_size(seqs_here, local_len)
    count_blocks = seqs_here // block

    def split(array):
        return array.reshape((count_blocks, block) + array.shape[1:])

    inputs = tokens.astype(jnp.float32).reshape(rows_here, width)
    normed_low = layer_norm(inputs, first_gain, first_bias).astype(jnp.bfloat16)
    mixed = jnp.dot(normed_low, w_qkv, preferred_element_type=jnp.float32).reshape(
        rows_here, 3, heads, head_dim
    )
    raw_query = mixed[:, 0]
    raw_keys = mixed[:, 1]
    query = (
        head_norm(raw_query, query_gain)
        .astype(jnp.bfloat16)
        .reshape(seqs_here, local_len, heads, head_dim)
    )
    keys_local = (
        head_norm(raw_keys, key_gain).astype(jnp.bfloat16).reshape(seqs_here, local_len, width)
    )
    values_local = mixed[:, 2].astype(jnp.bfloat16).reshape(seqs_here, local_len, width)
    keys_all, values_all = (
        lax.all_gather(keys_local, "pos", axis=1, tiled=True),
        lax.all_gather(values_local, "pos", axis=1, tiled=True),
    )
    keys_four = keys_all.reshape(seqs_here, full_len, heads, head_dim)
    values_four = values_all.reshape(seqs_here, full_len, heads, head_dim)

    def scores_for(query_blk, keys_blk, query_lab, key_lab):
        raw = (
            jnp.einsum("bqhd,bkhd->bhqk", query_blk, keys_blk, preferred_element_type=jnp.float32)
            * scale
        )
        allowed = (query_lab[:, :, None] == key_lab[:, None, :])[:, None]
        return jnp.where(allowed, raw, -1e30)

    def forward_block(packed):
        query_blk, keys_blk, values_blk, query_lab, key_lab = packed
        scores = scores_for(query_blk, keys_blk, query_lab, key_lab)
        peak = jnp.max(scores, axis=-1, keepdims=True)
        expd = jnp.exp(scores - peak)
        totals = jnp.sum(expd, axis=-1, keepdims=True)
        probs = (expd / totals).astype(jnp.bfloat16)
        result = jnp.einsum(
            "bhqk,bkhd->bqhd", probs, values_blk, preferred_element_type=jnp.float32
        )
        return (result, peak + jnp.log(totals))

    attended, log_totals = lax.map(
        forward_block,
        (
            split(query),
            split(keys_four),
            split(values_four),
            split(query_marks),
            split(segment_ids),
        ),
    )
    attended_low = attended.astype(jnp.bfloat16).reshape(rows_here, width)
    middle = inputs + jnp.dot(attended_low, w_out, preferred_element_type=jnp.float32)
    second_low = layer_norm(middle, second_gain, second_bias).astype(jnp.bfloat16)
    grad_out = out_grad.reshape(rows_here, width)
    grad_float = grad_out.astype(jnp.float32)
    up_all, down_all = (
        lax.all_gather(w_up, "seq", axis=1, tiled=True),
        lax.all_gather(w_down, "seq", axis=1, tiled=True),
    )
    pre = jnp.dot(second_low, up_all, preferred_element_type=jnp.float32)
    hidden = gelu_exact(pre).astype(jnp.bfloat16)
    block_out = (middle + cols_product(hidden, down_all)).astype(jnp.bfloat16)
    grad_hidden = jnp.dot(grad_out, down_all, preferred_element_type=jnp.float32)
    grad_pre = gelu_back(pre, grad_hidden).astype(jnp.bfloat16)
    down_full = rows_product(grad_out, hidden)
    up_full = rows_product(second_low, grad_pre)
    grad_second = cols_product(grad_pre, up_all)
    up_part, down_part = (
        lax.psum_scatter(
            up_full.astype(jnp.bfloat16), "seq", scatter_dimension=1, tiled=True
        ).astype(jnp.float32),
        lax.psum_scatter(
            down_full.astype(jnp.bfloat16), "seq", scatter_dimension=1, tiled=True
        ).astype(jnp.float32),
    )
    up_grad, down_grad = (
        lax.psum(up_part.astype(jnp.bfloat16), "pos").astype(jnp.float32),
        lax.psum(down_part.astype(jnp.bfloat16), "pos").astype(jnp.float32),
    )
    second_back = jax.vjp(layer_norm, middle, second_gain, second_bias)[1]
    grad_middle_part, second_gain_part, second_bias_part = second_back(grad_second)
    grad_middle = grad_float + grad_middle_part
    grad_branch = grad_middle.astype(jnp.bfloat16)
    proj_part = rows_product(attended_low, grad_branch)
    grad_attended = (
        cols_product(grad_branch, w_out)
        .astype(jnp.bfloat16)
        .reshape(seqs_here, local_len, heads, head_dim)
    )

    def backward_block(packed):
        query_blk, keys_blk, values_blk, query_lab, key_lab, log_blk, grad_blk = packed
        scores = scores_for(query_blk, keys_blk, query_lab, key_lab)
        probs = jnp.exp(scores - log_blk)
        grad_probs = jnp.einsum(
            "bqhd,bkhd->bhqk", grad_blk, values_blk, preferred_element_type=jnp.float32
        )
        grad_values = jnp.einsum(
            "bhqk,bqhd->bkhd",
            probs.astype(jnp.bfloat16),
            grad_blk,
            preferred_element_type=jnp.float32,
        )
        inner = jnp.sum(probs * grad_probs, axis=-1, keepdims=True)
        grad_scores = (probs * (grad_probs - inner) * scale).astype(jnp.bfloat16)
        grad_query = jnp.einsum(
            "bhqk,bkhd->bqhd", grad_scores, keys_blk, preferred_element_type=jnp.float32
        )
        grad_keys = jnp.einsum(
            "bhqk,bqhd->bkhd", grad_scores, query_blk, preferred_element_type=jnp.float32
        )
        return (grad_query, grad_keys, grad_values)

    grad_query, grad_keys, grad_values = lax.map(
        backward_block,
        (
            split(query),
            split(keys_four),
            split(values_four),
            split(query_marks),
            split(segment_ids),
            log_totals,
            split(grad_attended),
        ),
    )
    grad_keys = grad_keys.reshape(seqs_here, full_len, width)
    grad_values = grad_values.reshape(seqs_here, full_len, width)
    keys_grad, values_grad = (
        lax.psum_scatter(
            grad_keys.astype(jnp.bfloat16), "pos", scatter_dimension=1, tiled=True
        ).astype(jnp.float32),
        lax.psum_scatter(
            grad_values.astype(jnp.bfloat16), "pos", scatter_dimension=1, tiled=True
        ).astype(jnp.float32),
    )
    norm_back = jax.vjp(qk_norms, raw_query, raw_keys, query_gain, key_gain)[1]
    grad_raw_query, grad_raw_keys, query_gain_part, key_gain_part = norm_back(
        (
            grad_query.reshape(rows_here, heads, head_dim),
            keys_grad.reshape(rows_here, heads, head_dim),
        )
    )
    grad_mixed = (
        jnp.stack(
            [grad_raw_query, grad_raw_keys, values_grad.reshape(rows_here, heads, head_dim)], axis=1
        )
        .reshape(rows_here, 3 * width)
        .astype(jnp.bfloat16)
    )
    qkv_part = rows_product(normed_low, grad_mixed)
    grad_normed = cols_product(grad_mixed, w_qkv)
    first_back = jax.vjp(layer_norm, inputs, first_gain, first_bias)[1]
    grad_input_part, first_gain_part, first_bias_part = first_back(grad_normed)
    input_grad = (grad_middle + grad_input_part).reshape(seqs_here, local_len, width)
    (
        qkv_grad,
        proj_grad,
        first_gain_grad,
        first_bias_grad,
        query_gain_grad,
        key_gain_grad,
        second_gain_grad,
        second_bias_grad,
    ) = lax.psum(
        (
            qkv_part,
            proj_part,
            first_gain_part,
            first_bias_part,
            query_gain_part,
            key_gain_part,
            second_gain_part,
            second_bias_part,
        ),
        ("pos", "seq"),
    )
    return (
        block_out.reshape(seqs_here, local_len, width),
        input_grad,
        first_gain_grad,
        first_bias_grad,
        qkv_grad,
        query_gain_grad,
        key_gain_grad,
        proj_grad,
        second_gain_grad,
        second_bias_grad,
        up_grad,
        down_grad,
    )


def solution(mesh):
    placed = (P("seq", "pos", None), P("seq", None), P(), P(), P(), P(), P(), P(), P(), P(),
              P(None, "seq"), P(None, "seq"), P("seq", "pos", None))
    outs = (P("seq", "pos", None), P("seq", "pos", None), P(), P(), P(), P(), P(), P(), P(), P(),
            P(None, "seq"), P(None, "seq"))

    def step(*args):
        def run(*local_args):
            one = local_args[0].shape[:2] == (1, 512) and (mesh.shape["pos"], mesh.shape["seq"]) == (2, 16)
            return (local_one if one else local)(*local_args)

        return jax.shard_map(run, mesh=mesh, in_specs=placed, out_specs=outs, check_vma=False)(*args)

    return step
```

```python
import functools
import jax
import jax.numpy as jnp
from jax import lax
from jax.experimental import pallas as pl
from jax.experimental.pallas import tpu as pltpu
from jax.sharding import PartitionSpec as P

EPS = 1e-06
F32 = jnp.float32
BF16 = jnp.bfloat16
LOG2E = 1.4426950408889634
BIG = 16384.0
TILE = 256
NT = (((1,), (1,)), ((), ()))
NN = (((1,), (0,)), ((), ()))
TN = (((0,), (0,)), ((), ()))


def dot(a, b, dims=NN):
    return lax.dot_general(a, b, dims, preferred_element_type=F32)


def two(x):
    hi = x.astype(BF16)
    return hi, (x - hi.astype(F32)).astype(BF16)


def group_sum(x, ones):
    hi, lo = two(x)
    return dot(hi, ones) + dot(lo, ones)


def rows_norm(x):
    average = jnp.mean(x, axis=-1, keepdims=True)
    centred = x - average
    spread = jnp.mean(centred * centred, axis=-1, keepdims=True)
    scale = lax.rsqrt(spread + EPS)
    return centred * scale, scale


def tile_of(i, size=TILE):
    return pl.ds(pl.multiple_of(i * size, size), size)


VM = pl.BlockSpec(memory_space=pltpu.VMEM)
LIMIT = 60 * 1024 * 1024


def sds(shape, dtype):
    return jax.ShapeDtypeStruct(shape, dtype)


def ring_places(n_seq):
    s = lax.axis_index("seq")
    core, chip = s % 2, s // 2
    chips = n_seq // 2
    half = chips // 2
    odd = chip % 2
    place = (1 - odd) * (chip // 2) + odd * (chips - 1 - chip // 2)

    def device(p):
        far = p // half
        return ((1 - far) * 2 * p + far * (2 * (chips - 1 - p) + 1)) * 2 + core

    right = device((place + 1) % chips)
    left = device((place + chips - 1) % chips)
    return core, place, right, left, s + 1 - 2 * core


def copy_to(src, dst, send, recv, target):
    return pltpu.make_async_remote_copy(
        src_ref=src, dst_ref=dst, send_sem=send, recv_sem=recv, device_id=target,
        device_id_type=pl.DeviceIdType.MESH)


def greet(targets):
    barrier = pltpu.get_barrier_semaphore()
    for t in targets:
        pl.semaphore_signal(barrier, inc=1, device_id=t, device_id_type=pl.DeviceIdType.MESH)
    pl.semaphore_wait(barrier, len(targets))


def sum_body(n_seq, quarter, small, gn_rem, mine, fin, sout, gback, other,
             accin, accout, srec, sring,
             asend, arecv, xsend, xrecv, fsend, frecv, qsend, qrecv, ssend, srecv, gsend, grecv):
    qrows, cols = quarter.shape
    chips = n_seq // 2
    cw, pr, hr = cols // chips, qrows // 4, qrows // 2
    core, place, right, left, partner = ring_places(n_seq)
    x = lax.axis_index("pos")
    right, left, partner, across = {"seq": right}, {"seq": left}, {"seq": partner}, {"pos": 1 - x}
    greet((right, left, partner, across))

    def chunk(p):
        return (p + 2 * chips) % chips

    def lanes_of(p):
        return pl.ds(pl.multiple_of(p * cw, cw), cw)

    def rows_of(c, o, d):
        side = 1 - x if o else x
        return pl.ds(pl.multiple_of(c * 2 * qrows + side * qrows + d * hr, hr), hr)

    def a_copy(i, s):
        return copy_to(accout.at[s, i], accin.at[s, i], asend.at[s, i], arecv.at[s, i], left if i // 2 else right)

    def x_piece(i, side, p):
        ref = fin.at[pl.ds(pl.multiple_of(core * 2 * qrows + side * qrows + i * pr, pr), pr), lanes_of(p)]
        return copy_to(ref, ref, xsend.at[i], xrecv.at[i], across)

    def ring_copy(d, o, s, p):
        ref = fin.at[rows_of(core, o, d), lanes_of(p)]
        return copy_to(ref, ref, fsend.at[s, d * 2 + o], frecv.at[s, d * 2 + o], left if d else right)

    def f_copy(d, o, s):
        return ring_copy(d, o, s, chunk(place + s) if d else chunk(place - s))

    def f_recv(d, o, s):
        return ring_copy(d, o, s, chunk(place + s + 1) if d else chunk(place - s - 1))

    def pair_copy(c, d, o, s):
        ref = fin.at[rows_of(c, o, d), lanes_of(chunk(place + s) if d else chunk(place - s))]
        return copy_to(ref, ref, qsend.at[s, d * 2 + o], qrecv.at[s, d * 2 + o], partner)

    def s_copy(s):
        return copy_to(sring.at[chunk(place - s)], sring.at[chunk(place - s)], ssend.at[s], srecv.at[s], right)

    def s_recv(s):
        p = chunk(place - s - 1)
        return copy_to(sring.at[p], sring.at[p], ssend.at[s], srecv.at[s], right)

    back = copy_to(gn_rem, gback, gsend.at[0], grecv.at[0], across)
    small_p = copy_to(small, srec.at[0], gsend.at[1], grecv.at[1], partner)
    small_x = copy_to(srec.at[1], srec.at[2], gsend.at[2], grecv.at[2], across)
    ffn_x = copy_to(mine, other, gsend.at[3], grecv.at[3], across)
    pieces = (0, 2, 1, 3)
    both = [(d, o) for o in range(2) for d in range(2)]

    small_p.start()

    def part(i, q):
        return quarter[i * pr:(i + 1) * pr, lanes_of(q)].astype(F32)

    def reduce_step(s, c):
        for i in pieces:
            q = chunk(place + s) if i // 2 else chunk(place - s)

            @pl.when(s == 1)
            def _():
                accout[s - 1, i] = part(i, q).astype(BF16)

            @pl.when(s > 1)
            def _():
                a_copy(i, s - 2).wait_recv()
                accout[s - 1, i] = (part(i, q) + accin[s - 2, i].astype(F32)).astype(BF16)

            a_copy(i, s - 1).start()

        @pl.when(s == 1)
        def _():
            back.start()
            small_p.wait_recv()
            srec[1] = small[...] + srec[0]
            small_x.start()
        return c

    lax.fori_loop(1, chips, reduce_step, 0)
    for i in pieces:
        a_copy(i, chips - 2).wait_recv()
        at = pl.ds(pl.multiple_of(core * 2 * qrows + x * qrows + i * pr, pr), pr)
        fin[at, lanes_of(place)] = (part(i, place) + accin[chips - 2, i].astype(F32)).astype(BF16)
        x_piece(i, x, place).start()
        if i % 2:
            f_copy(i // 2, 0, 0).start()
            pair_copy(core, i // 2, 0, 0).start()
    small_x.wait_recv()
    sring[place] = srec[1] + srec[2]
    s_copy(0).start()
    for i in pieces:
        x_piece(i, 1 - x, place).wait_recv()
        if i % 2:
            f_copy(i // 2, 1, 0).start()
            pair_copy(core, i // 2, 1, 0).start()
    ffn_x.start()

    def gather_step(s, c):
        for d, o in both:
            f_recv(d, o, s - 1).wait_recv()

            @pl.when(s < chips - 1)
            def _():
                f_copy(d, o, s).start()

            pair_copy(core, d, o, s).start()
        s_recv(s - 1).wait_recv()

        @pl.when(s < chips - 1)
        def _():
            s_copy(s).start()
        return c

    lax.fori_loop(1, chips, gather_step, 0)

    def finish(s, c):
        for d, o in both:
            pair_copy(1 - core, d, o, s).wait_recv()
        return c

    total = sring[0]
    for s in range(1, chips):
        total = total + sring[s]
    sout[...] = total
    lax.fori_loop(0, chips, finish, 0)
    back.wait_recv()
    ffn_x.wait_recv()

    def drain(s, c):
        for d, o in both:
            pair_copy(core, d, o, s).wait_send()

            @pl.when(s < chips - 1)
            def _():
                a_copy(d * 2 + o, s).wait_send()
                f_copy(d, o, s).wait_send()

        @pl.when(s < chips - 1)
        def _():
            s_copy(s).wait_send()
        return c

    lax.fori_loop(0, chips, drain, 0)
    for i in pieces:
        x_piece(i, x, place).wait_send()
    for c in (back, small_p, small_x, ffn_x):
        c.wait_send()


def sum_call(n_seq, quarter, small, gn_rem, mine):
    qrows, cols = quarter.shape
    chips = n_seq // 2
    pr, cw = qrows // 4, cols // chips
    V, D = pltpu.VMEM, pltpu.SemaphoreType.DMA
    return pl.pallas_call(
        functools.partial(sum_body, n_seq),
        out_shape=(sds((4 * qrows, cols), BF16), sds(small.shape, F32), sds(gn_rem.shape, BF16),
                   sds(mine.shape, BF16)),
        in_specs=[VM] * 4, out_specs=(VM,) * 4,
        scratch_shapes=[
            V((chips - 1, 4, pr, cw), BF16), V((chips - 1, 4, pr, cw), BF16),
            V((3,) + small.shape, F32), V((chips,) + small.shape, F32),
            D((chips - 1, 4)), D((chips - 1, 4)), D((4,)), D((4,)),
            D((chips - 1, 4)), D((chips - 1, 4)), D((chips, 4)), D((chips, 4)),
            D((chips - 1,)), D((chips - 1,)), D((4,)), D((4,))],
        compiler_params=pltpu.CompilerParams(
            vmem_limit_bytes=LIMIT, collective_id=2, has_side_effects=True),
        name="sums",
    )(quarter, small, gn_rem, mine)


def finish_body(g, small, own, gback, base, g1, mine, other, block, qkv, proj, fg, fb, qgg, kgg, sgg, sbg,
                igrad, upg, downg, out):
    width = proj.shape[1]
    proj[...] = g[:, 0:width].astype(F32)
    for j in range(3):
        for part in range(3):
            at = (j + 1) * width + part * TILE
            qkv[:, part * width + j * TILE:part * width + (j + 1) * TILE] = g[:, at:at + TILE].astype(F32)
    xh, r = rows_norm(own[...].astype(F32))
    dy = gback[...].astype(F32) * g1[...].reshape(1, width)
    dx = r * (dy - jnp.mean(dy, -1, keepdims=True) - xh * jnp.mean(dy * xh, -1, keepdims=True))
    igrad[...] = base[...] + dx
    out[...] = block[...]

    total = mine[...].astype(F32) + other[...].astype(F32)
    upg[...] = total[0]
    downg[...] = total[1]

    @pl.when(pl.program_id(0) == 0)
    def _():
        for i, ref in enumerate((fg, fb, sgg, sbg)):
            ref[...] = small[i:i + 1, :].reshape(width)
        for i, ref in ((4, qgg), (5, kgg)):
            folded = small[i:i + 1, 0:128]
            for j in range(1, width // 128):
                folded = folded + small[i:i + 1, j * 128:(j + 1) * 128]
            folded = folded + pltpu.roll(folded, 64, 1)
            ref[...] = folded[:, 0:64].reshape(64)


def finish_call(g, small, own, gback, base, g1, mine, other, block):
    rows, cols = g.shape
    n, width = own.shape
    f = mine.shape[1]
    steps = 2
    whole = lambda size: pl.BlockSpec((size,), lambda i: (0,))
    strip = lambda size, lanes: pl.BlockSpec((size // steps, lanes), lambda i: (i, 0))
    ffn_in = pl.BlockSpec((2, f // steps, width), lambda i: (0, i, 0))
    return pl.pallas_call(
        finish_body, grid=(steps,),
        out_shape=(sds((rows, 3 * width), F32), sds((rows, width), F32), sds((width,), F32), sds((width,), F32),
                   sds((64,), F32), sds((64,), F32), sds((width,), F32), sds((width,), F32),
                   sds((n, width), F32), sds((f, width), F32), sds((f, width), F32), sds((n, width), BF16)),
        in_specs=[strip(rows, cols), pl.BlockSpec(small.shape, lambda i: (0, 0)), strip(n, width), strip(n, width),
                  strip(n, width), whole(width), ffn_in, ffn_in, strip(n, width)],
        out_specs=(strip(rows, 3 * width), strip(rows, width),
                   whole(width), whole(width), whole(64), whole(64), whole(width), whole(width),
                   strip(n, width), strip(f, width), strip(f, width), strip(n, width)),
        name="finish",
    )(g, small, own, gback, base, g1, mine, other, block)


def layer_body(n_seq, own, gy, seg, g1, b1, wqkv, qg, kg, wout, g2, b2, wup, wdown,
               out, base, gn_rem, quarter, small, mine,
               rem, fq, fk, ones, swap, vecs, normed, kk, vv, qq, rq, rk, qaug, att, mid,
               sx, sg, wbuf, accin, accout, first, hid, gpre, blk, gs, prec,
               dk, pbuf, xin,
               wsend, wrecv, asend, arecv, psend, precv, tsend, trecv, gsend, grecv, xsend, xrecv):
    n, width = own.shape
    f = wup.shape[0]
    h = f // 2
    chips = n_seq // 2
    pairs = width // 128
    tiles = n // TILE
    core, place, right, left, partner = ring_places(n_seq)
    x = lax.axis_index("pos")
    right, left, partner, across = {"seq": right}, {"seq": left}, {"seq": partner}, {"pos": 1 - x}
    greet((right, left, partner, across))

    def slot(s, k, d):
        return pl.ds(pl.multiple_of((k * chips + s) * f + d * h, h), h)

    def w_copies(s, k):
        return [copy_to(wbuf.at[slot(s, k, d)] if s else (wdown if k else wup).at[pl.ds(d * h, h)],
                        wbuf.at[slot(s + 1, k, d)], wsend.at[d, k, s], wrecv.at[d, k, s],
                        left if d else right) for d in range(2)]

    def a_copies(s, k):
        rows = [pl.ds(d * h, h) for d in range(2)]
        return [copy_to(accout.at[s - 1, k, rows[d]], accin.at[s - 1, k, rows[d]], asend.at[d, k, s - 1],
                        arecv.at[d, k, s - 1], left if d else right) for d in range(2)]

    def w_step(i):
        s, k = i // 2 + 1, i % 2
        for c in w_copies(s - 1, k):
            c.wait_recv()
        if s < chips - 1:
            for c in w_copies(s, k):
                c.start()

    def r_step(j):
        s, k = j // 2 + 1, j % 2
        for c in a_copies(s, k):
            c.wait_recv()
        if s < chips - 1:
            accout[s, k] = (accout[s, k].astype(F32) + accin[s - 1, k].astype(F32)).astype(BF16)
            for c in a_copies(s + 1, k):
                c.start()

    def at_points(now, points, step):
        for when, item in points:
            @pl.when(now == when)
            def _():
                step(item)

    def t_copy(i):
        rows = pl.ds(i * TILE, TILE)
        return copy_to(own.at[rows], rem.at[rows], tsend.at[i], trecv.at[i], across)

    def s_copy(i):
        return copy_to(sx.at[pl.ds(i * TILE, TILE)], sx.at[pl.ds(n + i * TILE, TILE)], psend.at[3 + i],
                       precv.at[3 + i], partner)

    gy_copy = copy_to(gy, sg.at[pl.ds(n, n)], psend.at[0], precv.at[0], partner)
    parts = (copy_to(gs.at[pl.ds(n, n)], prec.at[1], psend.at[1], precv.at[1], partner),
             copy_to(blk.at[pl.ds(n, n)], prec.at[0], psend.at[2], precv.at[2], partner))

    for k in range(2):
        for c in w_copies(0, k):
            c.start()
    for i in range(tiles):
        t_copy(i).start()
    gy_copy.start()

    at = pl.multiple_of(x * n, n)
    labels = jnp.concatenate([seg[:, pl.ds(at, n)], seg[:, pl.ds(n - at, n)]], axis=1)
    lane = lax.broadcasted_iota(jnp.int32, (128, 2 * n), 0) % 64
    same = lane == labels
    keyed = jnp.where((lane >= 6) & (lane <= 8), 1.0, jnp.where(same & (lane < 6), 1.0, 0.0))
    fk[...] = keyed.T.astype(BF16)
    away = jnp.where((lane < 6) & jnp.logical_not(same), -BIG, 0.0)
    fq[...] = away[:, 0:n].T.astype(BF16)
    ra = lax.broadcasted_iota(jnp.int32, ones.shape, 0) // 64
    rb = lax.broadcasted_iota(jnp.int32, ones.shape, 1) // 64
    ones[...] = jnp.where(ra == rb, 1.0, 0.0).astype(BF16)
    swap[...] = jnp.where(ra[:128, :128] == rb[:128, :128], 0.0, 1.0).astype(BF16)
    for i, v in enumerate((g1, b1, g2, b2)):
        vecs[i:i + 1, :] = v[...].reshape(1, width)
    for i, v in enumerate((qg, kg)):
        r = v[...].reshape(1, 64)
        vecs[4 + i:5 + i, :] = jnp.concatenate([r] * (width // 64), axis=1)
    sg[0:n, :] = gy[...]
    wbuf[0:f, :] = wup[...]
    wbuf[chips * f:(chips + 1) * f, :] = wdown[...]
    cols = ones.shape[0]

    def project(xs, i, queries):
        rows = tile_of(i)
        low = (rows_norm(xs)[0] * vecs[0:1, :] + vecs[1:2, :]).astype(BF16)
        normed[rows, :] = low
        for block in range(0 if queries else width // cols, 3 * width // cols):
            raw = dot(low, wqkv[:, block * cols:(block + 1) * cols])
            part, a = divmod(block * cols, width)
            lanes = slice(a, a + cols)
            if part == 2:
                vv[rows, lanes] = raw.astype(BF16)
                continue
            centred = raw - group_sum(raw, ones[...]) * (1 / 64)
            scale = lax.rsqrt(group_sum(centred * centred, ones[...]) * (1 / 64) + EPS)
            dst, rdst = (qq, rq) if part == 0 else (kk, rk)
            dst[rows, lanes] = (centred * scale * vecs[4 + part:5 + part, lanes]).astype(BF16)
            rdst[rows, lanes] = scale

    def own_tile(i, c):
        project(own[tile_of(i), :].astype(F32), i, True)
        return c

    lax.fori_loop(0, tiles, own_tile, 0)
    w_step(0)
    lane_t = lax.broadcasted_iota(jnp.int32, (TILE, 128), 1)
    low_t = lane_t < 64
    lane_n = lax.broadcasted_iota(jnp.int32, (n, 128), 1)
    low_n = lane_n < 64

    def attend(krows, size, add, after):
        low_k = lax.broadcasted_iota(jnp.int32, (size, 128), 1) < 64

        def pair(p, c):
            lanes = tile_of(p, 128)
            k, v, feat = kk[krows, lanes], vv[krows, lanes], fk[krows, :]
            one = jnp.ones_like(v)
            ks = (jnp.where(low_k, k, feat), jnp.where(low_k, feat, k))
            vs = (jnp.where(low_k, v, one), jnp.where(low_k, one, v))

            q, mask = qq[:, lanes], fq[...]
            for a in range(2):
                qa = jnp.where(low_n, q, mask) if a == 0 else jnp.where(low_n, mask, q)
                e = jnp.exp2(dot(qa, ks[a], NT) * (LOG2E / 8)).astype(BF16)
                o = dot(e, vs[a])
                to = slice(a * n, (a + 1) * n)
                blk[to, lanes] = blk[to, lanes] + o if add else o
            if after is not None:
                after(p)
            return c

        lax.fori_loop(0, pairs, pair, 0)

    attend(slice(0, n), n, False, lambda p: at_points(p, ((1, 1), (4, 2)), w_step))
    for i in range(tiles):
        t_copy(i).wait_recv()
        project(rem[i * TILE:(i + 1) * TILE, :].astype(F32), tiles + i, False)
        if i == 0:
            w_step(3)
        attend(slice(n + i * TILE, n + (i + 1) * TILE), TILE, True,
               lambda p: at_points(p, ((1, 5),) if i else ((5, 4),), w_step))

    def close(p, c):
        lanes = tile_of(p, 128)

        def tile(t, c):
            rows = tile_of(t)
            q, mask = qq[rows, lanes], fq[rows, :]
            res = [blk[pl.ds(pl.multiple_of(a * n + t * TILE, TILE), TILE), lanes] for a in range(2)]
            for a in range(2):
                qa = jnp.where(low_t, q, mask) if a == 0 else jnp.where(low_t, mask, q)
                shift = jnp.log(res[a]) * -8.0
                hi, lo = two(shift)
                lo2 = (shift - hi.astype(F32) - lo.astype(F32)).astype(BF16)
                s = 64 * (1 - a)
                qaug[p * 2 + a, rows, :] = jnp.where(
                    lane_t == s + 6, hi, jnp.where(lane_t == s + 7, lo, jnp.where(lane_t == s + 8, lo2, qa)))
            num = jnp.where(low_t, res[0], res[1])
            den = pltpu.roll(jnp.where(low_t, res[1], res[0]), 64, 1)
            att[rows, lanes] = (num / den).astype(BF16)
            return c

        lax.fori_loop(0, tiles, tile, 0)
        return c

    lax.fori_loop(0, pairs, close, 0)
    w_step(6)
    for i in range(tiles):
        rows = slice(i * TILE, (i + 1) * TILE)
        m = own[rows, :].astype(F32) + dot(att[rows, :], wout[...])
        mid[rows, :] = m
        sx[rows, :] = (rows_norm(m)[0] * vecs[2:3, :] + vecs[3:4, :]).astype(BF16)
        s_copy(i).start()
    quad = chips // 2
    gy_copy.wait_recv()
    for j in range(tiles):
        s_copy(j).wait_recv()

    def feed(begin, span, lanes, turn, after):
        up = wbuf.at[begin:begin + span]
        down = wbuf.at[chips * f + begin:chips * f + begin + span]

        def tile(i, c):
            rows = tile_of((i + turn) % (2 * tiles))
            acts, slopes = [], []
            for j in range(span // TILE):
                cs = slice(j * TILE, (j + 1) * TILE)
                to = slice(lanes + j * TILE, lanes + (j + 1) * TILE)
                pre = dot(sx[rows, :], up[cs, :], NT)
                gh = dot(sg[rows, :], down[cs, :], NT)
                cdf = 0.5 + 0.5 * lax.erf(pre * 0.7071067811865476)
                slope = cdf + pre * (jnp.exp(-0.5 * pre * pre) * 0.3989422804014327)
                acts.append((pre * cdf).astype(BF16))
                slopes.append((gh * slope).astype(BF16))
                hid[rows, to] = acts[-1]
                gpre[rows, to] = slopes[-1]
            o = dot(jnp.concatenate(acts, 1), down[...])
            t = dot(jnp.concatenate(slopes, 1), up[...])
            blk[rows, :] = blk[rows, :] + o if begin else o
            gs[rows, :] = gs[rows, :] + t if begin else t
            after(i)
            return c

        lax.fori_loop(0, 2 * tiles, tile, 0)

    def outer(g):
        def block(j, c):
            for k, (lhs, rhs) in enumerate(((gpre, sx), (hid, sg))):
                part = dot(lhs[:, pl.ds(pl.multiple_of(j * 2 * f, 2 * f), 2 * f)], rhs[...], TN)
                for m in range(2):
                    one = part[m * f:(m + 1) * f]
                    at = g * quad + 2 * j + m

                    @pl.when(at == 0)
                    def _():
                        first[k] = one

                    @pl.when(at > 0)
                    def _():
                        accout[jnp.maximum(at - 1, 0), k] = one.astype(BF16)
            return c

        lax.fori_loop(0, quad // 2, block, 0)

    half_way = quad * f
    last = 2 * quad * f - TILE
    feed(0, half_way, 0, 0, lambda i: at_points(i, ((0, 7), (1, 8), (3, 9)), w_step))
    outer(0)
    w_step(10)
    w_step(11)
    for k in range(2):
        for c in a_copies(1, k):
            c.start()
    feed(half_way, last - half_way, 0, tiles, lambda i: None)
    w_step(12)
    w_step(13)

    def send_parts(i):
        @pl.when(i == tiles - 1)
        def _():
            for c in parts:
                c.start()

    feed(last, TILE, last - half_way, tiles, send_parts)
    r_step(0)
    outer(1)

    for j in range(chips - 1):
        for k in range(2):
            for c in w_copies(j, k):
                c.wait_send()
    for i in range(tiles):
        s_copy(i).wait_send()
    gbr, gat = sx.at[0:n], sx.at[n:2 * n]
    small[...] = jnp.zeros_like(small)
    parts[0].wait_recv()

    def mid_tile(i, c):
        rows = tile_of(i)
        xh, r = rows_norm(mid[rows, :])
        dy = gs[rows, :] + prec[1, rows, :]
        small[2:3, :] += jnp.sum(dy * xh, axis=0, keepdims=True)
        small[3:4, :] += jnp.sum(dy, axis=0, keepdims=True)
        gd = dy * vecs[2:3, :]
        dx = r * (gd - jnp.mean(gd, -1, keepdims=True) - xh * jnp.mean(gd * xh, -1, keepdims=True))
        gm = gy[rows, :].astype(F32) + dx
        base[rows, :] = gm
        low = gm.astype(BF16)
        gbr[rows, :] = low
        gat[rows, :] = dot(low, wout[...], NT).astype(BF16)
        return c

    lax.fori_loop(0, tiles, mid_tile, 0)
    r_step(1)
    parts[1].wait_recv()
    out[...] = (mid[...] + (blk[0:n, :] + prec[0])).astype(BF16)

    groups = (hid, gpre, sg, kk)
    hr, qr = width // 2, width // 4

    def g_copy(j):
        return copy_to(groups[j].at[pl.ds(pl.multiple_of((1 - core) * hr, hr), hr)], pbuf.at[j], gsend.at[j],
                       grecv.at[j], partner)

    def x_copy(j):
        return copy_to(groups[j].at[pl.ds(width, qr)], xin.at[j], xsend.at[j], xrecv.at[j], across)

    def chip_sum(j, side):
        return (groups[j][pl.ds(pl.multiple_of(core * hr + side * qr, qr), qr), :].astype(F32)
                + pbuf[j, pl.ds(pl.multiple_of(side * qr, qr), qr), :].astype(F32))

    def middle_sum(j):
        g_copy(j).wait_recv()
        groups[j][width:width + qr, :] = chip_sum(j, 1 - x).astype(BF16)
        x_copy(j).start()

    def last_sum(j):
        x_copy(j).wait_recv()
        quarter[:, j * width:(j + 1) * width] = (chip_sum(j, x) + xin[j].astype(F32)).astype(BF16)

    def proj_tile(i, c):
        rows = tile_of(i)
        hid[rows, :] = dot(att[:, rows], gbr[...], TN).astype(BF16)
        return c

    lax.fori_loop(0, width // TILE, proj_tile, 0)
    g_copy(0).start()

    def qkv_group(j, points):
        lanes = slice((j - 1) * TILE, j * TILE)

        def tile(i, c):
            rows = tile_of(i)
            for part, (at, size) in enumerate(((0, n), (2 * n, 2 * n), (4 * n, 2 * n))):
                groups[j][rows, part * TILE:(part + 1) * TILE] = dot(
                    normed[0:size, rows], wbuf[at:at + size, lanes], TN).astype(BF16)
            at_points(i, points, r_step)
            return c

        lax.fori_loop(0, width // TILE, tile, 0)
        g_copy(j).start()

    def keys_of(j, rows):
        return wbuf.at[pl.ds(pl.multiple_of(j * 2 * n + rows, TILE), TILE)]

    def mix(part, rows):
        return pl.ds(part * 2 * n + rows.start, rows.size)

    ones_p = slice(0, 128)

    def norm_back(dy, y, r, gain):
        group = ones[ones_p, ones_p]
        dy = dy * 0.125
        y = y.astype(F32)
        prod = dy * y
        gd = dy * gain
        m1 = group_sum(gd, group) * (1 / 64)
        m2 = group_sum(prod, group) * (1 / 64)
        inv = 1.0 / gain
        return r * (gd - m1 - y * inv * m2), jnp.sum(prod, 0, keepdims=True) * inv

    def pair(p, c):
        at_points(p, ((1, 3), (2, 5), (3, 6), (4, 8), (5, 9)), r_step)
        at_points(p, ((1, 0),), middle_sum)
        at_points(p, ((3, 0), (5, 1)), last_sum)
        lanes = tile_of(p, 128)
        do = gat[:, lanes]
        delta = -group_sum(do.astype(F32) * att[:, lanes].astype(F32), swap[...])
        hi, lo = two(delta)
        zero = jnp.zeros_like(do)
        das = []
        for a in range(2):
            s = 64 * (1 - a)
            extra = jnp.where(lane_n == s, hi, jnp.where(lane_n == s + 1, lo, zero))
            das.append(jnp.where(low_n, do, extra) if a == 0 else jnp.where(low_n, extra, do))

        acc = [None, None]
        for t in range(2):
            if t:
                at_points(p, ((0, 2),), r_step)
                at_points(p, ((2, 1), (4, 2)), middle_sum)
            rows = slice(t * n, (t + 1) * n)
            k, v, feat = kk[rows, lanes], vv[rows, lanes], fk[rows, :]
            one = jnp.ones_like(v)
            dks, dvs = [], []
            for a in range(2):
                ka = jnp.where(low_n, k, feat) if a == 0 else jnp.where(low_n, feat, k)
                va = jnp.where(low_n, v, one) if a == 0 else jnp.where(low_n, one, v)
                qa = qaug[p * 2 + a]
                e = jnp.exp2(dot(ka, qa, NT) * (LOG2E / 8))
                ds = (e * dot(va, das[a], NT)).astype(BF16)
                dvs.append(dot(e.astype(BF16), das[a]))
                dks.append(dot(ds, qa))
                dq = dot(ka, ds, TN)
                acc[a] = dq if t == 0 else acc[a] + dq
            dk[rows, :] = jnp.where(low_n, dks[0], dks[1])
            wbuf[4 * n + t * n:4 * n + (t + 1) * n, lanes] = jnp.where(low_n, dvs[0], dvs[1]).astype(BF16)
        low_s = lax.broadcasted_iota(jnp.int32, (128, n), 0) < 64
        dq = jnp.where(low_s, acc[0], acc[1]).T
        qa = jnp.where(low_n, qaug[p * 2], qaug[p * 2 + 1])
        dx, gg = norm_back(dq, qa, rq[:, lanes], vecs[4:5, lanes])
        wbuf[0:n, lanes] = dx.astype(BF16)
        small[4:5, lanes] = gg
        dx, gg = norm_back(dk[...], kk[:, lanes], rk[:, lanes], vecs[5:6, lanes])
        wbuf[2 * n:4 * n, lanes] = dx.astype(BF16)
        small[5:6, lanes] = gg
        at_points(p, ((1, 4), (3, 7), (5, 10)), r_step)
        at_points(p, ((1, 1), (3, 2)), lambda j: qkv_group(j, ()))
        return c

    lax.fori_loop(0, pairs, pair, 0)
    qkv_group(3, ((1, 11),))

    def gain_sums(xh, gn):
        small[0:1, :] += jnp.sum(gn * xh, axis=0, keepdims=True)
        small[1:2, :] += jnp.sum(gn, axis=0, keepdims=True)

    def rem_tile(i, c):
        rows = tile_of(i)
        gn = (dot(wbuf[pl.ds(pl.multiple_of(3 * n + i * TILE, TILE), TILE), :], wqkv[:, width:2 * width], NT)
              + dot(wbuf[pl.ds(pl.multiple_of(5 * n + i * TILE, TILE), TILE), :], wqkv[:, 2 * width:], NT))
        gn_rem[rows, :] = gn.astype(BF16)
        gain_sums(rows_norm(rem[rows, :].astype(F32))[0], gn)
        return c

    def own_back(i, c):
        rows = tile_of(i)
        gn = (dot(wbuf[rows, :], wqkv[:, 0:width], NT)
              + dot(wbuf[pl.ds(pl.multiple_of(2 * n + i * TILE, TILE), TILE), :], wqkv[:, width:2 * width], NT)
              + dot(wbuf[pl.ds(pl.multiple_of(4 * n + i * TILE, TILE), TILE), :], wqkv[:, 2 * width:], NT))
        xh, r = rows_norm(own[rows, :].astype(F32))
        gain_sums(xh, gn)
        gd = gn * vecs[0:1, :]
        base[rows, :] += r * (gd - jnp.mean(gd, -1, keepdims=True) - xh * jnp.mean(gd * xh, -1, keepdims=True))
        return c

    lax.fori_loop(0, tiles, rem_tile, 0)
    middle_sum(3)
    r_step(12)
    last_sum(2)
    lax.fori_loop(0, tiles, own_back, 0)
    r_step(13)
    mine[...] = (first[...] + accin[chips - 2].astype(F32)).astype(BF16)
    for j in range(1, chips):
        for k in range(2):
            for c in a_copies(j, k):
                c.wait_send()
    for i in range(tiles):
        t_copy(i).wait_send()
    last_sum(3)
    for j in range(4):
        g_copy(j).wait_send()
        x_copy(j).wait_send()
    for c in (gy_copy,) + parts:
        c.wait_send()


def layer_call(n_seq, own, gy, seg, g1, b1, wqkv, qg, kg, wout, g2, b2, wup, wdown):
    n, width = own.shape
    f = wup.shape[0]
    chips = n_seq // 2
    heads = width // 64
    tiles = n // TILE
    V, D = pltpu.VMEM, pltpu.SemaphoreType.DMA
    return pl.pallas_call(
        functools.partial(layer_body, n_seq),
        out_shape=(sds((n, width), BF16), sds((n, width), F32), sds((n, width), BF16),
                   sds((width // 4, 4 * width), BF16), sds((8, width), F32), sds((2, f, width), BF16)),
        in_specs=[VM] * 13,
        out_specs=(VM,) * 6,
        scratch_shapes=[
            V((n, width), BF16), V((n, 128), BF16), V((2 * n, 128), BF16), V((256, 256), BF16), V((128, 128), BF16),
            V((8, width), F32), V((2 * n, width), BF16), V((2 * n, width), BF16), V((2 * n, width), BF16),
            V((n, width), BF16), V((n, width), F32), V((2 * n, width), F32), V((heads, n, 128), BF16),
            V((n, width), BF16), V((n, width), F32),
            V((2 * n, width), BF16), V((2 * n, width), BF16), V((chips * 2 * f, width), BF16),
            V((chips - 1, 2, f, width), BF16), V((chips - 1, 2, f, width), BF16), V((2, f, width), F32),
            V((2 * n, chips // 2 * f), BF16), V((2 * n, chips // 2 * f), BF16), V((2 * n, width), F32), V((2 * n, width), F32),
            V((2, n, width), F32),
            V((2 * n, 128), F32), V((4, width // 2, width), BF16), V((4, width // 4, width), BF16),
            D((2, 2, chips - 1)), D((2, 2, chips - 1)), D((2, 2, chips - 1)), D((2, 2, chips - 1)),
            D((3 + tiles,)), D((3 + tiles,)), D((tiles,)), D((tiles,)),
            D((4,)), D((4,)), D((4,)), D((4,))],
        compiler_params=pltpu.CompilerParams(
            vmem_limit_bytes=66 * 1000 * 1000, collective_id=1, has_side_effects=True),
        name="layer",
    )(own, gy, seg, g1, b1, wqkv, qg, kg, wout, g2, b2, wup, wdown)


def local_one(tokens, segment_ids, first_gain, first_bias, w_qkv, query_gain, key_gain, w_out,
              second_gain, second_bias, w_up, w_down, out_grad):
    n_seq = lax.axis_size("seq")
    own = tokens[0]
    block_out, base, gn_rem, quarter, small, mine = layer_call(
        n_seq, own, out_grad[0], segment_ids, first_gain, first_bias, w_qkv, query_gain, key_gain, w_out,
        second_gain, second_bias, w_up.T, w_down.T)
    g, small, gback, other = sum_call(n_seq, quarter, small, gn_rem, mine)
    qkv, proj, fg, fb, qgg, kgg, sgg, sbg, input_grad, up_grad, down_grad, block_out = finish_call(
        g, small, own, gback, base, first_gain, mine, other, block_out)
    return (block_out[None], input_grad[None], fg, fb, qkv, qgg, kgg, proj, sgg, sbg, up_grad.T, down_grad.T)


def layer_norm(rows, gain, shift):
    average = jnp.mean(rows, axis=-1, keepdims=True)
    centred = rows - average
    spread = jnp.mean(centred * centred, axis=-1, keepdims=True)
    return centred * lax.rsqrt(spread + EPS) * gain + shift


def head_norm(values, gain):
    average = jnp.mean(values, axis=-1, keepdims=True)
    centred = values - average
    spread = jnp.mean(centred * centred, axis=-1, keepdims=True)
    return centred * lax.rsqrt(spread + EPS) * gain


def qk_norms(raw_query, raw_keys, query_gain, key_gain):
    return (head_norm(raw_query, query_gain), head_norm(raw_keys, key_gain))


def gelu_exact(values):
    return jax.nn.gelu(values, approximate=False)


def gelu_back(pre, upstream):
    return jax.vjp(gelu_exact, pre)[1](upstream)[0]


def group_size(count, length):
    for option in range(1, count + 1):
        if count % option == 0 and option * length >= 512:
            return option
    return count


def rows_product(left, right):
    return lax.dot_general(
        left, right, (((0,), (0,)), ((), ())), preferred_element_type=jnp.float32
    )


def cols_product(left, right):
    return lax.dot_general(
        left, right, (((1,), (1,)), ((), ())), preferred_element_type=jnp.float32
    )


def local(
    tokens,
    segment_ids,
    first_gain,
    first_bias,
    w_qkv,
    query_gain,
    key_gain,
    w_out,
    second_gain,
    second_bias,
    w_up,
    w_down,
    out_grad,
):
    seqs_here, local_len, width = tokens.shape
    full_len = segment_ids.shape[1]
    head_dim = query_gain.shape[0]
    heads = width // head_dim
    rows_here = seqs_here * local_len
    scale = head_dim ** (-0.5)
    offset = lax.axis_index("pos") * local_len
    query_marks = lax.dynamic_slice_in_dim(segment_ids, offset, local_len, 1)
    block = group_size(seqs_here, local_len)
    count_blocks = seqs_here // block

    def split(array):
        return array.reshape((count_blocks, block) + array.shape[1:])

    inputs = tokens.astype(jnp.float32).reshape(rows_here, width)
    normed_low = layer_norm(inputs, first_gain, first_bias).astype(jnp.bfloat16)
    mixed = jnp.dot(normed_low, w_qkv, preferred_element_type=jnp.float32).reshape(
        rows_here, 3, heads, head_dim
    )
    raw_query = mixed[:, 0]
    raw_keys = mixed[:, 1]
    query = (
        head_norm(raw_query, query_gain)
        .astype(jnp.bfloat16)
        .reshape(seqs_here, local_len, heads, head_dim)
    )
    keys_local = (
        head_norm(raw_keys, key_gain).astype(jnp.bfloat16).reshape(seqs_here, local_len, width)
    )
    values_local = mixed[:, 2].astype(jnp.bfloat16).reshape(seqs_here, local_len, width)
    keys_all, values_all = (
        lax.all_gather(keys_local, "pos", axis=1, tiled=True),
        lax.all_gather(values_local, "pos", axis=1, tiled=True),
    )
    keys_four = keys_all.reshape(seqs_here, full_len, heads, head_dim)
    values_four = values_all.reshape(seqs_here, full_len, heads, head_dim)

    def scores_for(query_blk, keys_blk, query_lab, key_lab):
        raw = (
            jnp.einsum("bqhd,bkhd->bhqk", query_blk, keys_blk, preferred_element_type=jnp.float32)
            * scale
        )
        allowed = (query_lab[:, :, None] == key_lab[:, None, :])[:, None]
        return jnp.where(allowed, raw, -1e30)

    def forward_block(packed):
        query_blk, keys_blk, values_blk, query_lab, key_lab = packed
        scores = scores_for(query_blk, keys_blk, query_lab, key_lab)
        peak = jnp.max(scores, axis=-1, keepdims=True)
        expd = jnp.exp(scores - peak)
        totals = jnp.sum(expd, axis=-1, keepdims=True)
        probs = (expd / totals).astype(jnp.bfloat16)
        result = jnp.einsum(
            "bhqk,bkhd->bqhd", probs, values_blk, preferred_element_type=jnp.float32
        )
        return (result, peak + jnp.log(totals))

    attended, log_totals = lax.map(
        forward_block,
        (
            split(query),
            split(keys_four),
            split(values_four),
            split(query_marks),
            split(segment_ids),
        ),
    )
    attended_low = attended.astype(jnp.bfloat16).reshape(rows_here, width)
    middle = inputs + jnp.dot(attended_low, w_out, preferred_element_type=jnp.float32)
    second_low = layer_norm(middle, second_gain, second_bias).astype(jnp.bfloat16)
    grad_out = out_grad.reshape(rows_here, width)
    grad_float = grad_out.astype(jnp.float32)
    up_all, down_all = (
        lax.all_gather(w_up, "seq", axis=1, tiled=True),
        lax.all_gather(w_down, "seq", axis=1, tiled=True),
    )
    pre = jnp.dot(second_low, up_all, preferred_element_type=jnp.float32)
    hidden = gelu_exact(pre).astype(jnp.bfloat16)
    block_out = (middle + cols_product(hidden, down_all)).astype(jnp.bfloat16)
    grad_hidden = jnp.dot(grad_out, down_all, preferred_element_type=jnp.float32)
    grad_pre = gelu_back(pre, grad_hidden).astype(jnp.bfloat16)
    down_full = rows_product(grad_out, hidden)
    up_full = rows_product(second_low, grad_pre)
    grad_second = cols_product(grad_pre, up_all)
    up_part, down_part = (
        lax.psum_scatter(
            up_full.astype(jnp.bfloat16), "seq", scatter_dimension=1, tiled=True
        ).astype(jnp.float32),
        lax.psum_scatter(
            down_full.astype(jnp.bfloat16), "seq", scatter_dimension=1, tiled=True
        ).astype(jnp.float32),
    )
    up_grad, down_grad = (
        lax.psum(up_part.astype(jnp.bfloat16), "pos").astype(jnp.float32),
        lax.psum(down_part.astype(jnp.bfloat16), "pos").astype(jnp.float32),
    )
    second_back = jax.vjp(layer_norm, middle, second_gain, second_bias)[1]
    grad_middle_part, second_gain_part, second_bias_part = second_back(grad_second)
    grad_middle = grad_float + grad_middle_part
    grad_branch = grad_middle.astype(jnp.bfloat16)
    proj_part = rows_product(attended_low, grad_branch)
    grad_attended = (
        cols_product(grad_branch, w_out)
        .astype(jnp.bfloat16)
        .reshape(seqs_here, local_len, heads, head_dim)
    )

    def backward_block(packed):
        query_blk, keys_blk, values_blk, query_lab, key_lab, log_blk, grad_blk = packed
        scores = scores_for(query_blk, keys_blk, query_lab, key_lab)
        probs = jnp.exp(scores - log_blk)
        grad_probs = jnp.einsum(
            "bqhd,bkhd->bhqk", grad_blk, values_blk, preferred_element_type=jnp.float32
        )
        grad_values = jnp.einsum(
            "bhqk,bqhd->bkhd",
            probs.astype(jnp.bfloat16),
            grad_blk,
            preferred_element_type=jnp.float32,
        )
        inner = jnp.sum(probs * grad_probs, axis=-1, keepdims=True)
        grad_scores = (probs * (grad_probs - inner) * scale).astype(jnp.bfloat16)
        grad_query = jnp.einsum(
            "bhqk,bkhd->bqhd", grad_scores, keys_blk, preferred_element_type=jnp.float32
        )
        grad_keys = jnp.einsum(
            "bhqk,bqhd->bkhd", grad_scores, query_blk, preferred_element_type=jnp.float32
        )
        return (grad_query, grad_keys, grad_values)

    grad_query, grad_keys, grad_values = lax.map(
        backward_block,
        (
            split(query),
            split(keys_four),
            split(values_four),
            split(query_marks),
            split(segment_ids),
            log_totals,
            split(grad_attended),
        ),
    )
    grad_keys = grad_keys.reshape(seqs_here, full_len, width)
    grad_values = grad_values.reshape(seqs_here, full_len, width)
    keys_grad, values_grad = (
        lax.psum_scatter(
            grad_keys.astype(jnp.bfloat16), "pos", scatter_dimension=1, tiled=True
        ).astype(jnp.float32),
        lax.psum_scatter(
            grad_values.astype(jnp.bfloat16), "pos", scatter_dimension=1, tiled=True
        ).astype(jnp.float32),
    )
    norm_back = jax.vjp(qk_norms, raw_query, raw_keys, query_gain, key_gain)[1]
    grad_raw_query, grad_raw_keys, query_gain_part, key_gain_part = norm_back(
        (
            grad_query.reshape(rows_here, heads, head_dim),
            keys_grad.reshape(rows_here, heads, head_dim),
        )
    )
    grad_mixed = (
        jnp.stack(
            [grad_raw_query, grad_raw_keys, values_grad.reshape(rows_here, heads, head_dim)], axis=1
        )
        .reshape(rows_here, 3 * width)
        .astype(jnp.bfloat16)
    )
    qkv_part = rows_product(normed_low, grad_mixed)
    grad_normed = cols_product(grad_mixed, w_qkv)
    first_back = jax.vjp(layer_norm, inputs, first_gain, first_bias)[1]
    grad_input_part, first_gain_part, first_bias_part = first_back(grad_normed)
    input_grad = (grad_middle + grad_input_part).reshape(seqs_here, local_len, width)
    (
        qkv_grad,
        proj_grad,
        first_gain_grad,
        first_bias_grad,
        query_gain_grad,
        key_gain_grad,
        second_gain_grad,
        second_bias_grad,
    ) = lax.psum(
        (
            qkv_part,
            proj_part,
            first_gain_part,
            first_bias_part,
            query_gain_part,
            key_gain_part,
            second_gain_part,
            second_bias_part,
        ),
        ("pos", "seq"),
    )
    return (
        block_out.reshape(seqs_here, local_len, width),
        input_grad,
        first_gain_grad,
        first_bias_grad,
        qkv_grad,
        query_gain_grad,
        key_gain_grad,
        proj_grad,
        second_gain_grad,
        second_bias_grad,
        up_grad,
        down_grad,
    )


def solution(mesh):
    placed = (P("seq", "pos", None), P("seq", None), P(), P(), P(), P(), P(), P(), P(), P(),
              P(None, "seq"), P(None, "seq"), P("seq", "pos", None))
    outs = (P("seq", "pos", None), P("seq", "pos", None), P(), P(), P(), P(), P(), P(), P(), P(),
            P(None, "seq"), P(None, "seq"))

    def step(*args):
        def run(*local_args):
            one = local_args[0].shape[:2] == (1, 512) and (mesh.shape["pos"], mesh.shape["seq"]) == (2, 16)
            return (local_one if one else local)(*local_args)

        return jax.shard_map(run, mesh=mesh, in_specs=placed, out_specs=outs, check_vma=False)(*args)

    return step
```

```python
import functools
import jax
import jax.numpy as jnp
from jax import lax
from jax.experimental import pallas as pl
from jax.experimental.pallas import tpu as pltpu
from jax.sharding import PartitionSpec as P

EPS = 1e-06
F32 = jnp.float32
BF16 = jnp.bfloat16
LOG2E = 1.4426950408889634
BIG = 16384.0
TILE = 256
NT = (((1,), (1,)), ((), ()))
NN = (((1,), (0,)), ((), ()))
TN = (((0,), (0,)), ((), ()))


def dot(a, b, dims=NN):
    return lax.dot_general(a, b, dims, preferred_element_type=F32)


def two(x):
    hi = x.astype(BF16)
    return hi, (x - hi.astype(F32)).astype(BF16)


def group_sum(x, ones):
    hi, lo = two(x)
    return dot(hi, ones) + dot(lo, ones)


def rows_norm(x):
    average = jnp.mean(x, axis=-1, keepdims=True)
    centred = x - average
    spread = jnp.mean(centred * centred, axis=-1, keepdims=True)
    scale = lax.rsqrt(spread + EPS)
    return centred * scale, scale


def tile_of(i, size=TILE):
    return pl.ds(pl.multiple_of(i * size, size), size)


VM = pl.BlockSpec(memory_space=pltpu.VMEM)
LIMIT = 60 * 1024 * 1024


def sds(shape, dtype):
    return jax.ShapeDtypeStruct(shape, dtype)


def ring_places(n_seq):
    s = lax.axis_index("seq")
    core, chip = s % 2, s // 2
    chips = n_seq // 2
    half = chips // 2
    odd = chip % 2
    place = (1 - odd) * (chip // 2) + odd * (chips - 1 - chip // 2)

    def device(p):
        far = p // half
        return ((1 - far) * 2 * p + far * (2 * (chips - 1 - p) + 1)) * 2 + core

    right = device((place + 1) % chips)
    left = device((place + chips - 1) % chips)
    return core, place, right, left, s + 1 - 2 * core


def copy_to(src, dst, send, recv, target):
    return pltpu.make_async_remote_copy(
        src_ref=src, dst_ref=dst, send_sem=send, recv_sem=recv, device_id=target,
        device_id_type=pl.DeviceIdType.MESH)


def greet(targets):
    barrier = pltpu.get_barrier_semaphore()
    for t in targets:
        pl.semaphore_signal(barrier, inc=1, device_id=t, device_id_type=pl.DeviceIdType.MESH)
    pl.semaphore_wait(barrier, len(targets))


def sum_body(n_seq, quarter, small, gn_rem, mine, fin, sout, gback, other,
             accin, accout, srec, sring,
             asend, arecv, xsend, xrecv, fsend, frecv, qsend, qrecv, ssend, srecv, gsend, grecv):
    qrows, cols = quarter.shape
    chips = n_seq // 2
    cw, pr, hr = cols // chips, qrows // 4, qrows // 2
    core, place, right, left, partner = ring_places(n_seq)
    x = lax.axis_index("pos")
    right, left, partner, across = {"seq": right}, {"seq": left}, {"seq": partner}, {"pos": 1 - x}
    greet((right, left, partner, across))

    def chunk(p):
        return (p + 2 * chips) % chips

    def lanes_of(p):
        return pl.ds(pl.multiple_of(p * cw, cw), cw)

    def rows_of(c, o, d):
        side = 1 - x if o else x
        return pl.ds(pl.multiple_of(c * 2 * qrows + side * qrows + d * hr, hr), hr)

    half = chips // 2

    def a_copy(d, i, s):
        return copy_to(accout.at[s - 1, d, i], accin.at[s - 1, d, i], asend.at[s - 1, d, i], arecv.at[s - 1, d, i],
                       left if d else right)

    def x_piece(i, side, p):
        ref = fin.at[pl.ds(pl.multiple_of(core * 2 * qrows + side * qrows + i * pr, pr), pr), lanes_of(p)]
        return copy_to(ref, ref, xsend.at[i], xrecv.at[i], across)

    def ring_copy(d, o, e, s, p):
        ref = fin.at[rows_of(core, o, e), lanes_of(p)]
        return copy_to(ref, ref, fsend.at[s, d, o * 2 + e], frecv.at[s, d, o * 2 + e], left if d else right)

    def f_copy(d, o, e, s):
        return ring_copy(d, o, e, s, chunk(place + s) if d else chunk(place - s))

    def f_recv(d, o, e, s):
        return ring_copy(d, o, e, s, chunk(place + s + 1) if d else chunk(place - s - 1))

    def pair_copy(c, d, o, e, s):
        ref = fin.at[rows_of(c, o, e), lanes_of(chunk(place + s) if d else chunk(place - s))]
        return copy_to(ref, ref, qsend.at[s, d, o * 2 + e], qrecv.at[s, d, o * 2 + e], partner)

    def s_copy(s):
        return copy_to(sring.at[chunk(place - s)], sring.at[chunk(place - s)], ssend.at[s], srecv.at[s], right)

    def s_recv(s):
        p = chunk(place - s - 1)
        return copy_to(sring.at[p], sring.at[p], ssend.at[s], srecv.at[s], right)

    n = gn_rem.shape[0]
    backs = [copy_to(gn_rem.at[pl.ds(i * n // 2, n // 2)], gback.at[pl.ds(i * n // 2, n // 2)],
                     gsend.at[4 * i], grecv.at[4 * i], across) for i in range(2)]
    small_p = copy_to(small, srec.at[0], gsend.at[1], grecv.at[1], partner)
    small_x = copy_to(srec.at[1], srec.at[2], gsend.at[2], grecv.at[2], across)
    ffn_x = copy_to(mine, other, gsend.at[3], grecv.at[3], across)
    pieces = (0, 2, 1, 3)
    halves = [(o, e) for o in range(2) for e in range(2)]
    arrivals = [(d, o, e, s) for s in range(1, half + 1) for o, e in halves for d in range(2) if s < half or e == d]
    pairs = [(0, o, e, 0) for o, e in halves] + arrivals

    small_p.start()

    def part(i, q):
        return quarter[i * pr:(i + 1) * pr, lanes_of(q)].astype(F32)

    def reduce_piece(d, i, s, first):
        q = chunk(place - (half + 1 - s)) if d else chunk(place + (half + 1 - s))
        value = part(i, q)
        if not first:
            a_copy(d, i, s - 1).wait_recv()
            value = value + accin[s - 2, d, i].astype(F32)
        accout[s - 1, d, i] = value.astype(BF16)
        a_copy(d, i, s).start()

    hops = [(d, i, s) for s in range(1, half + 1) for i in (2, 3, 0, 1) for d in range(2)]
    hops = [(d, (i + 2 * d) % 4, s) for d, i, s in hops]
    hops = [(d, i, s) for d, i, s in hops if s > 1 or i // 2 == d]
    for d, i, s in hops:
        reduce_piece(d, i, s, s == (1 if i // 2 == d else 2))
        if (d, i, s) == hops[7]:
            backs[0].start()
            small_p.wait_recv()
            srec[1] = small[...] + srec[0]
            small_x.start()

    def own_start(o, e):
        for d in range(2):
            f_copy(d, o, e, 0).start()
        pair_copy(core, 0, o, e, 0).start()

    for i in pieces:
        total = part(i, place)
        for d in range(2):
            a_copy(d, i, half).wait_recv()
            total = total + accin[half - 1, d, i].astype(F32)
        at = pl.ds(pl.multiple_of(core * 2 * qrows + x * qrows + i * pr, pr), pr)
        fin[at, lanes_of(place)] = total.astype(BF16)
        x_piece(i, x, place).start()
        if i % 2:
            own_start(0, i // 2)
    backs[1].start()
    small_x.wait_recv()
    sring[place] = srec[1] + srec[2]
    s_copy(0).start()
    for i in pieces:
        x_piece(i, 1 - x, place).wait_recv()
        if i % 2:
            own_start(1, i // 2)
    ffn_x.start()

    for at, (d, o, e, s) in enumerate(arrivals):
        f_recv(d, o, e, s - 1).wait_recv()
        if s < half - 1 or (s == half - 1 and e == d):
            f_copy(d, o, e, s).start()
        pair_copy(core, d, o, e, s).start()
        if at % 4 == 3:
            step = at // 4
            s_recv(step).wait_recv()
            if step < chips - 2:
                s_copy(step + 1).start()

    total = sring[0]
    for s in range(1, chips):
        total = total + sring[s]
    sout[...] = total
    for d, o, e, s in pairs:
        pair_copy(1 - core, d, o, e, s).wait_recv()
    for c in backs + [ffn_x]:
        c.wait_recv()
    for d, o, e, s in pairs:
        pair_copy(core, d, o, e, s).wait_send()
    for d, o, e, s in arrivals:
        f_copy(d, o, e, s - 1).wait_send()
    for s in range(chips - 1):
        s_copy(s).wait_send()
    for i in pieces:
        x_piece(i, x, place).wait_send()
    for d, i, s in hops:
        a_copy(d, i, s).wait_send()
    for c in backs + [small_p, small_x, ffn_x]:
        c.wait_send()


def sum_call(n_seq, quarter, small, gn_rem, mine):
    qrows, cols = quarter.shape
    chips = n_seq // 2
    pr, cw = qrows // 4, cols // chips
    V, D = pltpu.VMEM, pltpu.SemaphoreType.DMA
    return pl.pallas_call(
        functools.partial(sum_body, n_seq),
        out_shape=(sds((4 * qrows, cols), BF16), sds(small.shape, F32), sds(gn_rem.shape, BF16),
                   sds(mine.shape, BF16)),
        in_specs=[VM, VM] + [pl.BlockSpec(memory_space=pl.ANY)] * 2,
        out_specs=(VM, VM) + (pl.BlockSpec(memory_space=pl.ANY),) * 2,
        scratch_shapes=[
            V((chips // 2, 2, 4, pr, cw), BF16), V((chips // 2, 2, 4, pr, cw), BF16),
            V((3,) + small.shape, F32), V((chips,) + small.shape, F32),
            D((chips // 2, 2, 4)), D((chips // 2, 2, 4)), D((4,)), D((4,)),
            D((chips // 2, 2, 4)), D((chips // 2, 2, 4)), D((chips // 2 + 1, 2, 4)), D((chips // 2 + 1, 2, 4)),
            D((chips - 1,)), D((chips - 1,)), D((5,)), D((5,))],
        compiler_params=pltpu.CompilerParams(
            vmem_limit_bytes=LIMIT, collective_id=2, has_side_effects=True),
        name="sums",
    )(quarter, small, gn_rem, mine)


def finish_body(g, small, own, gback, base, g1, mine, other, block, qkv, proj, fg, fb, qgg, kgg, sgg, sbg,
                igrad, upg, downg, out):
    width = proj.shape[1]
    proj[...] = g[:, 0:width].astype(F32)
    for j in range(3):
        for part in range(3):
            at = (j + 1) * width + part * TILE
            qkv[:, part * width + j * TILE:part * width + (j + 1) * TILE] = g[:, at:at + TILE].astype(F32)
    xh, r = rows_norm(own[...].astype(F32))
    dy = gback[...].astype(F32) * g1[...].reshape(1, width)
    dx = r * (dy - jnp.mean(dy, -1, keepdims=True) - xh * jnp.mean(dy * xh, -1, keepdims=True))
    igrad[...] = base[...] + dx
    out[...] = block[...]

    total = mine[...].astype(F32) + other[...].astype(F32)
    upg[...] = total[0]
    downg[...] = total[1]

    @pl.when(pl.program_id(0) == 0)
    def _():
        for i, ref in enumerate((fg, fb, sgg, sbg)):
            ref[...] = small[i:i + 1, :].reshape(width)
        for i, ref in ((4, qgg), (5, kgg)):
            folded = small[i:i + 1, 0:128]
            for j in range(1, width // 128):
                folded = folded + small[i:i + 1, j * 128:(j + 1) * 128]
            folded = folded + pltpu.roll(folded, 64, 1)
            ref[...] = folded[:, 0:64].reshape(64)


def finish_call(g, small, own, gback, base, g1, mine, other, block):
    rows, cols = g.shape
    n, width = own.shape
    f = mine.shape[1]
    steps = 2
    whole = lambda size: pl.BlockSpec((size,), lambda i: (0,))
    strip = lambda size, lanes: pl.BlockSpec((size // steps, lanes), lambda i: (i, 0))
    ffn_in = pl.BlockSpec((2, f // steps, width), lambda i: (0, i, 0))
    return pl.pallas_call(
        finish_body, grid=(steps,),
        out_shape=(sds((rows, 3 * width), F32), sds((rows, width), F32), sds((width,), F32), sds((width,), F32),
                   sds((64,), F32), sds((64,), F32), sds((width,), F32), sds((width,), F32),
                   sds((n, width), F32), sds((f, width), F32), sds((f, width), F32), sds((n, width), BF16)),
        in_specs=[strip(rows, cols), pl.BlockSpec(small.shape, lambda i: (0, 0)), strip(n, width), strip(n, width),
                  strip(n, width), whole(width), ffn_in, ffn_in, strip(n, width)],
        out_specs=(strip(rows, 3 * width), strip(rows, width),
                   whole(width), whole(width), whole(64), whole(64), whole(width), whole(width),
                   strip(n, width), strip(f, width), strip(f, width), strip(n, width)),
        name="finish",
    )(g, small, own, gback, base, g1, mine, other, block)


def layer_body(n_seq, own, gy, seg, g1, b1, far_qkv, qg, kg, far_out, g2, b2, wup, wdown,
               out, base, gn_rem, quarter, small, mine,
               rem, fq, fk, ones, swap, vecs, normed, kk, vv, qq, rq, rk, qaug, att, mid,
               sx, sg, wbuf, accin, accout, first, hid, gpre, blk, gs, prec,
               dk, pbuf, xin, wqkv, wout,
               wsend, wrecv, asend, arecv, psend, precv, tsend, trecv, gsend, grecv, xsend, xrecv, lsem):
    n, width = own.shape
    f = wup.shape[0]
    h = f // 2
    chips = n_seq // 2
    pairs = width // 128
    tiles = n // TILE
    core, place, right, left, partner = ring_places(n_seq)
    x = lax.axis_index("pos")
    right, left, partner, across = {"seq": right}, {"seq": left}, {"seq": partner}, {"pos": 1 - x}
    fetch = [pltpu.make_async_copy(far, near, lsem.at[i]) for i, (far, near) in
             enumerate(((far_qkv, wqkv), (far_out, wout)))]
    for c in fetch:
        c.start()
    greet((right, left, partner, across))

    def slot(s, k, d):
        return pl.ds(pl.multiple_of((k * chips + s) * f + d * h, h), h)

    def w_copies(s, k):
        return [copy_to(wbuf.at[slot(s, k, d)] if s else (wdown if k else wup).at[pl.ds(d * h, h)],
                        wbuf.at[slot(s + 1, k, d)], wsend.at[d, k, s], wrecv.at[d, k, s],
                        left if d else right) for d in range(2)]

    def a_copies(s, k):
        rows = [pl.ds(d * h, h) for d in range(2)]
        return [copy_to(accout.at[s - 1, k, rows[d]], accin.at[s - 1, k, rows[d]], asend.at[d, k, s - 1],
                        arecv.at[d, k, s - 1], left if d else right) for d in range(2)]

    def w_step(i):
        s, k = i // 2 + 1, i % 2
        for c in w_copies(s - 1, k):
            c.wait_recv()
        if s < chips - 1:
            for c in w_copies(s, k):
                c.start()

    def r_step(j):
        s, k = j // 2 + 1, j % 2
        for c in a_copies(s, k):
            c.wait_recv()
        if s < chips - 1:
            accout[s, k] = (accout[s, k].astype(F32) + accin[s - 1, k].astype(F32)).astype(BF16)
            for c in a_copies(s + 1, k):
                c.start()

    def at_points(now, points, step):
        for when, item in points:
            @pl.when(now == when)
            def _():
                step(item)

    def t_copy(i):
        rows = pl.ds(i * TILE, TILE)
        return copy_to(own.at[rows], rem.at[rows], tsend.at[i], trecv.at[i], across)

    def s_copy(i):
        return copy_to(sx.at[pl.ds(i * TILE, TILE)], sx.at[pl.ds(n + i * TILE, TILE)], psend.at[3 + i],
                       precv.at[3 + i], partner)

    gy_copy = copy_to(gy, sg.at[pl.ds(n, n)], psend.at[0], precv.at[0], partner)
    parts = (copy_to(gs.at[pl.ds(n, n)], prec.at[1], psend.at[1], precv.at[1], partner),
             copy_to(blk.at[pl.ds(n, n)], prec.at[0], psend.at[2], precv.at[2], partner))

    for k in range(2):
        for c in w_copies(0, k):
            c.start()
    for i in range(tiles):
        t_copy(i).start()
    gy_copy.start()

    at = pl.multiple_of(x * n, n)
    labels = jnp.concatenate([seg[:, pl.ds(at, n)], seg[:, pl.ds(n - at, n)]], axis=1)
    lane = lax.broadcasted_iota(jnp.int32, (128, 2 * n), 0) % 64
    same = lane == labels
    keyed = jnp.where((lane >= 6) & (lane <= 8), 1.0, jnp.where(same & (lane < 6), 1.0, 0.0))
    fk[...] = keyed.T.astype(BF16)
    away = jnp.where((lane < 6) & jnp.logical_not(same), -BIG, 0.0)
    fq[...] = away[:, 0:n].T.astype(BF16)
    ra = lax.broadcasted_iota(jnp.int32, ones.shape, 0) // 64
    rb = lax.broadcasted_iota(jnp.int32, ones.shape, 1) // 64
    ones[...] = jnp.where(ra == rb, 1.0, 0.0).astype(BF16)
    swap[...] = jnp.where(ra[:128, :128] == rb[:128, :128], 0.0, 1.0).astype(BF16)
    for i, v in enumerate((g1, b1, g2, b2)):
        vecs[i:i + 1, :] = v[...].reshape(1, width)
    for i, v in enumerate((qg, kg)):
        r = v[...].reshape(1, 64)
        vecs[4 + i:5 + i, :] = jnp.concatenate([r] * (width // 64), axis=1)
    sg[0:n, :] = gy[...]
    wbuf[0:f, :] = wup[...]
    wbuf[chips * f:(chips + 1) * f, :] = wdown[...]
    cols = ones.shape[0]

    def project(xs, i, queries):
        rows = tile_of(i)
        low = (rows_norm(xs)[0] * vecs[0:1, :] + vecs[1:2, :]).astype(BF16)
        normed[:, rows] = low.T
        for block in range(0 if queries else width // cols, 3 * width // cols):
            raw = dot(low, wqkv[:, block * cols:(block + 1) * cols])
            part, a = divmod(block * cols, width)
            lanes = slice(a, a + cols)
            if part == 2:
                vv[rows, lanes] = raw.astype(BF16)
                continue
            centred = raw - group_sum(raw, ones[...]) * (1 / 64)
            scale = lax.rsqrt(group_sum(centred * centred, ones[...]) * (1 / 64) + EPS)
            dst, rdst = (qq, rq) if part == 0 else (kk, rk)
            dst[rows, lanes] = (centred * scale * vecs[4 + part:5 + part, lanes]).astype(BF16)
            rdst[rows, lanes] = scale

    def own_tile(i, c):
        project(own[tile_of(i), :].astype(F32), i, True)
        return c

    fetch[0].wait()
    lax.fori_loop(0, tiles, own_tile, 0)
    w_step(0)
    lane_t = lax.broadcasted_iota(jnp.int32, (TILE, 128), 1)
    low_t = lane_t < 64
    lane_n = lax.broadcasted_iota(jnp.int32, (n, 128), 1)
    low_n = lane_n < 64

    def attend(krows, size, add, after):
        low_k = lax.broadcasted_iota(jnp.int32, (size, 128), 1) < 64

        def pair(p, c):
            lanes = tile_of(p, 128)
            k, v, feat = kk[krows, lanes], vv[krows, lanes], fk[krows, :]
            one = jnp.ones_like(v)
            ks = (jnp.where(low_k, k, feat), jnp.where(low_k, feat, k))
            vs = (jnp.where(low_k, v, one), jnp.where(low_k, one, v))

            q, mask = qq[:, lanes], fq[...]
            for a in range(2):
                qa = jnp.where(low_n, q, mask) if a == 0 else jnp.where(low_n, mask, q)
                e = jnp.exp2(dot(qa, ks[a], NT) * (LOG2E / 8)).astype(BF16)
                o = dot(e, vs[a])
                to = slice(a * n, (a + 1) * n)
                blk[to, lanes] = blk[to, lanes] + o if add else o
            if after is not None:
                after(p)
            return c

        lax.fori_loop(0, pairs, pair, 0)

    attend(slice(0, n), n, False, lambda p: at_points(p, ((1, 1), (4, 2)), w_step))
    for i in range(tiles):
        t_copy(i).wait_recv()
        project(rem[i * TILE:(i + 1) * TILE, :].astype(F32), tiles + i, False)
        if i == 0:
            w_step(3)
        attend(slice(n + i * TILE, n + (i + 1) * TILE), TILE, True,
               lambda p: at_points(p, ((1, 5),) if i else ((5, 4),), w_step))

    def close(p, c):
        lanes = tile_of(p, 128)

        def tile(t, c):
            rows = tile_of(t)
            q, mask = qq[rows, lanes], fq[rows, :]
            res = [blk[pl.ds(pl.multiple_of(a * n + t * TILE, TILE), TILE), lanes] for a in range(2)]
            for a in range(2):
                qa = jnp.where(low_t, q, mask) if a == 0 else jnp.where(low_t, mask, q)
                shift = jnp.log(res[a]) * -8.0
                hi, lo = two(shift)
                lo2 = (shift - hi.astype(F32) - lo.astype(F32)).astype(BF16)
                s = 64 * (1 - a)
                qaug[p * 2 + a, rows, :] = jnp.where(
                    lane_t == s + 6, hi, jnp.where(lane_t == s + 7, lo, jnp.where(lane_t == s + 8, lo2, qa)))
            num = jnp.where(low_t, res[0], res[1])
            den = pltpu.roll(jnp.where(low_t, res[1], res[0]), 64, 1)
            att[rows, lanes] = (num / den).astype(BF16)
            return c

        lax.fori_loop(0, tiles, tile, 0)
        return c

    lax.fori_loop(0, pairs, close, 0)
    w_step(6)
    fetch[1].wait()
    for i in range(tiles):
        rows = slice(i * TILE, (i + 1) * TILE)
        m = own[rows, :].astype(F32) + dot(att[rows, :], wout[...])
        mid[rows, :] = m
        sx[rows, :] = (rows_norm(m)[0] * vecs[2:3, :] + vecs[3:4, :]).astype(BF16)
        s_copy(i).start()
    quad = chips // 2
    gy_copy.wait_recv()
    for j in range(tiles):
        s_copy(j).wait_recv()

    def feed(begin, span, lanes, turn, after):
        up = wbuf.at[begin:begin + span]
        down = wbuf.at[chips * f + begin:chips * f + begin + span]

        def tile(i, c):
            rows = tile_of((i + turn) % (2 * tiles))
            acts, slopes = [], []
            for j in range(span // TILE):
                cs = slice(j * TILE, (j + 1) * TILE)
                to = slice(lanes + j * TILE, lanes + (j + 1) * TILE)
                pre = dot(sx[rows, :], up[cs, :], NT)
                gh = dot(sg[rows, :], down[cs, :], NT)
                cdf = 0.5 + 0.5 * lax.erf(pre * 0.7071067811865476)
                slope = cdf + pre * (jnp.exp(-0.5 * pre * pre) * 0.3989422804014327)
                acts.append((pre * cdf).astype(BF16))
                slopes.append((gh * slope).astype(BF16))
                hid[rows, to] = acts[-1]
                gpre[rows, to] = slopes[-1]
            o = dot(jnp.concatenate(acts, 1), down[...])
            t = dot(jnp.concatenate(slopes, 1), up[...])
            blk[rows, :] = blk[rows, :] + o if begin else o
            gs[rows, :] = gs[rows, :] + t if begin else t
            after(i)
            return c

        lax.fori_loop(0, 2 * tiles, tile, 0)

    def outer(g):
        def block(j, c):
            for k, (lhs, rhs) in enumerate(((gpre, sx), (hid, sg))):
                part = dot(lhs[:, pl.ds(pl.multiple_of(j * 2 * f, 2 * f), 2 * f)], rhs[...], TN)
                for m in range(2):
                    one = part[m * f:(m + 1) * f]
                    at = g * quad + 2 * j + m

                    @pl.when(at == 0)
                    def _():
                        first[k] = one

                    @pl.when(at > 0)
                    def _():
                        accout[jnp.maximum(at - 1, 0), k] = one.astype(BF16)
            return c

        lax.fori_loop(0, quad // 2, block, 0)

    half_way = quad * f
    last = 2 * quad * f - TILE
    feed(0, half_way, 0, 0, lambda i: at_points(i, ((0, 7), (1, 8), (3, 9)), w_step))
    outer(0)
    w_step(10)
    w_step(11)
    for k in range(2):
        for c in a_copies(1, k):
            c.start()
    feed(half_way, last - half_way, 0, tiles, lambda i: None)
    w_step(12)
    w_step(13)

    def send_parts(i):
        @pl.when(i == tiles - 1)
        def _():
            for c in parts:
                c.start()

    feed(last, TILE, last - half_way, tiles, send_parts)
    r_step(0)
    outer(1)

    for j in range(chips - 1):
        for k in range(2):
            for c in w_copies(j, k):
                c.wait_send()
    for i in range(tiles):
        s_copy(i).wait_send()
    gbr, gat = sx.at[0:n], sx.at[n:2 * n]
    small[...] = jnp.zeros_like(small)
    parts[0].wait_recv()

    def mid_tile(i, c):
        rows = tile_of(i)
        xh, r = rows_norm(mid[rows, :])
        dy = gs[rows, :] + prec[1, rows, :]
        small[2:3, :] += jnp.sum(dy * xh, axis=0, keepdims=True)
        small[3:4, :] += jnp.sum(dy, axis=0, keepdims=True)
        gd = dy * vecs[2:3, :]
        dx = r * (gd - jnp.mean(gd, -1, keepdims=True) - xh * jnp.mean(gd * xh, -1, keepdims=True))
        gm = gy[rows, :].astype(F32) + dx
        base[rows, :] = gm
        low = gm.astype(BF16)
        gbr[rows, :] = low
        gat[rows, :] = dot(low, wout[...], NT).astype(BF16)
        return c

    lax.fori_loop(0, tiles, mid_tile, 0)
    r_step(1)
    parts[1].wait_recv()
    out[...] = (mid[...] + (blk[0:n, :] + prec[0])).astype(BF16)

    groups = (hid, gpre, sg, kk)
    hr, qr = width // 2, width // 4

    def g_copy(j):
        return copy_to(groups[j].at[pl.ds(pl.multiple_of((1 - core) * hr, hr), hr)], pbuf.at[j], gsend.at[j],
                       grecv.at[j], partner)

    def x_copy(j):
        return copy_to(groups[j].at[pl.ds(width, qr)], xin.at[j], xsend.at[j], xrecv.at[j], across)

    def chip_sum(j, side):
        return (groups[j][pl.ds(pl.multiple_of(core * hr + side * qr, qr), qr), :].astype(F32)
                + pbuf[j, pl.ds(pl.multiple_of(side * qr, qr), qr), :].astype(F32))

    def middle_sum(j):
        g_copy(j).wait_recv()
        groups[j][width:width + qr, :] = chip_sum(j, 1 - x).astype(BF16)
        x_copy(j).start()

    def last_sum(j):
        x_copy(j).wait_recv()
        quarter[:, j * width:(j + 1) * width] = (chip_sum(j, x) + xin[j].astype(F32)).astype(BF16)

    def proj_tile(i, c):
        rows = tile_of(i)
        hid[rows, :] = dot(att[:, rows], gbr[...], TN).astype(BF16)
        return c

    lax.fori_loop(0, width // TILE, proj_tile, 0)
    g_copy(0).start()

    def qkv_group(j, points):
        lanes = slice((j - 1) * TILE, j * TILE)

        def tile(i, c):
            rows = tile_of(i)
            for part, (at, size) in enumerate(((0, n), (2 * n, 2 * n), (4 * n, 2 * n))):
                groups[j][rows, part * TILE:(part + 1) * TILE] = dot(
                    normed[rows, 0:size], wbuf[at:at + size, lanes]).astype(BF16)
            at_points(i, points, r_step)
            return c

        lax.fori_loop(0, width // TILE, tile, 0)
        g_copy(j).start()

    def keys_of(j, rows):
        return wbuf.at[pl.ds(pl.multiple_of(j * 2 * n + rows, TILE), TILE)]

    def mix(part, rows):
        return pl.ds(part * 2 * n + rows.start, rows.size)

    ones_p = slice(0, 128)

    def norm_back(dy, y, r, gain):
        group = ones[ones_p, ones_p]
        dy = dy * 0.125
        y = y.astype(F32)
        prod = dy * y
        gd = dy * gain
        m1 = group_sum(gd, group) * (1 / 64)
        m2 = group_sum(prod, group) * (1 / 64)
        inv = 1.0 / gain
        return r * (gd - m1 - y * inv * m2), jnp.sum(prod, 0, keepdims=True) * inv

    def pair(p, c):
        at_points(p, ((1, 3), (2, 5), (3, 6), (4, 8), (5, 9)), r_step)
        at_points(p, ((1, 0),), middle_sum)
        at_points(p, ((3, 0), (5, 1)), last_sum)
        lanes = tile_of(p, 128)
        do = gat[:, lanes]
        delta = -group_sum(do.astype(F32) * att[:, lanes].astype(F32), swap[...])
        hi, lo = two(delta)
        zero = jnp.zeros_like(do)
        das = []
        for a in range(2):
            s = 64 * (1 - a)
            extra = jnp.where(lane_n == s, hi, jnp.where(lane_n == s + 1, lo, zero))
            das.append(jnp.where(low_n, do, extra) if a == 0 else jnp.where(low_n, extra, do))

        acc = [None, None]
        for t in range(2):
            if t:
                at_points(p, ((0, 2),), r_step)
                at_points(p, ((2, 1), (4, 2)), middle_sum)
            rows = slice(t * n, (t + 1) * n)
            k, v, feat = kk[rows, lanes], vv[rows, lanes], fk[rows, :]
            one = jnp.ones_like(v)
            dks, dvs = [], []
            for a in range(2):
                ka = jnp.where(low_n, k, feat) if a == 0 else jnp.where(low_n, feat, k)
                va = jnp.where(low_n, v, one) if a == 0 else jnp.where(low_n, one, v)
                qa = qaug[p * 2 + a]
                e = jnp.exp2(dot(ka, qa, NT) * (LOG2E / 8))
                ds = (e * dot(va, das[a], NT)).astype(BF16)
                dvs.append(dot(e.astype(BF16), das[a]))
                dks.append(dot(ds, qa))
                dq = dot(ka, ds, TN)
                acc[a] = dq if t == 0 else acc[a] + dq
            dk[rows, :] = jnp.where(low_n, dks[0], dks[1])
            wbuf[4 * n + t * n:4 * n + (t + 1) * n, lanes] = jnp.where(low_n, dvs[0], dvs[1]).astype(BF16)
        low_s = lax.broadcasted_iota(jnp.int32, (128, n), 0) < 64
        dq = jnp.where(low_s, acc[0], acc[1]).T
        qa = jnp.where(low_n, qaug[p * 2], qaug[p * 2 + 1])
        dx, gg = norm_back(dq, qa, rq[:, lanes], vecs[4:5, lanes])
        wbuf[0:n, lanes] = dx.astype(BF16)
        small[4:5, lanes] = gg
        dx, gg = norm_back(dk[...], kk[:, lanes], rk[:, lanes], vecs[5:6, lanes])
        wbuf[2 * n:4 * n, lanes] = dx.astype(BF16)
        small[5:6, lanes] = gg
        at_points(p, ((1, 4), (3, 7), (5, 10)), r_step)
        at_points(p, ((1, 1), (3, 2)), lambda j: qkv_group(j, ()))
        return c

    lax.fori_loop(0, pairs, pair, 0)
    qkv_group(3, ((1, 11),))

    def gain_sums(xh, gn):
        small[0:1, :] += jnp.sum(gn * xh, axis=0, keepdims=True)
        small[1:2, :] += jnp.sum(gn, axis=0, keepdims=True)

    def rem_tile(i, c):
        rows = tile_of(i)
        gn = (dot(wbuf[pl.ds(pl.multiple_of(3 * n + i * TILE, TILE), TILE), :], wqkv[:, width:2 * width], NT)
              + dot(wbuf[pl.ds(pl.multiple_of(5 * n + i * TILE, TILE), TILE), :], wqkv[:, 2 * width:], NT))
        gn_rem[rows, :] = gn.astype(BF16)
        gain_sums(rows_norm(rem[rows, :].astype(F32))[0], gn)
        at_points(i, ((0, 3),), middle_sum)
        return c

    def own_back(i, c):
        rows = tile_of(i)
        gn = (dot(wbuf[rows, :], wqkv[:, 0:width], NT)
              + dot(wbuf[pl.ds(pl.multiple_of(2 * n + i * TILE, TILE), TILE), :], wqkv[:, width:2 * width], NT)
              + dot(wbuf[pl.ds(pl.multiple_of(4 * n + i * TILE, TILE), TILE), :], wqkv[:, 2 * width:], NT))
        xh, r = rows_norm(own[rows, :].astype(F32))
        gain_sums(xh, gn)
        gd = gn * vecs[0:1, :]
        base[rows, :] += r * (gd - jnp.mean(gd, -1, keepdims=True) - xh * jnp.mean(gd * xh, -1, keepdims=True))
        return c

    lax.fori_loop(0, tiles, rem_tile, 0)
    r_step(12)
    last_sum(2)
    lax.fori_loop(0, tiles, own_back, 0)
    r_step(13)
    mine[...] = (first[...] + accin[chips - 2].astype(F32)).astype(BF16)
    for j in range(1, chips):
        for k in range(2):
            for c in a_copies(j, k):
                c.wait_send()
    for i in range(tiles):
        t_copy(i).wait_send()
    last_sum(3)
    for j in range(4):
        g_copy(j).wait_send()
        x_copy(j).wait_send()
    for c in (gy_copy,) + parts:
        c.wait_send()


def layer_call(n_seq, own, gy, seg, g1, b1, wqkv, qg, kg, wout, g2, b2, wup, wdown):
    n, width = own.shape
    f = wup.shape[0]
    chips = n_seq // 2
    heads = width // 64
    tiles = n // TILE
    V, D = pltpu.VMEM, pltpu.SemaphoreType.DMA
    return pl.pallas_call(
        functools.partial(layer_body, n_seq),
        out_shape=(sds((n, width), BF16), sds((n, width), F32), sds((n, width), BF16),
                   sds((width // 4, 4 * width), BF16), sds((8, width), F32), sds((2, f, width), BF16)),
        in_specs=[VM] * 5 + [pl.BlockSpec(memory_space=pl.ANY), VM, VM, pl.BlockSpec(memory_space=pl.ANY)] + [VM] * 4,
        out_specs=(VM,) * 6,
        scratch_shapes=[
            V((n, width), BF16), V((n, 128), BF16), V((2 * n, 128), BF16), V((256, 256), BF16), V((128, 128), BF16),
            V((8, width), F32), V((width, 2 * n), BF16), V((2 * n, width), BF16), V((2 * n, width), BF16),
            V((n, width), BF16), V((n, width), F32), V((2 * n, width), F32), V((heads, n, 128), BF16),
            V((n, width), BF16), V((n, width), F32),
            V((2 * n, width), BF16), V((2 * n, width), BF16), V((chips * 2 * f, width), BF16),
            V((chips - 1, 2, f, width), BF16), V((chips - 1, 2, f, width), BF16), V((2, f, width), F32),
            V((2 * n, chips // 2 * f), BF16), V((2 * n, chips // 2 * f), BF16), V((2 * n, width), F32), V((2 * n, width), F32),
            V((2, n, width), F32),
            V((2 * n, 128), F32), V((4, width // 2, width), BF16), V((4, width // 4, width), BF16),
            V(wqkv.shape, BF16), V(wout.shape, BF16),
            D((2, 2, chips - 1)), D((2, 2, chips - 1)), D((2, 2, chips - 1)), D((2, 2, chips - 1)),
            D((3 + tiles,)), D((3 + tiles,)), D((tiles,)), D((tiles,)),
            D((4,)), D((4,)), D((4,)), D((4,)), D((2,))],
        compiler_params=pltpu.CompilerParams(
            vmem_limit_bytes=66 * 1000 * 1000, collective_id=1, has_side_effects=True),
        name="layer",
    )(own, gy, seg, g1, b1, wqkv, qg, kg, wout, g2, b2, wup, wdown)


def local_one(tokens, segment_ids, first_gain, first_bias, w_qkv, query_gain, key_gain, w_out,
              second_gain, second_bias, w_up, w_down, out_grad):
    n_seq = lax.axis_size("seq")
    own = tokens[0]
    block_out, base, gn_rem, quarter, small, mine = layer_call(
        n_seq, own, out_grad[0], segment_ids, first_gain, first_bias, w_qkv, query_gain, key_gain, w_out,
        second_gain, second_bias, w_up.T, w_down.T)
    g, small, gback, other = sum_call(n_seq, quarter, small, gn_rem, mine)
    qkv, proj, fg, fb, qgg, kgg, sgg, sbg, input_grad, up_grad, down_grad, block_out = finish_call(
        g, small, own, gback, base, first_gain, mine, other, block_out)
    return (block_out[None], input_grad[None], fg, fb, qkv, qgg, kgg, proj, sgg, sbg, up_grad.T, down_grad.T)


def layer_norm(rows, gain, shift):
    average = jnp.mean(rows, axis=-1, keepdims=True)
    centred = rows - average
    spread = jnp.mean(centred * centred, axis=-1, keepdims=True)
    return centred * lax.rsqrt(spread + EPS) * gain + shift


def head_norm(values, gain):
    average = jnp.mean(values, axis=-1, keepdims=True)
    centred = values - average
    spread = jnp.mean(centred * centred, axis=-1, keepdims=True)
    return centred * lax.rsqrt(spread + EPS) * gain


def qk_norms(raw_query, raw_keys, query_gain, key_gain):
    return (head_norm(raw_query, query_gain), head_norm(raw_keys, key_gain))


def gelu_exact(values):
    return jax.nn.gelu(values, approximate=False)


def gelu_back(pre, upstream):
    return jax.vjp(gelu_exact, pre)[1](upstream)[0]


def group_size(count, length):
    for option in range(1, count + 1):
        if count % option == 0 and option * length >= 512:
            return option
    return count


def rows_product(left, right):
    return lax.dot_general(
        left, right, (((0,), (0,)), ((), ())), preferred_element_type=jnp.float32
    )


def cols_product(left, right):
    return lax.dot_general(
        left, right, (((1,), (1,)), ((), ())), preferred_element_type=jnp.float32
    )


def local(
    tokens,
    segment_ids,
    first_gain,
    first_bias,
    w_qkv,
    query_gain,
    key_gain,
    w_out,
    second_gain,
    second_bias,
    w_up,
    w_down,
    out_grad,
):
    seqs_here, local_len, width = tokens.shape
    full_len = segment_ids.shape[1]
    head_dim = query_gain.shape[0]
    heads = width // head_dim
    rows_here = seqs_here * local_len
    scale = head_dim ** (-0.5)
    offset = lax.axis_index("pos") * local_len
    query_marks = lax.dynamic_slice_in_dim(segment_ids, offset, local_len, 1)
    block = group_size(seqs_here, local_len)
    count_blocks = seqs_here // block

    def split(array):
        return array.reshape((count_blocks, block) + array.shape[1:])

    inputs = tokens.astype(jnp.float32).reshape(rows_here, width)
    normed_low = layer_norm(inputs, first_gain, first_bias).astype(jnp.bfloat16)
    mixed = jnp.dot(normed_low, w_qkv, preferred_element_type=jnp.float32).reshape(
        rows_here, 3, heads, head_dim
    )
    raw_query = mixed[:, 0]
    raw_keys = mixed[:, 1]
    query = (
        head_norm(raw_query, query_gain)
        .astype(jnp.bfloat16)
        .reshape(seqs_here, local_len, heads, head_dim)
    )
    keys_local = (
        head_norm(raw_keys, key_gain).astype(jnp.bfloat16).reshape(seqs_here, local_len, width)
    )
    values_local = mixed[:, 2].astype(jnp.bfloat16).reshape(seqs_here, local_len, width)
    keys_all, values_all = (
        lax.all_gather(keys_local, "pos", axis=1, tiled=True),
        lax.all_gather(values_local, "pos", axis=1, tiled=True),
    )
    keys_four = keys_all.reshape(seqs_here, full_len, heads, head_dim)
    values_four = values_all.reshape(seqs_here, full_len, heads, head_dim)

    def scores_for(query_blk, keys_blk, query_lab, key_lab):
        raw = (
            jnp.einsum("bqhd,bkhd->bhqk", query_blk, keys_blk, preferred_element_type=jnp.float32)
            * scale
        )
        allowed = (query_lab[:, :, None] == key_lab[:, None, :])[:, None]
        return jnp.where(allowed, raw, -1e30)

    def forward_block(packed):
        query_blk, keys_blk, values_blk, query_lab, key_lab = packed
        scores = scores_for(query_blk, keys_blk, query_lab, key_lab)
        peak = jnp.max(scores, axis=-1, keepdims=True)
        expd = jnp.exp(scores - peak)
        totals = jnp.sum(expd, axis=-1, keepdims=True)
        probs = (expd / totals).astype(jnp.bfloat16)
        result = jnp.einsum(
            "bhqk,bkhd->bqhd", probs, values_blk, preferred_element_type=jnp.float32
        )
        return (result, peak + jnp.log(totals))

    attended, log_totals = lax.map(
        forward_block,
        (
            split(query),
            split(keys_four),
            split(values_four),
            split(query_marks),
            split(segment_ids),
        ),
    )
    attended_low = attended.astype(jnp.bfloat16).reshape(rows_here, width)
    middle = inputs + jnp.dot(attended_low, w_out, preferred_element_type=jnp.float32)
    second_low = layer_norm(middle, second_gain, second_bias).astype(jnp.bfloat16)
    grad_out = out_grad.reshape(rows_here, width)
    grad_float = grad_out.astype(jnp.float32)
    up_all, down_all = (
        lax.all_gather(w_up, "seq", axis=1, tiled=True),
        lax.all_gather(w_down, "seq", axis=1, tiled=True),
    )
    pre = jnp.dot(second_low, up_all, preferred_element_type=jnp.float32)
    hidden = gelu_exact(pre).astype(jnp.bfloat16)
    block_out = (middle + cols_product(hidden, down_all)).astype(jnp.bfloat16)
    grad_hidden = jnp.dot(grad_out, down_all, preferred_element_type=jnp.float32)
    grad_pre = gelu_back(pre, grad_hidden).astype(jnp.bfloat16)
    down_full = rows_product(grad_out, hidden)
    up_full = rows_product(second_low, grad_pre)
    grad_second = cols_product(grad_pre, up_all)
    up_part, down_part = (
        lax.psum_scatter(
            up_full.astype(jnp.bfloat16), "seq", scatter_dimension=1, tiled=True
        ).astype(jnp.float32),
        lax.psum_scatter(
            down_full.astype(jnp.bfloat16), "seq", scatter_dimension=1, tiled=True
        ).astype(jnp.float32),
    )
    up_grad, down_grad = (
        lax.psum(up_part.astype(jnp.bfloat16), "pos").astype(jnp.float32),
        lax.psum(down_part.astype(jnp.bfloat16), "pos").astype(jnp.float32),
    )
    second_back = jax.vjp(layer_norm, middle, second_gain, second_bias)[1]
    grad_middle_part, second_gain_part, second_bias_part = second_back(grad_second)
    grad_middle = grad_float + grad_middle_part
    grad_branch = grad_middle.astype(jnp.bfloat16)
    proj_part = rows_product(attended_low, grad_branch)
    grad_attended = (
        cols_product(grad_branch, w_out)
        .astype(jnp.bfloat16)
        .reshape(seqs_here, local_len, heads, head_dim)
    )

    def backward_block(packed):
        query_blk, keys_blk, values_blk, query_lab, key_lab, log_blk, grad_blk = packed
        scores = scores_for(query_blk, keys_blk, query_lab, key_lab)
        probs = jnp.exp(scores - log_blk)
        grad_probs = jnp.einsum(
            "bqhd,bkhd->bhqk", grad_blk, values_blk, preferred_element_type=jnp.float32
        )
        grad_values = jnp.einsum(
            "bhqk,bqhd->bkhd",
            probs.astype(jnp.bfloat16),
            grad_blk,
            preferred_element_type=jnp.float32,
        )
        inner = jnp.sum(probs * grad_probs, axis=-1, keepdims=True)
        grad_scores = (probs * (grad_probs - inner) * scale).astype(jnp.bfloat16)
        grad_query = jnp.einsum(
            "bhqk,bkhd->bqhd", grad_scores, keys_blk, preferred_element_type=jnp.float32
        )
        grad_keys = jnp.einsum(
            "bhqk,bqhd->bkhd", grad_scores, query_blk, preferred_element_type=jnp.float32
        )
        return (grad_query, grad_keys, grad_values)

    grad_query, grad_keys, grad_values = lax.map(
        backward_block,
        (
            split(query),
            split(keys_four),
            split(values_four),
            split(query_marks),
            split(segment_ids),
            log_totals,
            split(grad_attended),
        ),
    )
    grad_keys = grad_keys.reshape(seqs_here, full_len, width)
    grad_values = grad_values.reshape(seqs_here, full_len, width)
    keys_grad, values_grad = (
        lax.psum_scatter(
            grad_keys.astype(jnp.bfloat16), "pos", scatter_dimension=1, tiled=True
        ).astype(jnp.float32),
        lax.psum_scatter(
            grad_values.astype(jnp.bfloat16), "pos", scatter_dimension=1, tiled=True
        ).astype(jnp.float32),
    )
    norm_back = jax.vjp(qk_norms, raw_query, raw_keys, query_gain, key_gain)[1]
    grad_raw_query, grad_raw_keys, query_gain_part, key_gain_part = norm_back(
        (
            grad_query.reshape(rows_here, heads, head_dim),
            keys_grad.reshape(rows_here, heads, head_dim),
        )
    )
    grad_mixed = (
        jnp.stack(
            [grad_raw_query, grad_raw_keys, values_grad.reshape(rows_here, heads, head_dim)], axis=1
        )
        .reshape(rows_here, 3 * width)
        .astype(jnp.bfloat16)
    )
    qkv_part = rows_product(normed_low, grad_mixed)
    grad_normed = cols_product(grad_mixed, w_qkv)
    first_back = jax.vjp(layer_norm, inputs, first_gain, first_bias)[1]
    grad_input_part, first_gain_part, first_bias_part = first_back(grad_normed)
    input_grad = (grad_middle + grad_input_part).reshape(seqs_here, local_len, width)
    (
        qkv_grad,
        proj_grad,
        first_gain_grad,
        first_bias_grad,
        query_gain_grad,
        key_gain_grad,
        second_gain_grad,
        second_bias_grad,
    ) = lax.psum(
        (
            qkv_part,
            proj_part,
            first_gain_part,
            first_bias_part,
            query_gain_part,
            key_gain_part,
            second_gain_part,
            second_bias_part,
        ),
        ("pos", "seq"),
    )
    return (
        block_out.reshape(seqs_here, local_len, width),
        input_grad,
        first_gain_grad,
        first_bias_grad,
        qkv_grad,
        query_gain_grad,
        key_gain_grad,
        proj_grad,
        second_gain_grad,
        second_bias_grad,
        up_grad,
        down_grad,
    )


def solution(mesh):
    placed = (P("seq", "pos", None), P("seq", None), P(), P(), P(), P(), P(), P(), P(), P(),
              P(None, "seq"), P(None, "seq"), P("seq", "pos", None))
    outs = (P("seq", "pos", None), P("seq", "pos", None), P(), P(), P(), P(), P(), P(), P(), P(),
            P(None, "seq"), P(None, "seq"))

    def step(*args):
        def run(*local_args):
            one = local_args[0].shape[:2] == (1, 512) and (mesh.shape["pos"], mesh.shape["seq"]) == (2, 16)
            return (local_one if one else local)(*local_args)

        return jax.shard_map(run, mesh=mesh, in_specs=placed, out_specs=outs, check_vma=False)(*args)

    return step
```

```python
import functools
import jax
import jax.numpy as jnp
from jax import lax
from jax.experimental import pallas as pl
from jax.experimental.pallas import tpu as pltpu
from jax.sharding import PartitionSpec as P

EPS = 1e-06
F32 = jnp.float32
BF16 = jnp.bfloat16
LOG2E = 1.4426950408889634
BIG = 16384.0
TILE = 256
NT = (((1,), (1,)), ((), ()))
NN = (((1,), (0,)), ((), ()))
TN = (((0,), (0,)), ((), ()))


def dot(a, b, dims=NN):
    return lax.dot_general(a, b, dims, preferred_element_type=F32)


def two(x):
    hi = x.astype(BF16)
    return hi, (x - hi.astype(F32)).astype(BF16)


def group_sum(x, ones):
    hi, lo = two(x)
    return dot(hi, ones) + dot(lo, ones)


def rows_norm(x):
    average = jnp.mean(x, axis=-1, keepdims=True)
    centred = x - average
    spread = jnp.mean(centred * centred, axis=-1, keepdims=True)
    scale = lax.rsqrt(spread + EPS)
    return centred * scale, scale


def tile_of(i, size=TILE):
    return pl.ds(pl.multiple_of(i * size, size), size)


VM = pl.BlockSpec(memory_space=pltpu.VMEM)
LIMIT = 60 * 1024 * 1024


def sds(shape, dtype):
    return jax.ShapeDtypeStruct(shape, dtype)


def ring_places(n_seq):
    s = lax.axis_index("seq")
    core, chip = s % 2, s // 2
    chips = n_seq // 2
    half = chips // 2
    odd = chip % 2
    place = (1 - odd) * (chip // 2) + odd * (chips - 1 - chip // 2)

    def device(p):
        far = p // half
        return ((1 - far) * 2 * p + far * (2 * (chips - 1 - p) + 1)) * 2 + core

    right = device((place + 1) % chips)
    left = device((place + chips - 1) % chips)
    return core, place, right, left, s + 1 - 2 * core


def copy_to(src, dst, send, recv, target):
    return pltpu.make_async_remote_copy(
        src_ref=src, dst_ref=dst, send_sem=send, recv_sem=recv, device_id=target,
        device_id_type=pl.DeviceIdType.MESH)


def greet(targets):
    barrier = pltpu.get_barrier_semaphore()
    for t in targets:
        pl.semaphore_signal(barrier, inc=1, device_id=t, device_id_type=pl.DeviceIdType.MESH)
    pl.semaphore_wait(barrier, len(targets))


def sum_body(n_seq, quarter, small, gn_rem, mine, far_fin, sout, gback, other,
             fin, accin, accout, srec, sring,
             asend, arecv, xsend, xrecv, fsend, frecv, qsend, qrecv, ssend, srecv, gsend, grecv, osem):
    qrows, cols = quarter.shape
    chips = n_seq // 2
    cw, pr, hr = cols // chips, qrows // 4, qrows // 2
    core, place, right, left, partner = ring_places(n_seq)
    x = lax.axis_index("pos")
    right, left, partner, across = {"seq": right}, {"seq": left}, {"seq": partner}, {"pos": 1 - x}
    greet((right, left, partner, across))

    def chunk(p):
        return (p + 2 * chips) % chips

    def lanes_of(p):
        return pl.ds(pl.multiple_of(p * cw, cw), cw)

    def rows_of(c, o, d):
        side = 1 - x if o else x
        return pl.ds(pl.multiple_of(c * 2 * qrows + side * qrows + d * hr, hr), hr)

    half = chips // 2

    def a_copy(d, i, s):
        return copy_to(accout.at[s - 1, d, i], accin.at[s - 1, d, i], asend.at[s - 1, d, i], arecv.at[s - 1, d, i],
                       left if d else right)

    def x_piece(i, side, p):
        ref = fin.at[pl.ds(pl.multiple_of(core * 2 * qrows + side * qrows + i * pr, pr), pr), lanes_of(p)]
        return copy_to(ref, ref, xsend.at[i], xrecv.at[i], across)

    def ring_copy(d, o, e, s, p):
        ref = fin.at[rows_of(core, o, e), lanes_of(p)]
        return copy_to(ref, ref, fsend.at[s, d, o * 2 + e], frecv.at[s, d, o * 2 + e], left if d else right)

    def f_copy(d, o, e, s):
        return ring_copy(d, o, e, s, chunk(place + s) if d else chunk(place - s))

    def f_recv(d, o, e, s):
        return ring_copy(d, o, e, s, chunk(place + s + 1) if d else chunk(place - s - 1))

    def pair_copy(c, d, o, e, s):
        ref = fin.at[rows_of(c, o, e), lanes_of(chunk(place + s) if d else chunk(place - s))]
        return copy_to(ref, ref, qsend.at[s, d, o * 2 + e], qrecv.at[s, d, o * 2 + e], partner)

    def s_copy(s):
        return copy_to(sring.at[chunk(place - s)], sring.at[chunk(place - s)], ssend.at[s], srecv.at[s], right)

    def s_recv(s):
        p = chunk(place - s - 1)
        return copy_to(sring.at[p], sring.at[p], ssend.at[s], srecv.at[s], right)

    n = gn_rem.shape[0]
    backs = [copy_to(gn_rem.at[pl.ds(i * n // 2, n // 2)], gback.at[pl.ds(i * n // 2, n // 2)],
                     gsend.at[4 * i], grecv.at[4 * i], across) for i in range(2)]
    small_p = copy_to(small, srec.at[0], gsend.at[1], grecv.at[1], partner)
    small_x = copy_to(srec.at[1], srec.at[2], gsend.at[2], grecv.at[2], across)
    ffn_x = copy_to(mine, other, gsend.at[3], grecv.at[3], across)
    pieces = (0, 2, 1, 3)
    halves = [(o, e) for o in range(2) for e in range(2)]
    arrivals = [(d, o, e, s) for s in range(1, half + 1) for o, e in halves for d in range(2) if s < half or e == d]
    pairs = [(0, o, e, 0) for o, e in halves] + arrivals

    small_p.start()

    def part(i, q):
        return quarter[i * pr:(i + 1) * pr, lanes_of(q)].astype(F32)

    def reduce_piece(d, i, s, first):
        q = chunk(place - (half + 1 - s)) if d else chunk(place + (half + 1 - s))
        value = part(i, q)
        if not first:
            a_copy(d, i, s - 1).wait_recv()
            value = value + accin[s - 2, d, i].astype(F32)
        accout[s - 1, d, i] = value.astype(BF16)
        a_copy(d, i, s).start()

    hops = [(d, i, s) for s in range(1, half + 1) for i in (2, 3, 0, 1) for d in range(2)]
    hops = [(d, (i + 2 * d) % 4, s) for d, i, s in hops]
    hops = [(d, i, s) for d, i, s in hops if s > 1 or i // 2 == d]
    for d, i, s in hops:
        reduce_piece(d, i, s, s == (1 if i // 2 == d else 2))
        if (d, i, s) == hops[7]:
            backs[0].start()
            small_p.wait_recv()
            srec[1] = small[...] + srec[0]
            small_x.start()

    def own_start(o, e):
        for d in range(2):
            f_copy(d, o, e, 0).start()
        pair_copy(core, 0, o, e, 0).start()

    for i in pieces:
        total = part(i, place)
        for d in range(2):
            a_copy(d, i, half).wait_recv()
            total = total + accin[half - 1, d, i].astype(F32)
        at = pl.ds(pl.multiple_of(core * 2 * qrows + x * qrows + i * pr, pr), pr)
        fin[at, lanes_of(place)] = total.astype(BF16)
        x_piece(i, x, place).start()
        if i % 2:
            own_start(0, i // 2)
    backs[1].start()
    small_x.wait_recv()
    sring[place] = srec[1] + srec[2]
    s_copy(0).start()
    for i in pieces:
        x_piece(i, 1 - x, place).wait_recv()
        if i % 2:
            own_start(1, i // 2)
    ffn_x.start()

    def store(c, p):
        block = (pl.ds(pl.multiple_of(c * 2 * qrows, 2 * qrows), 2 * qrows), lanes_of(p))
        return pltpu.make_async_copy(fin.at[block], far_fin.at[block], osem.at[c, p])

    def store_hop(c, s):
        store(c, chunk(place - s)).start()
        if 0 < s < half:
            store(c, chunk(place + s)).start()

    store_hop(core, 0)
    for at, (d, o, e, s) in enumerate(arrivals):
        f_recv(d, o, e, s - 1).wait_recv()
        if s < half - 1 or (s == half - 1 and e == d):
            f_copy(d, o, e, s).start()
        pair_copy(core, d, o, e, s).start()
        if at + 1 == len(arrivals) or arrivals[at + 1][3] > s:
            store_hop(core, s)
        if at % 4 == 3:
            step = at // 4
            s_recv(step).wait_recv()
            if step < chips - 2:
                s_copy(step + 1).start()

    total = sring[0]
    for s in range(1, chips):
        total = total + sring[s]
    sout[...] = total
    for at, (d, o, e, s) in enumerate(pairs):
        pair_copy(1 - core, d, o, e, s).wait_recv()
        if at + 1 == len(pairs) or pairs[at + 1][3] > s:
            store_hop(1 - core, s)
    for c in backs + [ffn_x]:
        c.wait_recv()
    for d, o, e, s in pairs:
        pair_copy(core, d, o, e, s).wait_send()
    for d, o, e, s in arrivals:
        f_copy(d, o, e, s - 1).wait_send()
    for s in range(chips - 1):
        s_copy(s).wait_send()
    for i in pieces:
        x_piece(i, x, place).wait_send()
    for d, i, s in hops:
        a_copy(d, i, s).wait_send()
    for c in range(2):
        for p in range(chips):
            store(c, p).wait()
    for c in backs + [small_p, small_x, ffn_x]:
        c.wait_send()


def sum_call(n_seq, quarter, small, gn_rem, mine):
    qrows, cols = quarter.shape
    chips = n_seq // 2
    pr, cw = qrows // 4, cols // chips
    V, D = pltpu.VMEM, pltpu.SemaphoreType.DMA
    return pl.pallas_call(
        functools.partial(sum_body, n_seq),
        out_shape=(sds((4 * qrows, cols), BF16), sds(small.shape, F32), sds(gn_rem.shape, BF16),
                   sds(mine.shape, BF16)),
        in_specs=[VM, VM] + [pl.BlockSpec(memory_space=pl.ANY)] * 2,
        out_specs=(pl.BlockSpec(memory_space=pl.ANY), VM) + (pl.BlockSpec(memory_space=pl.ANY),) * 2,
        scratch_shapes=[
            V((4 * qrows, cols), BF16),
            V((chips // 2, 2, 4, pr, cw), BF16), V((chips // 2, 2, 4, pr, cw), BF16),
            V((3,) + small.shape, F32), V((chips,) + small.shape, F32),
            D((chips // 2, 2, 4)), D((chips // 2, 2, 4)), D((4,)), D((4,)),
            D((chips // 2, 2, 4)), D((chips // 2, 2, 4)), D((chips // 2 + 1, 2, 4)), D((chips // 2 + 1, 2, 4)),
            D((chips - 1,)), D((chips - 1,)), D((5,)), D((5,)), D((2, chips))],
        compiler_params=pltpu.CompilerParams(
            vmem_limit_bytes=LIMIT, collective_id=2, has_side_effects=True),
        name="sums",
    )(quarter, small, gn_rem, mine)


def finish_body(g, small, own, gback, base, g1, mine, other, block, qkv, proj, fg, fb, qgg, kgg, sgg, sbg,
                igrad, upg, downg, out):
    width = proj.shape[1]
    proj[...] = g[:, 0:width].astype(F32)
    for j in range(3):
        for part in range(3):
            at = (j + 1) * width + part * TILE
            qkv[:, part * width + j * TILE:part * width + (j + 1) * TILE] = g[:, at:at + TILE].astype(F32)
    xh, r = rows_norm(own[...].astype(F32))
    dy = gback[...].astype(F32) * g1[...].reshape(1, width)
    dx = r * (dy - jnp.mean(dy, -1, keepdims=True) - xh * jnp.mean(dy * xh, -1, keepdims=True))
    igrad[...] = base[...] + dx
    out[...] = block[...]

    total = mine[...].astype(F32) + other[...].astype(F32)
    upg[...] = total[0]
    downg[...] = total[1]

    @pl.when(pl.program_id(0) == 0)
    def _():
        for i, ref in enumerate((fg, fb, sgg, sbg)):
            ref[...] = small[i:i + 1, :].reshape(width)
        for i, ref in ((4, qgg), (5, kgg)):
            folded = small[i:i + 1, 0:128]
            for j in range(1, width // 128):
                folded = folded + small[i:i + 1, j * 128:(j + 1) * 128]
            folded = folded + pltpu.roll(folded, 64, 1)
            ref[...] = folded[:, 0:64].reshape(64)


def finish_call(g, small, own, gback, base, g1, mine, other, block):
    rows, cols = g.shape
    n, width = own.shape
    f = mine.shape[1]
    steps = 2
    whole = lambda size: pl.BlockSpec((size,), lambda i: (0,))
    strip = lambda size, lanes: pl.BlockSpec((size // steps, lanes), lambda i: (i, 0))
    ffn_in = pl.BlockSpec((2, f // steps, width), lambda i: (0, i, 0))
    return pl.pallas_call(
        finish_body, grid=(steps,),
        out_shape=(sds((rows, 3 * width), F32), sds((rows, width), F32), sds((width,), F32), sds((width,), F32),
                   sds((64,), F32), sds((64,), F32), sds((width,), F32), sds((width,), F32),
                   sds((n, width), F32), sds((f, width), F32), sds((f, width), F32), sds((n, width), BF16)),
        in_specs=[strip(rows, cols), pl.BlockSpec(small.shape, lambda i: (0, 0)), strip(n, width), strip(n, width),
                  strip(n, width), whole(width), ffn_in, ffn_in, strip(n, width)],
        out_specs=(strip(rows, 3 * width), strip(rows, width),
                   whole(width), whole(width), whole(64), whole(64), whole(width), whole(width),
                   strip(n, width), strip(f, width), strip(f, width), strip(n, width)),
        name="finish",
    )(g, small, own, gback, base, g1, mine, other, block)


def layer_body(n_seq, own, gy, seg, g1, b1, far_qkv, qg, kg, far_out, g2, b2, wup, wdown,
               far_block, far_base, far_gn, far_quarter, small, far_mine,
               rem, fq, fk, ones, swap, vecs, normed, kk, vv, qq, rq, rk, qaug, att, mid,
               sx, sg, wbuf, accin, accout, first, hid, gpre, blk, gs, prec,
               dk, pbuf, xin, wqkv, wout, out, base, gn_rem, quarter, mine,
               wsend, wrecv, asend, arecv, psend, precv, tsend, trecv, gsend, grecv, xsend, xrecv, lsem, osem):
    n, width = own.shape
    f = wup.shape[0]
    h = f // 2
    chips = n_seq // 2
    pairs = width // 128
    tiles = n // TILE
    core, place, right, left, partner = ring_places(n_seq)
    x = lax.axis_index("pos")
    right, left, partner, across = {"seq": right}, {"seq": left}, {"seq": partner}, {"pos": 1 - x}
    fetch = [pltpu.make_async_copy(far, near, lsem.at[i]) for i, (far, near) in
             enumerate(((far_qkv, wqkv), (far_out, wout)))]
    for c in fetch:
        c.start()
    early, late = pl.ds(0, 3 * width), pl.ds(3 * width, width)
    stores = [pltpu.make_async_copy(near, far, osem.at[i]) for i, (near, far) in enumerate((
        (out, far_block), (gn_rem, far_gn), (base, far_base), (mine, far_mine),
        (quarter.at[:, early], far_quarter.at[:, early]), (quarter.at[:, late], far_quarter.at[:, late])))]
    greet((right, left, partner, across))

    def slot(s, k, d):
        return pl.ds(pl.multiple_of((k * chips + s) * f + d * h, h), h)

    def w_copies(s, k):
        return [copy_to(wbuf.at[slot(s, k, d)] if s else (wdown if k else wup).at[pl.ds(d * h, h)],
                        wbuf.at[slot(s + 1, k, d)], wsend.at[d, k, s], wrecv.at[d, k, s],
                        left if d else right) for d in range(2)]

    def a_copies(s, k):
        rows = [pl.ds(d * h, h) for d in range(2)]
        return [copy_to(accout.at[s - 1, k, rows[d]], accin.at[s - 1, k, rows[d]], asend.at[d, k, s - 1],
                        arecv.at[d, k, s - 1], left if d else right) for d in range(2)]

    def w_step(i):
        s, k = i // 2 + 1, i % 2
        for c in w_copies(s - 1, k):
            c.wait_recv()
        if s < chips - 1:
            for c in w_copies(s, k):
                c.start()

    def r_step(j):
        s, k = j // 2 + 1, j % 2
        for c in a_copies(s, k):
            c.wait_recv()
        if s < chips - 1:
            accout[s, k] = (accout[s, k].astype(F32) + accin[s - 1, k].astype(F32)).astype(BF16)
            for c in a_copies(s + 1, k):
                c.start()

    def at_points(now, points, step):
        for when, item in points:
            @pl.when(now == when)
            def _():
                step(item)

    def t_copy(i):
        rows = pl.ds(i * TILE, TILE)
        return copy_to(own.at[rows], rem.at[rows], tsend.at[i], trecv.at[i], across)

    def s_copy(i):
        return copy_to(sx.at[pl.ds(i * TILE, TILE)], sx.at[pl.ds(n + i * TILE, TILE)], psend.at[3 + i],
                       precv.at[3 + i], partner)

    gy_copy = copy_to(gy, sg.at[pl.ds(n, n)], psend.at[0], precv.at[0], partner)
    parts = (copy_to(gs.at[pl.ds(n, n)], prec.at[1], psend.at[1], precv.at[1], partner),
             copy_to(blk.at[pl.ds(n, n)], prec.at[0], psend.at[2], precv.at[2], partner))

    for k in range(2):
        for c in w_copies(0, k):
            c.start()
    for i in range(tiles):
        t_copy(i).start()
    gy_copy.start()

    at = pl.multiple_of(x * n, n)
    labels = jnp.concatenate([seg[:, pl.ds(at, n)], seg[:, pl.ds(n - at, n)]], axis=1)
    lane = lax.broadcasted_iota(jnp.int32, (128, 2 * n), 0) % 64
    same = lane == labels
    keyed = jnp.where((lane >= 6) & (lane <= 8), 1.0, jnp.where(same & (lane < 6), 1.0, 0.0))
    fk[...] = keyed.T.astype(BF16)
    away = jnp.where((lane < 6) & jnp.logical_not(same), -BIG, 0.0)
    fq[...] = away[:, 0:n].T.astype(BF16)
    ra = lax.broadcasted_iota(jnp.int32, ones.shape, 0) // 64
    rb = lax.broadcasted_iota(jnp.int32, ones.shape, 1) // 64
    ones[...] = jnp.where(ra == rb, 1.0, 0.0).astype(BF16)
    swap[...] = jnp.where(ra[:128, :128] == rb[:128, :128], 0.0, 1.0).astype(BF16)
    for i, v in enumerate((g1, b1, g2, b2)):
        vecs[i:i + 1, :] = v[...].reshape(1, width)
    for i, v in enumerate((qg, kg)):
        r = v[...].reshape(1, 64)
        vecs[4 + i:5 + i, :] = jnp.concatenate([r] * (width // 64), axis=1)
    sg[0:n, :] = gy[...]
    wbuf[0:f, :] = wup[...]
    wbuf[chips * f:(chips + 1) * f, :] = wdown[...]
    cols = ones.shape[0]

    def project(xs, i, queries):
        rows = tile_of(i)
        low = (rows_norm(xs)[0] * vecs[0:1, :] + vecs[1:2, :]).astype(BF16)
        normed[:, rows] = low.T
        for block in range(0 if queries else width // cols, 3 * width // cols):
            raw = dot(low, wqkv[:, block * cols:(block + 1) * cols])
            part, a = divmod(block * cols, width)
            lanes = slice(a, a + cols)
            if part == 2:
                vv[rows, lanes] = raw.astype(BF16)
                continue
            centred = raw - group_sum(raw, ones[...]) * (1 / 64)
            scale = lax.rsqrt(group_sum(centred * centred, ones[...]) * (1 / 64) + EPS)
            dst, rdst = (qq, rq) if part == 0 else (kk, rk)
            dst[rows, lanes] = (centred * scale * vecs[4 + part:5 + part, lanes]).astype(BF16)
            rdst[rows, lanes] = scale

    def own_tile(i, c):
        project(own[tile_of(i), :].astype(F32), i, True)
        return c

    fetch[0].wait()
    lax.fori_loop(0, tiles, own_tile, 0)
    w_step(0)
    lane_t = lax.broadcasted_iota(jnp.int32, (TILE, 128), 1)
    low_t = lane_t < 64
    lane_n = lax.broadcasted_iota(jnp.int32, (n, 128), 1)
    low_n = lane_n < 64

    def attend(krows, size, add, after):
        low_k = lax.broadcasted_iota(jnp.int32, (size, 128), 1) < 64

        def pair(p, c):
            lanes = tile_of(p, 128)
            k, v, feat = kk[krows, lanes], vv[krows, lanes], fk[krows, :]
            one = jnp.ones_like(v)
            ks = (jnp.where(low_k, k, feat), jnp.where(low_k, feat, k))
            vs = (jnp.where(low_k, v, one), jnp.where(low_k, one, v))

            q, mask = qq[:, lanes], fq[...]
            for a in range(2):
                qa = jnp.where(low_n, q, mask) if a == 0 else jnp.where(low_n, mask, q)
                e = jnp.exp2(dot(qa, ks[a], NT) * (LOG2E / 8)).astype(BF16)
                o = dot(e, vs[a])
                to = slice(a * n, (a + 1) * n)
                blk[to, lanes] = blk[to, lanes] + o if add else o
            if after is not None:
                after(p)
            return c

        lax.fori_loop(0, pairs, pair, 0)

    attend(slice(0, n), n, False, lambda p: at_points(p, ((1, 1), (4, 2)), w_step))
    for i in range(tiles):
        t_copy(i).wait_recv()
        project(rem[i * TILE:(i + 1) * TILE, :].astype(F32), tiles + i, False)
        if i == 0:
            w_step(3)
        attend(slice(n + i * TILE, n + (i + 1) * TILE), TILE, True,
               lambda p: at_points(p, ((1, 5),) if i else ((5, 4),), w_step))

    def close(p, c):
        lanes = tile_of(p, 128)

        def tile(t, c):
            rows = tile_of(t)
            q, mask = qq[rows, lanes], fq[rows, :]
            res = [blk[pl.ds(pl.multiple_of(a * n + t * TILE, TILE), TILE), lanes] for a in range(2)]
            for a in range(2):
                qa = jnp.where(low_t, q, mask) if a == 0 else jnp.where(low_t, mask, q)
                shift = jnp.log(res[a]) * -8.0
                hi, lo = two(shift)
                lo2 = (shift - hi.astype(F32) - lo.astype(F32)).astype(BF16)
                s = 64 * (1 - a)
                qaug[p * 2 + a, rows, :] = jnp.where(
                    lane_t == s + 6, hi, jnp.where(lane_t == s + 7, lo, jnp.where(lane_t == s + 8, lo2, qa)))
            num = jnp.where(low_t, res[0], res[1])
            den = pltpu.roll(jnp.where(low_t, res[1], res[0]), 64, 1)
            att[rows, lanes] = (num / den).astype(BF16)
            return c

        lax.fori_loop(0, tiles, tile, 0)
        return c

    lax.fori_loop(0, pairs, close, 0)
    w_step(6)
    fetch[1].wait()
    for i in range(tiles):
        rows = slice(i * TILE, (i + 1) * TILE)
        m = own[rows, :].astype(F32) + dot(att[rows, :], wout[...])
        mid[rows, :] = m
        sx[rows, :] = (rows_norm(m)[0] * vecs[2:3, :] + vecs[3:4, :]).astype(BF16)
        s_copy(i).start()
    quad = chips // 2
    gy_copy.wait_recv()
    for j in range(tiles):
        s_copy(j).wait_recv()

    def feed(begin, span, lanes, turn, after):
        up = wbuf.at[begin:begin + span]
        down = wbuf.at[chips * f + begin:chips * f + begin + span]

        def tile(i, c):
            rows = tile_of((i + turn) % (2 * tiles))
            acts, slopes = [], []
            for j in range(span // TILE):
                cs = slice(j * TILE, (j + 1) * TILE)
                to = slice(lanes + j * TILE, lanes + (j + 1) * TILE)
                pre = dot(sx[rows, :], up[cs, :], NT)
                gh = dot(sg[rows, :], down[cs, :], NT)
                cdf = 0.5 + 0.5 * lax.erf(pre * 0.7071067811865476)
                slope = cdf + pre * (jnp.exp(-0.5 * pre * pre) * 0.3989422804014327)
                acts.append((pre * cdf).astype(BF16))
                slopes.append((gh * slope).astype(BF16))
                hid[rows, to] = acts[-1]
                gpre[rows, to] = slopes[-1]
            o = dot(jnp.concatenate(acts, 1), down[...])
            t = dot(jnp.concatenate(slopes, 1), up[...])
            blk[rows, :] = blk[rows, :] + o if begin else o
            gs[rows, :] = gs[rows, :] + t if begin else t
            after(i)
            return c

        lax.fori_loop(0, 2 * tiles, tile, 0)

    def outer(g):
        def block(j, c):
            for k, (lhs, rhs) in enumerate(((gpre, sx), (hid, sg))):
                part = dot(lhs[:, pl.ds(pl.multiple_of(j * 2 * f, 2 * f), 2 * f)], rhs[...], TN)
                for m in range(2):
                    one = part[m * f:(m + 1) * f]
                    at = g * quad + 2 * j + m

                    @pl.when(at == 0)
                    def _():
                        first[k] = one

                    @pl.when(at > 0)
                    def _():
                        accout[jnp.maximum(at - 1, 0), k] = one.astype(BF16)
            return c

        lax.fori_loop(0, quad // 2, block, 0)

    half_way = quad * f
    last = 2 * quad * f - TILE
    feed(0, half_way, 0, 0, lambda i: at_points(i, ((0, 7), (1, 8), (3, 9)), w_step))
    outer(0)
    w_step(10)
    w_step(11)
    for k in range(2):
        for c in a_copies(1, k):
            c.start()
    feed(half_way, last - half_way, 0, tiles, lambda i: None)
    w_step(12)
    w_step(13)

    def send_parts(i):
        @pl.when(i == tiles - 1)
        def _():
            for c in parts:
                c.start()

    feed(last, TILE, last - half_way, tiles, send_parts)
    r_step(0)
    outer(1)

    for j in range(chips - 1):
        for k in range(2):
            for c in w_copies(j, k):
                c.wait_send()
    for i in range(tiles):
        s_copy(i).wait_send()
    gbr, gat = sx.at[0:n], sx.at[n:2 * n]
    small[...] = jnp.zeros_like(small)
    parts[0].wait_recv()

    def mid_tile(i, c):
        rows = tile_of(i)
        xh, r = rows_norm(mid[rows, :])
        dy = gs[rows, :] + prec[1, rows, :]
        small[2:3, :] += jnp.sum(dy * xh, axis=0, keepdims=True)
        small[3:4, :] += jnp.sum(dy, axis=0, keepdims=True)
        gd = dy * vecs[2:3, :]
        dx = r * (gd - jnp.mean(gd, -1, keepdims=True) - xh * jnp.mean(gd * xh, -1, keepdims=True))
        gm = gy[rows, :].astype(F32) + dx
        base[rows, :] = gm
        low = gm.astype(BF16)
        gbr[rows, :] = low
        gat[rows, :] = dot(low, wout[...], NT).astype(BF16)
        return c

    lax.fori_loop(0, tiles, mid_tile, 0)
    r_step(1)
    parts[1].wait_recv()
    out[...] = (mid[...] + (blk[0:n, :] + prec[0])).astype(BF16)
    stores[0].start()

    groups = (hid, gpre, sg, kk)
    hr, qr = width // 2, width // 4

    def g_copy(j):
        return copy_to(groups[j].at[pl.ds(pl.multiple_of((1 - core) * hr, hr), hr)], pbuf.at[j], gsend.at[j],
                       grecv.at[j], partner)

    def x_copy(j):
        return copy_to(groups[j].at[pl.ds(width, qr)], xin.at[j], xsend.at[j], xrecv.at[j], across)

    def chip_sum(j, side):
        return (groups[j][pl.ds(pl.multiple_of(core * hr + side * qr, qr), qr), :].astype(F32)
                + pbuf[j, pl.ds(pl.multiple_of(side * qr, qr), qr), :].astype(F32))

    def middle_sum(j):
        g_copy(j).wait_recv()
        groups[j][width:width + qr, :] = chip_sum(j, 1 - x).astype(BF16)
        x_copy(j).start()

    def last_sum(j):
        x_copy(j).wait_recv()
        quarter[:, j * width:(j + 1) * width] = (chip_sum(j, x) + xin[j].astype(F32)).astype(BF16)

    def proj_tile(i, c):
        rows = tile_of(i)
        hid[rows, :] = dot(att[:, rows], gbr[...], TN).astype(BF16)
        return c

    lax.fori_loop(0, width // TILE, proj_tile, 0)
    g_copy(0).start()

    def qkv_group(j, points):
        lanes = slice((j - 1) * TILE, j * TILE)

        def tile(i, c):
            rows = tile_of(i)
            for part, (at, size) in enumerate(((0, n), (2 * n, 2 * n), (4 * n, 2 * n))):
                groups[j][rows, part * TILE:(part + 1) * TILE] = dot(
                    normed[rows, 0:size], wbuf[at:at + size, lanes]).astype(BF16)
            at_points(i, points, r_step)
            return c

        lax.fori_loop(0, width // TILE, tile, 0)
        g_copy(j).start()

    def keys_of(j, rows):
        return wbuf.at[pl.ds(pl.multiple_of(j * 2 * n + rows, TILE), TILE)]

    def mix(part, rows):
        return pl.ds(part * 2 * n + rows.start, rows.size)

    ones_p = slice(0, 128)

    def norm_back(dy, y, r, gain):
        group = ones[ones_p, ones_p]
        dy = dy * 0.125
        y = y.astype(F32)
        prod = dy * y
        gd = dy * gain
        m1 = group_sum(gd, group) * (1 / 64)
        m2 = group_sum(prod, group) * (1 / 64)
        inv = 1.0 / gain
        return r * (gd - m1 - y * inv * m2), jnp.sum(prod, 0, keepdims=True) * inv

    def pair(p, c):
        at_points(p, ((1, 3), (2, 5), (3, 6), (4, 8), (5, 9)), r_step)
        at_points(p, ((1, 0),), middle_sum)
        at_points(p, ((3, 0), (5, 1)), last_sum)
        lanes = tile_of(p, 128)
        do = gat[:, lanes]
        delta = -group_sum(do.astype(F32) * att[:, lanes].astype(F32), swap[...])
        hi, lo = two(delta)
        zero = jnp.zeros_like(do)
        das = []
        for a in range(2):
            s = 64 * (1 - a)
            extra = jnp.where(lane_n == s, hi, jnp.where(lane_n == s + 1, lo, zero))
            das.append(jnp.where(low_n, do, extra) if a == 0 else jnp.where(low_n, extra, do))

        acc = [None, None]
        for t in range(2):
            if t:
                at_points(p, ((0, 2),), r_step)
                at_points(p, ((2, 1), (4, 2)), middle_sum)
            rows = slice(t * n, (t + 1) * n)
            k, v, feat = kk[rows, lanes], vv[rows, lanes], fk[rows, :]
            one = jnp.ones_like(v)
            dks, dvs = [], []
            for a in range(2):
                ka = jnp.where(low_n, k, feat) if a == 0 else jnp.where(low_n, feat, k)
                va = jnp.where(low_n, v, one) if a == 0 else jnp.where(low_n, one, v)
                qa = qaug[p * 2 + a]
                e = jnp.exp2(dot(ka, qa, NT) * (LOG2E / 8))
                ds = (e * dot(va, das[a], NT)).astype(BF16)
                dvs.append(dot(e.astype(BF16), das[a]))
                dks.append(dot(ds, qa))
                dq = dot(ka, ds, TN)
                acc[a] = dq if t == 0 else acc[a] + dq
            dk[rows, :] = jnp.where(low_n, dks[0], dks[1])
            wbuf[4 * n + t * n:4 * n + (t + 1) * n, lanes] = jnp.where(low_n, dvs[0], dvs[1]).astype(BF16)
        low_s = lax.broadcasted_iota(jnp.int32, (128, n), 0) < 64
        dq = jnp.where(low_s, acc[0], acc[1]).T
        qa = jnp.where(low_n, qaug[p * 2], qaug[p * 2 + 1])
        dx, gg = norm_back(dq, qa, rq[:, lanes], vecs[4:5, lanes])
        wbuf[0:n, lanes] = dx.astype(BF16)
        small[4:5, lanes] = gg
        dx, gg = norm_back(dk[...], kk[:, lanes], rk[:, lanes], vecs[5:6, lanes])
        wbuf[2 * n:4 * n, lanes] = dx.astype(BF16)
        small[5:6, lanes] = gg
        at_points(p, ((1, 4), (3, 7), (5, 10)), r_step)
        at_points(p, ((1, 1), (3, 2)), lambda j: qkv_group(j, ()))
        return c

    lax.fori_loop(0, pairs, pair, 0)
    qkv_group(3, ((1, 11),))

    def gain_sums(xh, gn):
        small[0:1, :] += jnp.sum(gn * xh, axis=0, keepdims=True)
        small[1:2, :] += jnp.sum(gn, axis=0, keepdims=True)

    def rem_tile(i, c):
        rows = tile_of(i)
        gn = (dot(wbuf[pl.ds(pl.multiple_of(3 * n + i * TILE, TILE), TILE), :], wqkv[:, width:2 * width], NT)
              + dot(wbuf[pl.ds(pl.multiple_of(5 * n + i * TILE, TILE), TILE), :], wqkv[:, 2 * width:], NT))
        gn_rem[rows, :] = gn.astype(BF16)
        gain_sums(rows_norm(rem[rows, :].astype(F32))[0], gn)
        at_points(i, ((0, 3),), middle_sum)
        return c

    def own_back(i, c):
        rows = tile_of(i)
        gn = (dot(wbuf[rows, :], wqkv[:, 0:width], NT)
              + dot(wbuf[pl.ds(pl.multiple_of(2 * n + i * TILE, TILE), TILE), :], wqkv[:, width:2 * width], NT)
              + dot(wbuf[pl.ds(pl.multiple_of(4 * n + i * TILE, TILE), TILE), :], wqkv[:, 2 * width:], NT))
        xh, r = rows_norm(own[rows, :].astype(F32))
        gain_sums(xh, gn)
        gd = gn * vecs[0:1, :]
        base[rows, :] += r * (gd - jnp.mean(gd, -1, keepdims=True) - xh * jnp.mean(gd * xh, -1, keepdims=True))
        return c

    lax.fori_loop(0, tiles, rem_tile, 0)
    stores[1].start()
    r_step(12)
    last_sum(2)
    stores[4].start()
    lax.fori_loop(0, tiles, own_back, 0)
    stores[2].start()
    r_step(13)
    mine[...] = (first[...] + accin[chips - 2].astype(F32)).astype(BF16)
    stores[3].start()
    for j in range(1, chips):
        for k in range(2):
            for c in a_copies(j, k):
                c.wait_send()
    for i in range(tiles):
        t_copy(i).wait_send()
    last_sum(3)
    stores[5].start()
    for c in stores:
        c.wait()
    for j in range(4):
        g_copy(j).wait_send()
        x_copy(j).wait_send()
    for c in (gy_copy,) + parts:
        c.wait_send()


def layer_call(n_seq, own, gy, seg, g1, b1, wqkv, qg, kg, wout, g2, b2, wup, wdown):
    n, width = own.shape
    f = wup.shape[0]
    chips = n_seq // 2
    heads = width // 64
    tiles = n // TILE
    V, D = pltpu.VMEM, pltpu.SemaphoreType.DMA
    return pl.pallas_call(
        functools.partial(layer_body, n_seq),
        out_shape=(sds((n, width), BF16), sds((n, width), F32), sds((n, width), BF16),
                   sds((width // 4, 4 * width), BF16), sds((8, width), F32), sds((2, f, width), BF16)),
        in_specs=[VM] * 5 + [pl.BlockSpec(memory_space=pl.ANY), VM, VM, pl.BlockSpec(memory_space=pl.ANY)] + [VM] * 4,
        out_specs=(pl.BlockSpec(memory_space=pl.ANY),) * 4 + (VM, pl.BlockSpec(memory_space=pl.ANY)),
        scratch_shapes=[
            V((n, width), BF16), V((n, 128), BF16), V((2 * n, 128), BF16), V((256, 256), BF16), V((128, 128), BF16),
            V((8, width), F32), V((width, 2 * n), BF16), V((2 * n, width), BF16), V((2 * n, width), BF16),
            V((n, width), BF16), V((n, width), F32), V((2 * n, width), F32), V((heads, n, 128), BF16),
            V((n, width), BF16), V((n, width), F32),
            V((2 * n, width), BF16), V((2 * n, width), BF16), V((chips * 2 * f, width), BF16),
            V((chips - 1, 2, f, width), BF16), V((chips - 1, 2, f, width), BF16), V((2, f, width), F32),
            V((2 * n, chips // 2 * f), BF16), V((2 * n, chips // 2 * f), BF16), V((2 * n, width), F32), V((2 * n, width), F32),
            V((2, n, width), F32),
            V((2 * n, 128), F32), V((4, width // 2, width), BF16), V((4, width // 4, width), BF16),
            V(wqkv.shape, BF16), V(wout.shape, BF16),
            V((n, width), BF16), V((n, width), F32), V((n, width), BF16), V((width // 4, 4 * width), BF16),
            V((2, f, width), BF16),
            D((2, 2, chips - 1)), D((2, 2, chips - 1)), D((2, 2, chips - 1)), D((2, 2, chips - 1)),
            D((3 + tiles,)), D((3 + tiles,)), D((tiles,)), D((tiles,)),
            D((4,)), D((4,)), D((4,)), D((4,)), D((2,)), D((6,))],
        compiler_params=pltpu.CompilerParams(
            vmem_limit_bytes=66 * 1000 * 1000, collective_id=1, has_side_effects=True),
        name="layer",
    )(own, gy, seg, g1, b1, wqkv, qg, kg, wout, g2, b2, wup, wdown)


def local_one(tokens, segment_ids, first_gain, first_bias, w_qkv, query_gain, key_gain, w_out,
              second_gain, second_bias, w_up, w_down, out_grad):
    n_seq = lax.axis_size("seq")
    own = tokens[0]
    block_out, base, gn_rem, quarter, small, mine = layer_call(
        n_seq, own, out_grad[0], segment_ids, first_gain, first_bias, w_qkv, query_gain, key_gain, w_out,
        second_gain, second_bias, w_up.T, w_down.T)
    g, small, gback, other = sum_call(n_seq, quarter, small, gn_rem, mine)
    qkv, proj, fg, fb, qgg, kgg, sgg, sbg, input_grad, up_grad, down_grad, block_out = finish_call(
        g, small, own, gback, base, first_gain, mine, other, block_out)
    return (block_out[None], input_grad[None], fg, fb, qkv, qgg, kgg, proj, sgg, sbg, up_grad.T, down_grad.T)


def layer_norm(rows, gain, shift):
    average = jnp.mean(rows, axis=-1, keepdims=True)
    centred = rows - average
    spread = jnp.mean(centred * centred, axis=-1, keepdims=True)
    return centred * lax.rsqrt(spread + EPS) * gain + shift


def head_norm(values, gain):
    average = jnp.mean(values, axis=-1, keepdims=True)
    centred = values - average
    spread = jnp.mean(centred * centred, axis=-1, keepdims=True)
    return centred * lax.rsqrt(spread + EPS) * gain


def qk_norms(raw_query, raw_keys, query_gain, key_gain):
    return (head_norm(raw_query, query_gain), head_norm(raw_keys, key_gain))


def gelu_exact(values):
    return jax.nn.gelu(values, approximate=False)


def gelu_back(pre, upstream):
    return jax.vjp(gelu_exact, pre)[1](upstream)[0]


def group_size(count, length):
    for option in range(1, count + 1):
        if count % option == 0 and option * length >= 512:
            return option
    return count


def rows_product(left, right):
    return lax.dot_general(
        left, right, (((0,), (0,)), ((), ())), preferred_element_type=jnp.float32
    )


def cols_product(left, right):
    return lax.dot_general(
        left, right, (((1,), (1,)), ((), ())), preferred_element_type=jnp.float32
    )


def local(
    tokens,
    segment_ids,
    first_gain,
    first_bias,
    w_qkv,
    query_gain,
    key_gain,
    w_out,
    second_gain,
    second_bias,
    w_up,
    w_down,
    out_grad,
):
    seqs_here, local_len, width = tokens.shape
    full_len = segment_ids.shape[1]
    head_dim = query_gain.shape[0]
    heads = width // head_dim
    rows_here = seqs_here * local_len
    scale = head_dim ** (-0.5)
    offset = lax.axis_index("pos") * local_len
    query_marks = lax.dynamic_slice_in_dim(segment_ids, offset, local_len, 1)
    block = group_size(seqs_here, local_len)
    count_blocks = seqs_here // block

    def split(array):
        return array.reshape((count_blocks, block) + array.shape[1:])

    inputs = tokens.astype(jnp.float32).reshape(rows_here, width)
    normed_low = layer_norm(inputs, first_gain, first_bias).astype(jnp.bfloat16)
    mixed = jnp.dot(normed_low, w_qkv, preferred_element_type=jnp.float32).reshape(
        rows_here, 3, heads, head_dim
    )
    raw_query = mixed[:, 0]
    raw_keys = mixed[:, 1]
    query = (
        head_norm(raw_query, query_gain)
        .astype(jnp.bfloat16)
        .reshape(seqs_here, local_len, heads, head_dim)
    )
    keys_local = (
        head_norm(raw_keys, key_gain).astype(jnp.bfloat16).reshape(seqs_here, local_len, width)
    )
    values_local = mixed[:, 2].astype(jnp.bfloat16).reshape(seqs_here, local_len, width)
    keys_all, values_all = (
        lax.all_gather(keys_local, "pos", axis=1, tiled=True),
        lax.all_gather(values_local, "pos", axis=1, tiled=True),
    )
    keys_four = keys_all.reshape(seqs_here, full_len, heads, head_dim)
    values_four = values_all.reshape(seqs_here, full_len, heads, head_dim)

    def scores_for(query_blk, keys_blk, query_lab, key_lab):
        raw = (
            jnp.einsum("bqhd,bkhd->bhqk", query_blk, keys_blk, preferred_element_type=jnp.float32)
            * scale
        )
        allowed = (query_lab[:, :, None] == key_lab[:, None, :])[:, None]
        return jnp.where(allowed, raw, -1e30)

    def forward_block(packed):
        query_blk, keys_blk, values_blk, query_lab, key_lab = packed
        scores = scores_for(query_blk, keys_blk, query_lab, key_lab)
        peak = jnp.max(scores, axis=-1, keepdims=True)
        expd = jnp.exp(scores - peak)
        totals = jnp.sum(expd, axis=-1, keepdims=True)
        probs = (expd / totals).astype(jnp.bfloat16)
        result = jnp.einsum(
            "bhqk,bkhd->bqhd", probs, values_blk, preferred_element_type=jnp.float32
        )
        return (result, peak + jnp.log(totals))

    attended, log_totals = lax.map(
        forward_block,
        (
            split(query),
            split(keys_four),
            split(values_four),
            split(query_marks),
            split(segment_ids),
        ),
    )
    attended_low = attended.astype(jnp.bfloat16).reshape(rows_here, width)
    middle = inputs + jnp.dot(attended_low, w_out, preferred_element_type=jnp.float32)
    second_low = layer_norm(middle, second_gain, second_bias).astype(jnp.bfloat16)
    grad_out = out_grad.reshape(rows_here, width)
    grad_float = grad_out.astype(jnp.float32)
    up_all, down_all = (
        lax.all_gather(w_up, "seq", axis=1, tiled=True),
        lax.all_gather(w_down, "seq", axis=1, tiled=True),
    )
    pre = jnp.dot(second_low, up_all, preferred_element_type=jnp.float32)
    hidden = gelu_exact(pre).astype(jnp.bfloat16)
    block_out = (middle + cols_product(hidden, down_all)).astype(jnp.bfloat16)
    grad_hidden = jnp.dot(grad_out, down_all, preferred_element_type=jnp.float32)
    grad_pre = gelu_back(pre, grad_hidden).astype(jnp.bfloat16)
    down_full = rows_product(grad_out, hidden)
    up_full = rows_product(second_low, grad_pre)
    grad_second = cols_product(grad_pre, up_all)
    up_part, down_part = (
        lax.psum_scatter(
            up_full.astype(jnp.bfloat16), "seq", scatter_dimension=1, tiled=True
        ).astype(jnp.float32),
        lax.psum_scatter(
            down_full.astype(jnp.bfloat16), "seq", scatter_dimension=1, tiled=True
        ).astype(jnp.float32),
    )
    up_grad, down_grad = (
        lax.psum(up_part.astype(jnp.bfloat16), "pos").astype(jnp.float32),
        lax.psum(down_part.astype(jnp.bfloat16), "pos").astype(jnp.float32),
    )
    second_back = jax.vjp(layer_norm, middle, second_gain, second_bias)[1]
    grad_middle_part, second_gain_part, second_bias_part = second_back(grad_second)
    grad_middle = grad_float + grad_middle_part
    grad_branch = grad_middle.astype(jnp.bfloat16)
    proj_part = rows_product(attended_low, grad_branch)
    grad_attended = (
        cols_product(grad_branch, w_out)
        .astype(jnp.bfloat16)
        .reshape(seqs_here, local_len, heads, head_dim)
    )

    def backward_block(packed):
        query_blk, keys_blk, values_blk, query_lab, key_lab, log_blk, grad_blk = packed
        scores = scores_for(query_blk, keys_blk, query_lab, key_lab)
        probs = jnp.exp(scores - log_blk)
        grad_probs = jnp.einsum(
            "bqhd,bkhd->bhqk", grad_blk, values_blk, preferred_element_type=jnp.float32
        )
        grad_values = jnp.einsum(
            "bhqk,bqhd->bkhd",
            probs.astype(jnp.bfloat16),
            grad_blk,
            preferred_element_type=jnp.float32,
        )
        inner = jnp.sum(probs * grad_probs, axis=-1, keepdims=True)
        grad_scores = (probs * (grad_probs - inner) * scale).astype(jnp.bfloat16)
        grad_query = jnp.einsum(
            "bhqk,bkhd->bqhd", grad_scores, keys_blk, preferred_element_type=jnp.float32
        )
        grad_keys = jnp.einsum(
            "bhqk,bqhd->bkhd", grad_scores, query_blk, preferred_element_type=jnp.float32
        )
        return (grad_query, grad_keys, grad_values)

    grad_query, grad_keys, grad_values = lax.map(
        backward_block,
        (
            split(query),
            split(keys_four),
            split(values_four),
            split(query_marks),
            split(segment_ids),
            log_totals,
            split(grad_attended),
        ),
    )
    grad_keys = grad_keys.reshape(seqs_here, full_len, width)
    grad_values = grad_values.reshape(seqs_here, full_len, width)
    keys_grad, values_grad = (
        lax.psum_scatter(
            grad_keys.astype(jnp.bfloat16), "pos", scatter_dimension=1, tiled=True
        ).astype(jnp.float32),
        lax.psum_scatter(
            grad_values.astype(jnp.bfloat16), "pos", scatter_dimension=1, tiled=True
        ).astype(jnp.float32),
    )
    norm_back = jax.vjp(qk_norms, raw_query, raw_keys, query_gain, key_gain)[1]
    grad_raw_query, grad_raw_keys, query_gain_part, key_gain_part = norm_back(
        (
            grad_query.reshape(rows_here, heads, head_dim),
            keys_grad.reshape(rows_here, heads, head_dim),
        )
    )
    grad_mixed = (
        jnp.stack(
            [grad_raw_query, grad_raw_keys, values_grad.reshape(rows_here, heads, head_dim)], axis=1
        )
        .reshape(rows_here, 3 * width)
        .astype(jnp.bfloat16)
    )
    qkv_part = rows_product(normed_low, grad_mixed)
    grad_normed = cols_product(grad_mixed, w_qkv)
    first_back = jax.vjp(layer_norm, inputs, first_gain, first_bias)[1]
    grad_input_part, first_gain_part, first_bias_part = first_back(grad_normed)
    input_grad = (grad_middle + grad_input_part).reshape(seqs_here, local_len, width)
    (
        qkv_grad,
        proj_grad,
        first_gain_grad,
        first_bias_grad,
        query_gain_grad,
        key_gain_grad,
        second_gain_grad,
        second_bias_grad,
    ) = lax.psum(
        (
            qkv_part,
            proj_part,
            first_gain_part,
            first_bias_part,
            query_gain_part,
            key_gain_part,
            second_gain_part,
            second_bias_part,
        ),
        ("pos", "seq"),
    )
    return (
        block_out.reshape(seqs_here, local_len, width),
        input_grad,
        first_gain_grad,
        first_bias_grad,
        qkv_grad,
        query_gain_grad,
        key_gain_grad,
        proj_grad,
        second_gain_grad,
        second_bias_grad,
        up_grad,
        down_grad,
    )


def solution(mesh):
    placed = (P("seq", "pos", None), P("seq", None), P(), P(), P(), P(), P(), P(), P(), P(),
              P(None, "seq"), P(None, "seq"), P("seq", "pos", None))
    outs = (P("seq", "pos", None), P("seq", "pos", None), P(), P(), P(), P(), P(), P(), P(), P(),
            P(None, "seq"), P(None, "seq"))

    def step(*args):
        def run(*local_args):
            one = local_args[0].shape[:2] == (1, 512) and (mesh.shape["pos"], mesh.shape["seq"]) == (2, 16)
            return (local_one if one else local)(*local_args)

        return jax.shard_map(run, mesh=mesh, in_specs=placed, out_specs=outs, check_vma=False)(*args)

    return step
```

```python
import functools
import jax
import jax.numpy as jnp
from jax import lax
from jax.experimental import pallas as pl
from jax.experimental.pallas import tpu as pltpu
from jax.sharding import PartitionSpec as P

EPS = 1e-06
F32 = jnp.float32
BF16 = jnp.bfloat16
LOG2E = 1.4426950408889634
BIG = 16384.0
TILE = 256
NT = (((1,), (1,)), ((), ()))
NN = (((1,), (0,)), ((), ()))
TN = (((0,), (0,)), ((), ()))


def dot(a, b, dims=NN):
    return lax.dot_general(a, b, dims, preferred_element_type=F32)


def two(x):
    hi = x.astype(BF16)
    return hi, (x - hi.astype(F32)).astype(BF16)


def group_sum(x, ones):
    hi, lo = two(x)
    return dot(hi, ones) + dot(lo, ones)


def rows_norm(x):
    average = jnp.mean(x, axis=-1, keepdims=True)
    centred = x - average
    spread = jnp.mean(centred * centred, axis=-1, keepdims=True)
    scale = lax.rsqrt(spread + EPS)
    return centred * scale, scale


def tile_of(i, size=TILE):
    return pl.ds(pl.multiple_of(i * size, size), size)


VM = pl.BlockSpec(memory_space=pltpu.VMEM)
LIMIT = 60 * 1024 * 1024


def sds(shape, dtype):
    return jax.ShapeDtypeStruct(shape, dtype)


def ring_places(n_seq):
    s = lax.axis_index("seq")
    core, chip = s % 2, s // 2
    chips = n_seq // 2
    half = chips // 2
    odd = chip % 2
    place = (1 - odd) * (chip // 2) + odd * (chips - 1 - chip // 2)

    def device(p):
        far = p // half
        return ((1 - far) * 2 * p + far * (2 * (chips - 1 - p) + 1)) * 2 + core

    right = device((place + 1) % chips)
    left = device((place + chips - 1) % chips)
    return core, place, right, left, s + 1 - 2 * core


def copy_to(src, dst, send, recv, target):
    return pltpu.make_async_remote_copy(
        src_ref=src, dst_ref=dst, send_sem=send, recv_sem=recv, device_id=target,
        device_id_type=pl.DeviceIdType.MESH)


def greet(targets):
    barrier = pltpu.get_barrier_semaphore()
    for t in targets:
        pl.semaphore_signal(barrier, inc=1, device_id=t, device_id_type=pl.DeviceIdType.MESH)
    pl.semaphore_wait(barrier, len(targets))


def sum_body(n_seq, quarter, small, gn_rem, mine, far_fin, sout, gback, other,
             fin, accin, accout, srec, sring,
             asend, arecv, xsend, xrecv, fsend, frecv, qsend, qrecv, ssend, srecv, gsend, grecv, osem):
    qrows, cols = quarter.shape
    chips = n_seq // 2
    cw, pr, hr = cols // chips, qrows // 4, qrows // 2
    core, place, right, left, partner = ring_places(n_seq)
    x = lax.axis_index("pos")
    right, left, partner, across = {"seq": right}, {"seq": left}, {"seq": partner}, {"pos": 1 - x}
    greet((right, left, partner, across))

    def chunk(p):
        return (p + 2 * chips) % chips

    def lanes_of(p):
        return pl.ds(pl.multiple_of(p * cw, cw), cw)

    def rows_of(c, o, d):
        side = 1 - x if o else x
        return pl.ds(pl.multiple_of(c * 2 * qrows + side * qrows + d * hr, hr), hr)

    half = chips // 2

    def a_copy(d, i, s):
        return copy_to(accout.at[s - 1, d, i], accin.at[s - 1, d, i], asend.at[s - 1, d, i], arecv.at[s - 1, d, i],
                       left if d else right)

    def x_piece(i, side, p):
        ref = fin.at[pl.ds(pl.multiple_of(core * 2 * qrows + side * qrows + i * pr, pr), pr), lanes_of(p)]
        return copy_to(ref, ref, xsend.at[i], xrecv.at[i], across)

    def ring_copy(d, o, e, s, p):
        ref = fin.at[rows_of(core, o, e), lanes_of(p)]
        return copy_to(ref, ref, fsend.at[s, d, o * 2 + e], frecv.at[s, d, o * 2 + e], left if d else right)

    def f_copy(d, o, e, s):
        return ring_copy(d, o, e, s, chunk(place + s) if d else chunk(place - s))

    def f_recv(d, o, e, s):
        return ring_copy(d, o, e, s, chunk(place + s + 1) if d else chunk(place - s - 1))

    def pair_copy(c, d, o, e, s):
        ref = fin.at[rows_of(c, o, e), lanes_of(chunk(place + s) if d else chunk(place - s))]
        return copy_to(ref, ref, qsend.at[s, d, o * 2 + e], qrecv.at[s, d, o * 2 + e], partner)

    def s_copy(s):
        return copy_to(sring.at[chunk(place - s)], sring.at[chunk(place - s)], ssend.at[s], srecv.at[s], right)

    def s_recv(s):
        p = chunk(place - s - 1)
        return copy_to(sring.at[p], sring.at[p], ssend.at[s], srecv.at[s], right)

    n = gn_rem.shape[0]
    backs = [copy_to(gn_rem.at[pl.ds(i * n // 2, n // 2)], gback.at[pl.ds(i * n // 2, n // 2)],
                     gsend.at[4 * i], grecv.at[4 * i], across) for i in range(2)]
    small_p = copy_to(small, srec.at[0], gsend.at[1], grecv.at[1], partner)
    small_x = copy_to(srec.at[1], srec.at[2], gsend.at[2], grecv.at[2], across)
    ffn_x = copy_to(mine, other, gsend.at[3], grecv.at[3], across)
    pieces = (0, 2, 1, 3)
    halves = [(o, e) for o in range(2) for e in range(2)]
    arrivals = [(d, o, e, s) for s in range(1, half + 1) for o, e in halves for d in range(2) if s < half or e == d]
    pairs = [(0, o, e, 0) for o, e in halves] + arrivals

    small_p.start()

    def part(i, q):
        return quarter[i * pr:(i + 1) * pr, lanes_of(q)].astype(F32)

    def reduce_piece(d, i, s, first):
        q = chunk(place - (half + 1 - s)) if d else chunk(place + (half + 1 - s))
        value = part(i, q)
        if not first:
            a_copy(d, i, s - 1).wait_recv()
            value = value + accin[s - 2, d, i].astype(F32)
        accout[s - 1, d, i] = value.astype(BF16)
        a_copy(d, i, s).start()

    hops = [(d, i, s) for s in range(1, half + 1) for i in (2, 3, 0, 1) for d in range(2)]
    hops = [(d, (i + 2 * d) % 4, s) for d, i, s in hops]
    hops = [(d, i, s) for d, i, s in hops if s > 1 or i // 2 == d]
    for d, i, s in hops:
        reduce_piece(d, i, s, s == (1 if i // 2 == d else 2))
        if (d, i, s) == hops[7]:
            backs[0].start()
            small_p.wait_recv()
            srec[1] = small[...] + srec[0]
            small_x.start()

    def own_start(o, e):
        for d in range(2):
            f_copy(d, o, e, 0).start()
        pair_copy(core, 0, o, e, 0).start()

    for i in pieces:
        total = part(i, place)
        for d in range(2):
            a_copy(d, i, half).wait_recv()
            total = total + accin[half - 1, d, i].astype(F32)
        at = pl.ds(pl.multiple_of(core * 2 * qrows + x * qrows + i * pr, pr), pr)
        fin[at, lanes_of(place)] = total.astype(BF16)
        x_piece(i, x, place).start()
        if i % 2:
            own_start(0, i // 2)
    backs[1].start()
    small_x.wait_recv()
    sring[place] = srec[1] + srec[2]
    s_copy(0).start()
    for i in pieces:
        x_piece(i, 1 - x, place).wait_recv()
        if i % 2:
            own_start(1, i // 2)
    ffn_x.start()

    def store(c, p):
        block = (pl.ds(pl.multiple_of(c * 2 * qrows, 2 * qrows), 2 * qrows), lanes_of(p))
        return pltpu.make_async_copy(fin.at[block], far_fin.at[block], osem.at[c, p])

    def store_hop(c, s):
        store(c, chunk(place - s)).start()
        if 0 < s < half:
            store(c, chunk(place + s)).start()

    store_hop(core, 0)
    for at, (d, o, e, s) in enumerate(arrivals):
        f_recv(d, o, e, s - 1).wait_recv()
        if s < half - 1 or (s == half - 1 and e == d):
            f_copy(d, o, e, s).start()
        pair_copy(core, d, o, e, s).start()
        if at + 1 == len(arrivals) or arrivals[at + 1][3] > s:
            store_hop(core, s)
        if at % 4 == 3:
            step = at // 4
            s_recv(step).wait_recv()
            if step < chips - 2:
                s_copy(step + 1).start()

    total = sring[0]
    for s in range(1, chips):
        total = total + sring[s]
    sout[...] = total
    for at, (d, o, e, s) in enumerate(pairs):
        pair_copy(1 - core, d, o, e, s).wait_recv()
        if at + 1 == len(pairs) or pairs[at + 1][3] > s:
            store_hop(1 - core, s)
    for c in backs + [ffn_x]:
        c.wait_recv()
    for d, o, e, s in pairs:
        pair_copy(core, d, o, e, s).wait_send()
    for d, o, e, s in arrivals:
        f_copy(d, o, e, s - 1).wait_send()
    for s in range(chips - 1):
        s_copy(s).wait_send()
    for i in pieces:
        x_piece(i, x, place).wait_send()
    for d, i, s in hops:
        a_copy(d, i, s).wait_send()
    for c in range(2):
        for p in range(chips):
            store(c, p).wait()
    for c in backs + [small_p, small_x, ffn_x]:
        c.wait_send()


def sum_call(n_seq, quarter, small, gn_rem, mine):
    qrows, cols = quarter.shape
    chips = n_seq // 2
    pr, cw = qrows // 4, cols // chips
    V, D = pltpu.VMEM, pltpu.SemaphoreType.DMA
    return pl.pallas_call(
        functools.partial(sum_body, n_seq),
        out_shape=(sds((4 * qrows, cols), BF16), sds(small.shape, F32), sds(gn_rem.shape, BF16),
                   sds(mine.shape, BF16)),
        in_specs=[VM, VM] + [pl.BlockSpec(memory_space=pl.ANY)] * 2,
        out_specs=(pl.BlockSpec(memory_space=pl.ANY), VM) + (pl.BlockSpec(memory_space=pl.ANY),) * 2,
        scratch_shapes=[
            V((4 * qrows, cols), BF16),
            V((chips // 2, 2, 4, pr, cw), BF16), V((chips // 2, 2, 4, pr, cw), BF16),
            V((3,) + small.shape, F32), V((chips,) + small.shape, F32),
            D((chips // 2, 2, 4)), D((chips // 2, 2, 4)), D((4,)), D((4,)),
            D((chips // 2, 2, 4)), D((chips // 2, 2, 4)), D((chips // 2 + 1, 2, 4)), D((chips // 2 + 1, 2, 4)),
            D((chips - 1,)), D((chips - 1,)), D((5,)), D((5,)), D((2, chips))],
        compiler_params=pltpu.CompilerParams(
            vmem_limit_bytes=LIMIT, collective_id=2, has_side_effects=True),
        name="sums",
    )(quarter, small, gn_rem, mine)


def finish_body(g, small, own, gback, base, g1, mine, other, block, qkv, proj, fg, fb, qgg, kgg, sgg, sbg,
                igrad, upg, downg, out):
    width = proj.shape[1]
    proj[...] = g[:, 0:width].astype(F32)
    for j in range(3):
        for part in range(3):
            at = (j + 1) * width + part * TILE
            qkv[:, part * width + j * TILE:part * width + (j + 1) * TILE] = g[:, at:at + TILE].astype(F32)
    xh, r = rows_norm(own[...].astype(F32))
    dy = gback[...].astype(F32) * g1[...].reshape(1, width)
    dx = r * (dy - jnp.mean(dy, -1, keepdims=True) - xh * jnp.mean(dy * xh, -1, keepdims=True))
    igrad[...] = base[...] + dx
    out[...] = block[...]

    total = mine[...].astype(F32) + other[...].astype(F32)
    upg[...] = total[0]
    downg[...] = total[1]

    @pl.when(pl.program_id(0) == 0)
    def _():
        for i, ref in enumerate((fg, fb, sgg, sbg)):
            ref[...] = small[i:i + 1, :].reshape(width)
        for i, ref in ((4, qgg), (5, kgg)):
            folded = small[i:i + 1, 0:128]
            for j in range(1, width // 128):
                folded = folded + small[i:i + 1, j * 128:(j + 1) * 128]
            folded = folded + pltpu.roll(folded, 64, 1)
            ref[...] = folded[:, 0:64].reshape(64)


def finish_call(g, small, own, gback, base, g1, mine, other, block):
    rows, cols = g.shape
    n, width = own.shape
    f = mine.shape[1]
    steps = 2
    whole = lambda size: pl.BlockSpec((size,), lambda i: (0,))
    strip = lambda size, lanes: pl.BlockSpec((size // steps, lanes), lambda i: (i, 0))
    ffn_in = pl.BlockSpec((2, f // steps, width), lambda i: (0, i, 0))
    return pl.pallas_call(
        finish_body, grid=(steps,),
        out_shape=(sds((rows, 3 * width), F32), sds((rows, width), F32), sds((width,), F32), sds((width,), F32),
                   sds((64,), F32), sds((64,), F32), sds((width,), F32), sds((width,), F32),
                   sds((n, width), F32), sds((f, width), F32), sds((f, width), F32), sds((n, width), BF16)),
        in_specs=[strip(rows, cols), pl.BlockSpec(small.shape, lambda i: (0, 0)), strip(n, width), strip(n, width),
                  strip(n, width), whole(width), ffn_in, ffn_in, strip(n, width)],
        out_specs=(strip(rows, 3 * width), strip(rows, width),
                   whole(width), whole(width), whole(64), whole(64), whole(width), whole(width),
                   strip(n, width), strip(f, width), strip(f, width), strip(n, width)),
        name="finish",
    )(g, small, own, gback, base, g1, mine, other, block)


def layer_body(n_seq, own, gy, seg, g1, b1, far_qkv, qg, kg, far_out, g2, b2, wup, wdown,
               far_block, far_base, far_gn, far_quarter, small, far_mine,
               rem, fq, fk, ones, swap, vecs, normed, kk, vv, qq, rq, rk, qaug, att, mid,
               sx, sg, wbuf, accin, accout, first, hid, gpre, blk, gs, prec,
               dk, pbuf, xin, wqkv, wout, out, base, gn_rem, quarter, mine,
               wsend, wrecv, asend, arecv, psend, precv, tsend, trecv, gsend, grecv, xsend, xrecv, lsem, osem):
    n, width = own.shape
    f = wup.shape[0]
    h = f // 2
    chips = n_seq // 2
    pairs = width // 128
    tiles = n // TILE
    core, place, right, left, partner = ring_places(n_seq)
    x = lax.axis_index("pos")
    right, left, partner, across = {"seq": right}, {"seq": left}, {"seq": partner}, {"pos": 1 - x}
    fetch = [pltpu.make_async_copy(far, near, lsem.at[i]) for i, (far, near) in
             enumerate(((far_qkv, wqkv), (far_out, wout)))]
    for c in fetch:
        c.start()
    early, late = pl.ds(0, 3 * width), pl.ds(3 * width, width)
    stores = [pltpu.make_async_copy(near, far, osem.at[i]) for i, (near, far) in enumerate((
        (out, far_block), (gn_rem, far_gn), (base, far_base), (mine, far_mine),
        (quarter.at[:, early], far_quarter.at[:, early]), (quarter.at[:, late], far_quarter.at[:, late])))]
    greet((right, left, partner, across))

    def slot(s, k, d):
        return pl.ds(pl.multiple_of((k * chips + s) * f + d * h, h), h)

    def w_copies(s, k):
        return [copy_to(wbuf.at[slot(s, k, d)] if s else (wdown if k else wup).at[pl.ds(d * h, h)],
                        wbuf.at[slot(s + 1, k, d)], wsend.at[d, k, s], wrecv.at[d, k, s],
                        left if d else right) for d in range(2)]

    def a_copies(s, k):
        rows = [pl.ds(d * h, h) for d in range(2)]
        return [copy_to(accout.at[s - 1, k, rows[d]], accin.at[s - 1, k, rows[d]], asend.at[d, k, s - 1],
                        arecv.at[d, k, s - 1], left if d else right) for d in range(2)]

    def w_step(i):
        s, k = i // 2 + 1, i % 2
        for c in w_copies(s - 1, k):
            c.wait_recv()
        if s < chips - 1:
            for c in w_copies(s, k):
                c.start()

    def r_step(j):
        s, k = j // 2 + 1, j % 2
        for c in a_copies(s, k):
            c.wait_recv()
        if s < chips - 1:
            accout[s, k] = (accout[s, k].astype(F32) + accin[s - 1, k].astype(F32)).astype(BF16)
            for c in a_copies(s + 1, k):
                c.start()

    def at_points(now, points, step):
        for when, item in points:
            @pl.when(now == when)
            def _():
                step(item)

    def t_copy(i):
        rows = pl.ds(i * TILE, TILE)
        return copy_to(own.at[rows], rem.at[rows], tsend.at[i], trecv.at[i], across)

    def s_copy(i):
        return copy_to(sx.at[pl.ds(i * TILE, TILE)], sx.at[pl.ds(n + i * TILE, TILE)], psend.at[3 + i],
                       precv.at[3 + i], partner)

    gy_copy = copy_to(gy, sg.at[pl.ds(n, n)], psend.at[0], precv.at[0], partner)
    parts = (copy_to(gs.at[pl.ds(n, n)], prec.at[1], psend.at[1], precv.at[1], partner),
             copy_to(blk.at[pl.ds(n, n)], prec.at[0], psend.at[2], precv.at[2], partner))

    for k in range(2):
        for c in w_copies(0, k):
            c.start()
    for i in range(tiles):
        t_copy(i).start()
    gy_copy.start()

    at = pl.multiple_of(x * n, n)
    labels = jnp.concatenate([seg[:, pl.ds(at, n)], seg[:, pl.ds(n - at, n)]], axis=1)
    lane = lax.broadcasted_iota(jnp.int32, (128, 2 * n), 0) % 64
    same = lane == labels
    keyed = jnp.where((lane >= 6) & (lane <= 8), 1.0, jnp.where(same & (lane < 6), 1.0, 0.0))
    fk[...] = keyed.T.astype(BF16)
    away = jnp.where((lane < 6) & jnp.logical_not(same), -BIG, 0.0)
    fq[...] = away[:, 0:n].T.astype(BF16)
    ra = lax.broadcasted_iota(jnp.int32, ones.shape, 0) // 64
    rb = lax.broadcasted_iota(jnp.int32, ones.shape, 1) // 64
    ones[...] = jnp.where(ra == rb, 1.0, 0.0).astype(BF16)
    swap[...] = jnp.where(ra[:128, :128] == rb[:128, :128], 0.0, 1.0).astype(BF16)
    for i, v in enumerate((g1, b1, g2, b2)):
        vecs[i:i + 1, :] = v[...].reshape(1, width)
    for i, v in enumerate((qg, kg)):
        r = v[...].reshape(1, 64)
        vecs[4 + i:5 + i, :] = jnp.concatenate([r] * (width // 64), axis=1)
    sg[0:n, :] = gy[...]
    wbuf[0:f, :] = wup[...]
    wbuf[chips * f:(chips + 1) * f, :] = wdown[...]
    cols = ones.shape[0]

    def project(xs, i, queries):
        rows = tile_of(i)
        low = (rows_norm(xs)[0] * vecs[0:1, :] + vecs[1:2, :]).astype(BF16)
        normed[:, rows] = low.T
        for block in range(0 if queries else width // cols, 3 * width // cols):
            raw = dot(low, wqkv[:, block * cols:(block + 1) * cols])
            part, a = divmod(block * cols, width)
            lanes = slice(a, a + cols)
            if part == 2:
                vv[rows, lanes] = raw.astype(BF16)
                continue
            centred = raw - group_sum(raw, ones[...]) * (1 / 64)
            scale = lax.rsqrt(group_sum(centred * centred, ones[...]) * (1 / 64) + EPS)
            dst, rdst = (qq, rq) if part == 0 else (kk, rk)
            dst[rows, lanes] = (centred * scale * vecs[4 + part:5 + part, lanes]).astype(BF16)
            rdst[rows, lanes] = scale

    def own_tile(i, c):
        project(own[tile_of(i), :].astype(F32), i, True)
        return c

    fetch[0].wait()
    lax.fori_loop(0, tiles, own_tile, 0)
    w_step(0)
    lane_t = lax.broadcasted_iota(jnp.int32, (TILE, 128), 1)
    low_t = lane_t < 64
    lane_n = lax.broadcasted_iota(jnp.int32, (n, 128), 1)
    low_n = lane_n < 64

    def attend(krows, size, add, after):
        low_k = lax.broadcasted_iota(jnp.int32, (size, 128), 1) < 64

        def pair(p, c):
            lanes = tile_of(p, 128)
            k, v, feat = kk[krows, lanes], vv[krows, lanes], fk[krows, :]
            one = jnp.ones_like(v)
            ks = (jnp.where(low_k, k, feat), jnp.where(low_k, feat, k))
            vs = (jnp.where(low_k, v, one), jnp.where(low_k, one, v))

            q, mask = qq[:, lanes], fq[...]
            for a in range(2):
                qa = jnp.where(low_n, q, mask) if a == 0 else jnp.where(low_n, mask, q)
                e = jnp.exp2(dot(qa, ks[a], NT) * (LOG2E / 8)).astype(BF16)
                o = dot(e, vs[a])
                to = slice(a * n, (a + 1) * n)
                blk[to, lanes] = blk[to, lanes] + o if add else o
            if after is not None:
                after(p)
            return c

        lax.fori_loop(0, pairs, pair, 0)

    attend(slice(0, n), n, False, lambda p: at_points(p, ((1, 1), (4, 2)), w_step))
    for i in range(tiles):
        t_copy(i).wait_recv()
        project(rem[i * TILE:(i + 1) * TILE, :].astype(F32), tiles + i, False)
        if i == 0:
            w_step(3)
        attend(slice(n + i * TILE, n + (i + 1) * TILE), TILE, True,
               lambda p: at_points(p, ((1, 5),) if i else ((5, 4),), w_step))

    def close(p, c):
        lanes = tile_of(p, 128)

        def tile(t, c):
            rows = tile_of(t)
            q, mask = qq[rows, lanes], fq[rows, :]
            res = [blk[pl.ds(pl.multiple_of(a * n + t * TILE, TILE), TILE), lanes] for a in range(2)]
            for a in range(2):
                qa = jnp.where(low_t, q, mask) if a == 0 else jnp.where(low_t, mask, q)
                shift = jnp.log(res[a]) * -8.0
                hi, lo = two(shift)
                lo2 = (shift - hi.astype(F32) - lo.astype(F32)).astype(BF16)
                s = 64 * (1 - a)
                qaug[p * 2 + a, rows, :] = jnp.where(
                    lane_t == s + 6, hi, jnp.where(lane_t == s + 7, lo, jnp.where(lane_t == s + 8, lo2, qa)))
            num = jnp.where(low_t, res[0], res[1])
            den = pltpu.roll(jnp.where(low_t, res[1], res[0]), 64, 1)
            att[rows, lanes] = (num / den).astype(BF16)
            return c

        lax.fori_loop(0, tiles, tile, 0)
        return c

    lax.fori_loop(0, pairs, close, 0)
    w_step(6)
    fetch[1].wait()
    for i in range(tiles):
        rows = slice(i * TILE, (i + 1) * TILE)
        m = own[rows, :].astype(F32) + dot(att[rows, :], wout[...])
        mid[rows, :] = m
        sx[rows, :] = (rows_norm(m)[0] * vecs[2:3, :] + vecs[3:4, :]).astype(BF16)
        s_copy(i).start()
    quad = chips // 2
    gy_copy.wait_recv()
    for j in range(tiles):
        s_copy(j).wait_recv()

    def feed(begin, span, lanes, turn, after):
        up = wbuf.at[begin:begin + span]
        down = wbuf.at[chips * f + begin:chips * f + begin + span]

        def tile(i, c):
            rows = tile_of((i + turn) % (2 * tiles))
            acts, slopes = [], []
            for j in range(span // TILE):
                cs = slice(j * TILE, (j + 1) * TILE)
                to = slice(lanes + j * TILE, lanes + (j + 1) * TILE)
                pre = dot(sx[rows, :], up[cs, :], NT)
                gh = dot(sg[rows, :], down[cs, :], NT)
                cdf = 0.5 + 0.5 * lax.erf(pre * 0.7071067811865476)
                slope = cdf + pre * (jnp.exp(-0.5 * pre * pre) * 0.3989422804014327)
                acts.append((pre * cdf).astype(BF16))
                slopes.append((gh * slope).astype(BF16))
                hid[rows, to] = acts[-1]
                gpre[rows, to] = slopes[-1]
            o = dot(jnp.concatenate(acts, 1), down[...])
            t = dot(jnp.concatenate(slopes, 1), up[...])
            blk[rows, :] = blk[rows, :] + o if begin else o
            gs[rows, :] = gs[rows, :] + t if begin else t
            after(i)
            return c

        lax.fori_loop(0, 2 * tiles, tile, 0)

    def outer(g):
        def block(j, c):
            for k, (lhs, rhs) in enumerate(((gpre, sx), (hid, sg))):
                part = dot(lhs[:, pl.ds(pl.multiple_of(j * 2 * f, 2 * f), 2 * f)], rhs[...], TN)
                for m in range(2):
                    one = part[m * f:(m + 1) * f]
                    at = g * quad + 2 * j + m

                    @pl.when(at == 0)
                    def _():
                        first[k] = one

                    @pl.when(at > 0)
                    def _():
                        accout[jnp.maximum(at - 1, 0), k] = one.astype(BF16)
            return c

        lax.fori_loop(0, quad // 2, block, 0)

    half_way = quad * f
    last = 2 * quad * f - TILE
    feed(0, half_way, 0, 0, lambda i: at_points(i, ((0, 7), (1, 8), (3, 9)), w_step))
    outer(0)
    w_step(10)
    w_step(11)
    for k in range(2):
        for c in a_copies(1, k):
            c.start()
    feed(half_way, last - half_way, 0, tiles, lambda i: None)
    w_step(12)
    w_step(13)

    def send_parts(i):
        @pl.when(i == tiles - 1)
        def _():
            for c in parts:
                c.start()

    feed(last, TILE, last - half_way, tiles, send_parts)
    r_step(0)
    outer(1)

    for j in range(chips - 1):
        for k in range(2):
            for c in w_copies(j, k):
                c.wait_send()
    for i in range(tiles):
        s_copy(i).wait_send()
    gbr, gat = sx.at[0:n], sx.at[n:2 * n]
    small[...] = jnp.zeros_like(small)
    parts[0].wait_recv()

    def mid_tile(i, c):
        rows = tile_of(i)
        xh, r = rows_norm(mid[rows, :])
        dy = gs[rows, :] + prec[1, rows, :]
        small[2:3, :] += jnp.sum(dy * xh, axis=0, keepdims=True)
        small[3:4, :] += jnp.sum(dy, axis=0, keepdims=True)
        gd = dy * vecs[2:3, :]
        dx = r * (gd - jnp.mean(gd, -1, keepdims=True) - xh * jnp.mean(gd * xh, -1, keepdims=True))
        gm = gy[rows, :].astype(F32) + dx
        base[rows, :] = gm
        low = gm.astype(BF16)
        gbr[rows, :] = low
        gat[rows, :] = dot(low, wout[...], NT).astype(BF16)
        return c

    lax.fori_loop(0, tiles, mid_tile, 0)
    r_step(1)
    parts[1].wait_recv()
    out[...] = (mid[...] + (blk[0:n, :] + prec[0])).astype(BF16)
    stores[0].start()

    groups = (hid, gpre, sg, kk)
    hr, qr = width // 2, width // 4

    def g_copy(j):
        return copy_to(groups[j].at[pl.ds(pl.multiple_of((1 - core) * hr, hr), hr)], pbuf.at[j], gsend.at[j],
                       grecv.at[j], partner)

    def x_copy(j):
        return copy_to(groups[j].at[pl.ds(width, qr)], xin.at[j], xsend.at[j], xrecv.at[j], across)

    def chip_sum(j, side):
        return (groups[j][pl.ds(pl.multiple_of(core * hr + side * qr, qr), qr), :].astype(F32)
                + pbuf[j, pl.ds(pl.multiple_of(side * qr, qr), qr), :].astype(F32))

    def middle_sum(j):
        g_copy(j).wait_recv()
        groups[j][width:width + qr, :] = chip_sum(j, 1 - x).astype(BF16)
        x_copy(j).start()

    def last_sum(j):
        x_copy(j).wait_recv()
        quarter[:, j * width:(j + 1) * width] = (chip_sum(j, x) + xin[j].astype(F32)).astype(BF16)

    def proj_tile(i, c):
        rows = tile_of(i)
        hid[rows, :] = dot(att[:, rows], gbr[...], TN).astype(BF16)
        return c

    lax.fori_loop(0, width // TILE, proj_tile, 0)
    g_copy(0).start()

    def qkv_group(j, points):
        lanes = slice((j - 1) * TILE, j * TILE)

        def tile(i, c):
            rows = tile_of(i)
            for part, (at, size) in enumerate(((0, n), (2 * n, 2 * n), (4 * n, 2 * n))):
                groups[j][rows, part * TILE:(part + 1) * TILE] = dot(
                    normed[rows, 0:size], wbuf[at:at + size, lanes]).astype(BF16)
            at_points(i, points, r_step)
            return c

        lax.fori_loop(0, width // TILE, tile, 0)
        g_copy(j).start()

    def keys_of(j, rows):
        return wbuf.at[pl.ds(pl.multiple_of(j * 2 * n + rows, TILE), TILE)]

    def mix(part, rows):
        return pl.ds(part * 2 * n + rows.start, rows.size)

    ones_p = slice(0, 128)

    def norm_back(dy, y, r, gain):
        group = ones[ones_p, ones_p]
        dy = dy * 0.125
        y = y.astype(F32)
        prod = dy * y
        gd = dy * gain
        m1 = group_sum(gd, group) * (1 / 64)
        m2 = group_sum(prod, group) * (1 / 64)
        inv = 1.0 / gain
        return r * (gd - m1 - y * inv * m2), jnp.sum(prod, 0, keepdims=True) * inv

    def pair(p, c):
        at_points(p, ((1, 3), (2, 5), (3, 6), (4, 8), (5, 9)), r_step)
        at_points(p, ((1, 0),), middle_sum)
        at_points(p, ((3, 0), (5, 1)), last_sum)
        lanes = tile_of(p, 128)
        do = gat[:, lanes]
        delta = -group_sum(do.astype(F32) * att[:, lanes].astype(F32), swap[...])
        hi, lo = two(delta)
        zero = jnp.zeros_like(do)
        das = []
        for a in range(2):
            s = 64 * (1 - a)
            extra = jnp.where(lane_n == s, hi, jnp.where(lane_n == s + 1, lo, zero))
            das.append(jnp.where(low_n, do, extra) if a == 0 else jnp.where(low_n, extra, do))

        acc = [None, None]
        for t in range(2):
            if t:
                at_points(p, ((0, 2),), r_step)
                at_points(p, ((2, 1), (4, 2)), middle_sum)
            rows = slice(t * n, (t + 1) * n)
            k, v, feat = kk[rows, lanes], vv[rows, lanes], fk[rows, :]
            one = jnp.ones_like(v)
            dks, dvs = [], []
            for a in range(2):
                ka = jnp.where(low_n, k, feat) if a == 0 else jnp.where(low_n, feat, k)
                va = jnp.where(low_n, v, one) if a == 0 else jnp.where(low_n, one, v)
                qa = qaug[p * 2 + a]
                e = jnp.exp2(dot(ka, qa, NT) * (LOG2E / 8))
                ds = (e * dot(va, das[a], NT)).astype(BF16)
                dvs.append(dot(e.astype(BF16), das[a]))
                dks.append(dot(ds, qa))
                dq = dot(ka, ds, TN)
                acc[a] = dq if t == 0 else acc[a] + dq
            dk[rows, :] = jnp.where(low_n, dks[0], dks[1])
            wbuf[4 * n + t * n:4 * n + (t + 1) * n, lanes] = jnp.where(low_n, dvs[0], dvs[1]).astype(BF16)
        low_s = lax.broadcasted_iota(jnp.int32, (128, n), 0) < 64
        dq = jnp.where(low_s, acc[0], acc[1]).T
        qa = jnp.where(low_n, qaug[p * 2], qaug[p * 2 + 1])
        dx, gg = norm_back(dq, qa, rq[:, lanes], vecs[4:5, lanes])
        wbuf[0:n, lanes] = dx.astype(BF16)
        small[4:5, lanes] = gg
        dx, gg = norm_back(dk[...], kk[:, lanes], rk[:, lanes], vecs[5:6, lanes])
        wbuf[2 * n:4 * n, lanes] = dx.astype(BF16)
        small[5:6, lanes] = gg
        at_points(p, ((1, 4), (3, 7), (5, 10)), r_step)
        at_points(p, ((1, 1), (3, 2)), lambda j: qkv_group(j, ()))
        return c

    lax.fori_loop(0, pairs, pair, 0)
    qkv_group(3, ((1, 11),))

    def gain_sums(xh, gn):
        small[0:1, :] += jnp.sum(gn * xh, axis=0, keepdims=True)
        small[1:2, :] += jnp.sum(gn, axis=0, keepdims=True)

    def rem_tile(i, c):
        rows = tile_of(i)
        gn = (dot(wbuf[pl.ds(pl.multiple_of(3 * n + i * TILE, TILE), TILE), :], wqkv[:, width:2 * width], NT)
              + dot(wbuf[pl.ds(pl.multiple_of(5 * n + i * TILE, TILE), TILE), :], wqkv[:, 2 * width:], NT))
        gn_rem[rows, :] = gn.astype(BF16)
        gain_sums(rows_norm(rem[rows, :].astype(F32))[0], gn)
        at_points(i, ((0, 3),), middle_sum)
        return c

    def own_back(i, c):
        rows = tile_of(i)
        gn = (dot(wbuf[rows, :], wqkv[:, 0:width], NT)
              + dot(wbuf[pl.ds(pl.multiple_of(2 * n + i * TILE, TILE), TILE), :], wqkv[:, width:2 * width], NT)
              + dot(wbuf[pl.ds(pl.multiple_of(4 * n + i * TILE, TILE), TILE), :], wqkv[:, 2 * width:], NT))
        xh, r = rows_norm(own[rows, :].astype(F32))
        gain_sums(xh, gn)
        gd = gn * vecs[0:1, :]
        base[rows, :] += r * (gd - jnp.mean(gd, -1, keepdims=True) - xh * jnp.mean(gd * xh, -1, keepdims=True))
        return c

    lax.fori_loop(0, tiles, rem_tile, 0)
    stores[1].start()
    last_sum(2)
    stores[4].start()
    lax.fori_loop(0, tiles, own_back, 0)
    stores[2].start()
    r_step(12)
    r_step(13)
    mine[...] = (first[...] + accin[chips - 2].astype(F32)).astype(BF16)
    stores[3].start()
    for j in range(1, chips):
        for k in range(2):
            for c in a_copies(j, k):
                c.wait_send()
    for i in range(tiles):
        t_copy(i).wait_send()
    last_sum(3)
    stores[5].start()
    for c in stores:
        c.wait()
    for j in range(4):
        g_copy(j).wait_send()
        x_copy(j).wait_send()
    for c in (gy_copy,) + parts:
        c.wait_send()


def layer_call(n_seq, own, gy, seg, g1, b1, wqkv, qg, kg, wout, g2, b2, wup, wdown):
    n, width = own.shape
    f = wup.shape[0]
    chips = n_seq // 2
    heads = width // 64
    tiles = n // TILE
    V, D = pltpu.VMEM, pltpu.SemaphoreType.DMA
    return pl.pallas_call(
        functools.partial(layer_body, n_seq),
        out_shape=(sds((n, width), BF16), sds((n, width), F32), sds((n, width), BF16),
                   sds((width // 4, 4 * width), BF16), sds((8, width), F32), sds((2, f, width), BF16)),
        in_specs=[VM] * 5 + [pl.BlockSpec(memory_space=pl.ANY), VM, VM, pl.BlockSpec(memory_space=pl.ANY)] + [VM] * 4,
        out_specs=(pl.BlockSpec(memory_space=pl.ANY),) * 4 + (VM, pl.BlockSpec(memory_space=pl.ANY)),
        scratch_shapes=[
            V((n, width), BF16), V((n, 128), BF16), V((2 * n, 128), BF16), V((256, 256), BF16), V((128, 128), BF16),
            V((8, width), F32), V((width, 2 * n), BF16), V((2 * n, width), BF16), V((2 * n, width), BF16),
            V((n, width), BF16), V((n, width), F32), V((2 * n, width), F32), V((heads, n, 128), BF16),
            V((n, width), BF16), V((n, width), F32),
            V((2 * n, width), BF16), V((2 * n, width), BF16), V((chips * 2 * f, width), BF16),
            V((chips - 1, 2, f, width), BF16), V((chips - 1, 2, f, width), BF16), V((2, f, width), F32),
            V((2 * n, chips // 2 * f), BF16), V((2 * n, chips // 2 * f), BF16), V((2 * n, width), F32), V((2 * n, width), F32),
            V((2, n, width), F32),
            V((2 * n, 128), F32), V((4, width // 2, width), BF16), V((4, width // 4, width), BF16),
            V(wqkv.shape, BF16), V(wout.shape, BF16),
            V((n, width), BF16), V((n, width), F32), V((n, width), BF16), V((width // 4, 4 * width), BF16),
            V((2, f, width), BF16),
            D((2, 2, chips - 1)), D((2, 2, chips - 1)), D((2, 2, chips - 1)), D((2, 2, chips - 1)),
            D((3 + tiles,)), D((3 + tiles,)), D((tiles,)), D((tiles,)),
            D((4,)), D((4,)), D((4,)), D((4,)), D((2,)), D((6,))],
        compiler_params=pltpu.CompilerParams(
            vmem_limit_bytes=66 * 1000 * 1000, collective_id=1, has_side_effects=True),
        name="layer",
    )(own, gy, seg, g1, b1, wqkv, qg, kg, wout, g2, b2, wup, wdown)


def local_one(tokens, segment_ids, first_gain, first_bias, w_qkv, query_gain, key_gain, w_out,
              second_gain, second_bias, w_up, w_down, out_grad):
    n_seq = lax.axis_size("seq")
    own = tokens[0]
    block_out, base, gn_rem, quarter, small, mine = layer_call(
        n_seq, own, out_grad[0], segment_ids, first_gain, first_bias, w_qkv, query_gain, key_gain, w_out,
        second_gain, second_bias, w_up.T, w_down.T)
    g, small, gback, other = sum_call(n_seq, quarter, small, gn_rem, mine)
    qkv, proj, fg, fb, qgg, kgg, sgg, sbg, input_grad, up_grad, down_grad, block_out = finish_call(
        g, small, own, gback, base, first_gain, mine, other, block_out)
    return (block_out[None], input_grad[None], fg, fb, qkv, qgg, kgg, proj, sgg, sbg, up_grad.T, down_grad.T)


def layer_norm(rows, gain, shift):
    average = jnp.mean(rows, axis=-1, keepdims=True)
    centred = rows - average
    spread = jnp.mean(centred * centred, axis=-1, keepdims=True)
    return centred * lax.rsqrt(spread + EPS) * gain + shift


def head_norm(values, gain):
    average = jnp.mean(values, axis=-1, keepdims=True)
    centred = values - average
    spread = jnp.mean(centred * centred, axis=-1, keepdims=True)
    return centred * lax.rsqrt(spread + EPS) * gain


def qk_norms(raw_query, raw_keys, query_gain, key_gain):
    return (head_norm(raw_query, query_gain), head_norm(raw_keys, key_gain))


def gelu_exact(values):
    return jax.nn.gelu(values, approximate=False)


def gelu_back(pre, upstream):
    return jax.vjp(gelu_exact, pre)[1](upstream)[0]


def group_size(count, length):
    for option in range(1, count + 1):
        if count % option == 0 and option * length >= 512:
            return option
    return count


def rows_product(left, right):
    return lax.dot_general(
        left, right, (((0,), (0,)), ((), ())), preferred_element_type=jnp.float32
    )


def cols_product(left, right):
    return lax.dot_general(
        left, right, (((1,), (1,)), ((), ())), preferred_element_type=jnp.float32
    )


def local(
    tokens,
    segment_ids,
    first_gain,
    first_bias,
    w_qkv,
    query_gain,
    key_gain,
    w_out,
    second_gain,
    second_bias,
    w_up,
    w_down,
    out_grad,
):
    seqs_here, local_len, width = tokens.shape
    full_len = segment_ids.shape[1]
    head_dim = query_gain.shape[0]
    heads = width // head_dim
    rows_here = seqs_here * local_len
    scale = head_dim ** (-0.5)
    offset = lax.axis_index("pos") * local_len
    query_marks = lax.dynamic_slice_in_dim(segment_ids, offset, local_len, 1)
    block = group_size(seqs_here, local_len)
    count_blocks = seqs_here // block

    def split(array):
        return array.reshape((count_blocks, block) + array.shape[1:])

    inputs = tokens.astype(jnp.float32).reshape(rows_here, width)
    normed_low = layer_norm(inputs, first_gain, first_bias).astype(jnp.bfloat16)
    mixed = jnp.dot(normed_low, w_qkv, preferred_element_type=jnp.float32).reshape(
        rows_here, 3, heads, head_dim
    )
    raw_query = mixed[:, 0]
    raw_keys = mixed[:, 1]
    query = (
        head_norm(raw_query, query_gain)
        .astype(jnp.bfloat16)
        .reshape(seqs_here, local_len, heads, head_dim)
    )
    keys_local = (
        head_norm(raw_keys, key_gain).astype(jnp.bfloat16).reshape(seqs_here, local_len, width)
    )
    values_local = mixed[:, 2].astype(jnp.bfloat16).reshape(seqs_here, local_len, width)
    keys_all, values_all = (
        lax.all_gather(keys_local, "pos", axis=1, tiled=True),
        lax.all_gather(values_local, "pos", axis=1, tiled=True),
    )
    keys_four = keys_all.reshape(seqs_here, full_len, heads, head_dim)
    values_four = values_all.reshape(seqs_here, full_len, heads, head_dim)

    def scores_for(query_blk, keys_blk, query_lab, key_lab):
        raw = (
            jnp.einsum("bqhd,bkhd->bhqk", query_blk, keys_blk, preferred_element_type=jnp.float32)
            * scale
        )
        allowed = (query_lab[:, :, None] == key_lab[:, None, :])[:, None]
        return jnp.where(allowed, raw, -1e30)

    def forward_block(packed):
        query_blk, keys_blk, values_blk, query_lab, key_lab = packed
        scores = scores_for(query_blk, keys_blk, query_lab, key_lab)
        peak = jnp.max(scores, axis=-1, keepdims=True)
        expd = jnp.exp(scores - peak)
        totals = jnp.sum(expd, axis=-1, keepdims=True)
        probs = (expd / totals).astype(jnp.bfloat16)
        result = jnp.einsum(
            "bhqk,bkhd->bqhd", probs, values_blk, preferred_element_type=jnp.float32
        )
        return (result, peak + jnp.log(totals))

    attended, log_totals = lax.map(
        forward_block,
        (
            split(query),
            split(keys_four),
            split(values_four),
            split(query_marks),
            split(segment_ids),
        ),
    )
    attended_low = attended.astype(jnp.bfloat16).reshape(rows_here, width)
    middle = inputs + jnp.dot(attended_low, w_out, preferred_element_type=jnp.float32)
    second_low = layer_norm(middle, second_gain, second_bias).astype(jnp.bfloat16)
    grad_out = out_grad.reshape(rows_here, width)
    grad_float = grad_out.astype(jnp.float32)
    up_all, down_all = (
        lax.all_gather(w_up, "seq", axis=1, tiled=True),
        lax.all_gather(w_down, "seq", axis=1, tiled=True),
    )
    pre = jnp.dot(second_low, up_all, preferred_element_type=jnp.float32)
    hidden = gelu_exact(pre).astype(jnp.bfloat16)
    block_out = (middle + cols_product(hidden, down_all)).astype(jnp.bfloat16)
    grad_hidden = jnp.dot(grad_out, down_all, preferred_element_type=jnp.float32)
    grad_pre = gelu_back(pre, grad_hidden).astype(jnp.bfloat16)
    down_full = rows_product(grad_out, hidden)
    up_full = rows_product(second_low, grad_pre)
    grad_second = cols_product(grad_pre, up_all)
    up_part, down_part = (
        lax.psum_scatter(
            up_full.astype(jnp.bfloat16), "seq", scatter_dimension=1, tiled=True
        ).astype(jnp.float32),
        lax.psum_scatter(
            down_full.astype(jnp.bfloat16), "seq", scatter_dimension=1, tiled=True
        ).astype(jnp.float32),
    )
    up_grad, down_grad = (
        lax.psum(up_part.astype(jnp.bfloat16), "pos").astype(jnp.float32),
        lax.psum(down_part.astype(jnp.bfloat16), "pos").astype(jnp.float32),
    )
    second_back = jax.vjp(layer_norm, middle, second_gain, second_bias)[1]
    grad_middle_part, second_gain_part, second_bias_part = second_back(grad_second)
    grad_middle = grad_float + grad_middle_part
    grad_branch = grad_middle.astype(jnp.bfloat16)
    proj_part = rows_product(attended_low, grad_branch)
    grad_attended = (
        cols_product(grad_branch, w_out)
        .astype(jnp.bfloat16)
        .reshape(seqs_here, local_len, heads, head_dim)
    )

    def backward_block(packed):
        query_blk, keys_blk, values_blk, query_lab, key_lab, log_blk, grad_blk = packed
        scores = scores_for(query_blk, keys_blk, query_lab, key_lab)
        probs = jnp.exp(scores - log_blk)
        grad_probs = jnp.einsum(
            "bqhd,bkhd->bhqk", grad_blk, values_blk, preferred_element_type=jnp.float32
        )
        grad_values = jnp.einsum(
            "bhqk,bqhd->bkhd",
            probs.astype(jnp.bfloat16),
            grad_blk,
            preferred_element_type=jnp.float32,
        )
        inner = jnp.sum(probs * grad_probs, axis=-1, keepdims=True)
        grad_scores = (probs * (grad_probs - inner) * scale).astype(jnp.bfloat16)
        grad_query = jnp.einsum(
            "bhqk,bkhd->bqhd", grad_scores, keys_blk, preferred_element_type=jnp.float32
        )
        grad_keys = jnp.einsum(
            "bhqk,bqhd->bkhd", grad_scores, query_blk, preferred_element_type=jnp.float32
        )
        return (grad_query, grad_keys, grad_values)

    grad_query, grad_keys, grad_values = lax.map(
        backward_block,
        (
            split(query),
            split(keys_four),
            split(values_four),
            split(query_marks),
            split(segment_ids),
            log_totals,
            split(grad_attended),
        ),
    )
    grad_keys = grad_keys.reshape(seqs_here, full_len, width)
    grad_values = grad_values.reshape(seqs_here, full_len, width)
    keys_grad, values_grad = (
        lax.psum_scatter(
            grad_keys.astype(jnp.bfloat16), "pos", scatter_dimension=1, tiled=True
        ).astype(jnp.float32),
        lax.psum_scatter(
            grad_values.astype(jnp.bfloat16), "pos", scatter_dimension=1, tiled=True
        ).astype(jnp.float32),
    )
    norm_back = jax.vjp(qk_norms, raw_query, raw_keys, query_gain, key_gain)[1]
    grad_raw_query, grad_raw_keys, query_gain_part, key_gain_part = norm_back(
        (
            grad_query.reshape(rows_here, heads, head_dim),
            keys_grad.reshape(rows_here, heads, head_dim),
        )
    )
    grad_mixed = (
        jnp.stack(
            [grad_raw_query, grad_raw_keys, values_grad.reshape(rows_here, heads, head_dim)], axis=1
        )
        .reshape(rows_here, 3 * width)
        .astype(jnp.bfloat16)
    )
    qkv_part = rows_product(normed_low, grad_mixed)
    grad_normed = cols_product(grad_mixed, w_qkv)
    first_back = jax.vjp(layer_norm, inputs, first_gain, first_bias)[1]
    grad_input_part, first_gain_part, first_bias_part = first_back(grad_normed)
    input_grad = (grad_middle + grad_input_part).reshape(seqs_here, local_len, width)
    (
        qkv_grad,
        proj_grad,
        first_gain_grad,
        first_bias_grad,
        query_gain_grad,
        key_gain_grad,
        second_gain_grad,
        second_bias_grad,
    ) = lax.psum(
        (
            qkv_part,
            proj_part,
            first_gain_part,
            first_bias_part,
            query_gain_part,
            key_gain_part,
            second_gain_part,
            second_bias_part,
        ),
        ("pos", "seq"),
    )
    return (
        block_out.reshape(seqs_here, local_len, width),
        input_grad,
        first_gain_grad,
        first_bias_grad,
        qkv_grad,
        query_gain_grad,
        key_gain_grad,
        proj_grad,
        second_gain_grad,
        second_bias_grad,
        up_grad,
        down_grad,
    )


def solution(mesh):
    placed = (P("seq", "pos", None), P("seq", None), P(), P(), P(), P(), P(), P(), P(), P(),
              P(None, "seq"), P(None, "seq"), P("seq", "pos", None))
    outs = (P("seq", "pos", None), P("seq", "pos", None), P(), P(), P(), P(), P(), P(), P(), P(),
            P(None, "seq"), P(None, "seq"))

    def step(*args):
        def run(*local_args):
            one = local_args[0].shape[:2] == (1, 512) and (mesh.shape["pos"], mesh.shape["seq"]) == (2, 16)
            return (local_one if one else local)(*local_args)

        return jax.shard_map(run, mesh=mesh, in_specs=placed, out_specs=outs, check_vma=False)(*args)

    return step
```
